32 devices in a mesh: obs: 4 (over z), td: 8 (over y, x, core).
Axes of the slice: x: 2, y: 2, z: 4, core: 2. Of those that a mesh axis runs over, the one named last changes fastest.
Arguments:
- timestreams: bfloat16 [4, 128, 8192], P('obs', 'td'), may hold values from -6 to 6
- filter_taps: bfloat16 [4, 128, 8, 129], P('obs', 'td'), may hold values from -0.5 to 0.5
- scan_bounds: int32 [4, 32], P('obs'), may hold values from 0 to 8192, as said below
- tile_index: int32 [4, 64], P('obs', 'td'), may hold values from 0 to 15
- det_weights: bfloat16 [4, 128], P('obs'), may hold values from 0.29882812 to 3
- positions: float32 [2, 128], replicated, may hold values from -1 to 1
- wafer_group: int32 [128], replicated, may hold values from 0 to 7, as said below
Outputs:
- filtered_residual: float32 [4, 128, 8192], P('obs', 'td')
- sky_map: float32 [16, 128, 128], P(None, ('obs', 'td'))
The draws below stay inside these ranges and needn't reach their ends.
Inputs may be any that keep to these rules, and one draw needn't show every extreme that they name: `scan_bounds`: each row is strictly increasing, starts with 0 and ends with 8192. `wafer_group`: every wafer group holds the same number of detectors.
All inputs are finite; a program needn't handle non-finite values.
Results may differ from the reference program's by a relative error of at most 0.009.
Values may be sent and summed in bfloat16 or wider, within the bound.
A program may use at most 128 MiB of HBM per device.

```python
import math
import jax
import jax.numpy as jnp
from jax import lax

TAPS = 129
BANDS = 8
TILE = 128
WAFERS = 8
POLY = 6
NINT = 16
OBS = 4
DET = 128
SAMP = 8192
TILES = 16


def draw_wafer_group(key, part):
    order = jax.random.permutation(jax.random.fold_in(key, 17), DET)
    return (order % WAFERS).astype(jnp.int32)


def draw_scan_bounds(key, part):
    keys = jax.random.split(jax.random.fold_in(key, 29), OBS)

    def one_row(row_key):
        inner = jax.random.permutation(row_key, SAMP - 1)[:2 * NINT - 2] + 1
        inner = jnp.sort(inner.astype(jnp.int32))
        return jnp.concatenate([jnp.zeros((1,), jnp.int32), inner, jnp.full((1,), SAMP, jnp.int32)])
    return jax.vmap(one_row)(keys)


def touch_ends(array, rng, low, high):
    shape = array.shape
    place = [jax.random.randint(jax.random.fold_in(rng, axis), (), 0, shape[axis]) for axis in range(len(shape))]
    array = array.at[tuple(place)].set(low)
    longest = shape.index(max(shape))
    place[longest] = (place[longest] + 1) % shape[longest]
    return array.at[tuple(place)].set(high)


def block_scale(stream_key, extent, cuts, smallest, largest):
    factor_of = 1.0
    for position, blocks in cuts:
        steps = jax.random.uniform(jax.random.fold_in(jax.random.fold_in(stream_key, 6), position), (blocks,), jnp.float32, smallest / len(cuts), largest / len(cuts))
        factor_of = factor_of * jnp.repeat(jnp.exp(steps), extent[position] // blocks).reshape((-1,) + (1,) * (len(extent) - 1 - position))
    return factor_of


def noise(rng, extent, width, limit, shards=(), held_as=jnp.bfloat16):
    entries = width * jax.random.normal(rng, extent, jnp.float32)
    if shards:
        entries = entries * block_scale(rng, extent, shards, -0.22, 0.18)
    return jnp.clip(entries, -limit, limit).astype(held_as)


def setup_inputs(seed: int = 0) -> dict:
    streams_of = jax.random.split(jax.random.key(seed), 8)
    return {
        "timestreams": noise(streams_of[0], (OBS, DET, SAMP), 1.0, 6.0, ((0, 4), (1, 8))),
        "filter_taps": noise(streams_of[1], (OBS, DET, BANDS, TAPS), TAPS ** -0.5, 0.5, ((0, 4), (1, 8))),
        "scan_bounds": draw_scan_bounds(jax.random.fold_in(streams_of[7], 71), 0),
        "tile_index": touch_ends(jax.random.randint(streams_of[3], (OBS, SAMP // TILE), 0, TILES), jax.random.fold_in(streams_of[3], 1), 0, TILES - 1).astype(jnp.int32),
        "det_weights": jnp.clip(jnp.exp(math.log(3.0) - 2.306499 * jax.random.uniform(streams_of[4], (OBS, DET), jnp.float32) ** block_scale(streams_of[4], (OBS, DET), ((0, 4),), -0.2, 0.2)), 0.29882812, 3.0).astype(jnp.bfloat16),
        "positions": jnp.clip(jax.random.uniform(streams_of[5], (2, DET), jnp.float32, -1.0, 1.0), -1.0, 1.0),
        "wafer_group": draw_wafer_group(jax.random.fold_in(streams_of[7], 71), 0),
    }


prior_weight = 1.0

def toeplitz(band_taps):
    leading = band_taps.shape[:-1]
    half = TAPS // 2
    padded = jnp.concatenate([jnp.zeros(leading + (TILE - half,), band_taps.dtype), band_taps, jnp.zeros(leading + (3 * TILE - TAPS + half,), band_taps.dtype)], axis=-1)
    repeated = jnp.tile(padded, (1,) * len(leading) + (TILE,))
    repeated = repeated[..., :TILE * (4 * TILE - 1)].reshape(leading + (TILE, 4 * TILE - 1))
    return repeated[..., :3 * TILE]

def windows_of(signal):
    blocks = jnp.pad(signal, ((0, 0), (0, 0), (TILE, TILE)))
    blocks = blocks.reshape(signal.shape[0], signal.shape[1], -1, TILE)
    return jnp.concatenate([blocks[:, :, :-2], blocks[:, :, 1:-1], blocks[:, :, 2:]], axis=-1)

def forward_filter(signal, filter_taps):
    windows = windows_of(signal)
    per_band = windows.shape[2] // BANDS
    pieces = []
    for band_idx in range(BANDS):
        kernel = toeplitz(filter_taps[:, :, band_idx]).astype(jnp.float32)
        band_part = windows[:, :, band_idx * per_band:(band_idx + 1) * per_band].astype(jnp.float32)
        pieces.append(jnp.einsum('odnj,odij->odni', band_part, kernel, precision=lax.Precision.HIGHEST))
    return jnp.concatenate(pieces, axis=2).reshape(signal.shape)

def adjoint_filter(signal, filter_taps):
    blocks = signal.reshape(signal.shape[0], signal.shape[1], -1, TILE)
    per_band = blocks.shape[2] // BANDS
    pieces = []
    for band_idx in range(BANDS):
        kernel = toeplitz(filter_taps[:, :, band_idx]).astype(jnp.float32)
        band_part = blocks[:, :, band_idx * per_band:(band_idx + 1) * per_band].astype(jnp.float32)
        pieces.append(jnp.einsum('odni,odij->odnj', band_part, kernel, precision=lax.Precision.HIGHEST))
    spread = jnp.concatenate(pieces, axis=2)
    zero_block = jnp.zeros(spread.shape[:2] + (1, TILE), jnp.float32)
    from_next = jnp.concatenate([spread[:, :, 1:, :TILE], zero_block], axis=2)
    from_prev = jnp.concatenate([zero_block, spread[:, :, :-1, 2 * TILE:]], axis=2)
    summed = spread[:, :, :, TILE:2 * TILE] + from_next + from_prev
    return summed.reshape(signal.shape)

def make_basis(positions, wafer_group):
    x_pos = positions[0]
    y_pos = positions[1]
    monomials = jnp.stack([jnp.ones_like(x_pos), x_pos, y_pos, x_pos * x_pos, x_pos * y_pos, y_pos * y_pos])
    member = (wafer_group[None, :] == jnp.arange(WAFERS, dtype=jnp.int32)[:, None]).astype(jnp.float32)
    basis_b = (member[:, None, :] * monomials[None]).reshape(WAFERS * POLY, -1).astype(jnp.bfloat16)
    basis_f = basis_b.astype(jnp.float32)
    gram_matrix = jnp.dot(basis_f, basis_f.T, precision=lax.Precision.HIGHEST)
    factor = jnp.linalg.cholesky(gram_matrix)
    lower_inv = lax.linalg.triangular_solve(factor, jnp.eye(WAFERS * POLY, dtype=jnp.float32), left_side=True, lower=True)
    inverse = jnp.dot(lower_inv.T, lower_inv, precision=lax.Precision.HIGHEST)
    return (basis_b, basis_f, inverse)

def remove_poly(gathered, basis):
    basis_b, basis_f, inverse = basis
    coef_raw = jnp.einsum('md,nds->nms', basis_f, gathered.astype(jnp.float32), precision=lax.Precision.HIGHEST)
    coefficients = jnp.einsum('mq,nqs->nms', inverse, coef_raw, precision=lax.Precision.HIGHEST)
    fitted = jnp.einsum('md,nms->nds', basis_f, coefficients, precision=lax.Precision.HIGHEST)
    return (gathered.astype(jnp.float32) - fitted).astype(jnp.bfloat16)

def scan_flags(bounds, offset, length):
    sample = offset + jnp.arange(length, dtype=jnp.int32)
    passed = jnp.sum((bounds[:, :, None] <= sample[None, None, :]).astype(jnp.int32), axis=1)
    return (passed % 2).astype(jnp.float32)

def bin_maps(cleaned, in_scan, det_weights, tile_index):
    obs_count, det_count, samples = cleaned.shape
    groups = det_count // TILE
    block_count = samples // TILE
    masked = cleaned.astype(jnp.float32) * in_scan[:, None, :]
    shaped = masked.reshape(obs_count, groups, TILE, block_count, TILE)
    weight_rows = det_weights.astype(jnp.float32).reshape(obs_count, groups, TILE)
    block_sums = jnp.einsum('oqr,oqrbc->obrc', weight_rows, shaped, precision=lax.Precision.HIGHEST)
    row_weight = jnp.sum(weight_rows, axis=1)
    one_hot = (tile_index[:, :, None] == jnp.arange(TILES, dtype=jnp.int32)[None, None, :]).astype(jnp.float32)
    weighted_sum = jnp.einsum('obt,obrc->trc', one_hot, block_sums, precision=lax.Precision.HIGHEST)
    scan_blocks = in_scan.reshape(obs_count, block_count, TILE)
    hit_weight = jnp.einsum('obt,or,obc->trc', one_hot, row_weight, scan_blocks, precision=lax.Precision.HIGHEST)
    return (weighted_sum, hit_weight, one_hot)

def rescan_residual(cleaned, in_scan, sky_b, one_hot):
    obs_count, det_count, samples = cleaned.shape
    groups = det_count // TILE
    block_count = samples // TILE
    selected = jnp.einsum('obt,trc->orbc', one_hot, sky_b.astype(jnp.float32), precision=lax.Precision.HIGHEST)
    shaped = cleaned.astype(jnp.float32).reshape(obs_count, groups, TILE, block_count, TILE)
    deviation = shaped - selected[:, None]
    flags = in_scan.reshape(obs_count, 1, 1, block_count, TILE)
    return (flags * deviation).astype(jnp.bfloat16).reshape(obs_count, det_count, samples)

def reference(timestreams, filter_taps, scan_bounds, tile_index, det_weights, positions, wafer_group):
    basis = make_basis(positions, wafer_group)
    weighted_sum = jnp.zeros((TILES, TILE, TILE), jnp.float32)
    hit_weight = jnp.zeros((TILES, TILE, TILE), jnp.float32)
    kept = []
    for obs_idx in range(OBS):
        filtered = forward_filter(timestreams[obs_idx:obs_idx + 1], filter_taps[obs_idx:obs_idx + 1]).astype(jnp.bfloat16)
        cleaned = remove_poly(filtered, basis)
        in_scan = scan_flags(scan_bounds[obs_idx:obs_idx + 1], 0, SAMP)
        part_sum, part_hit, one_hot = bin_maps(cleaned, in_scan, det_weights[obs_idx:obs_idx + 1], tile_index[obs_idx:obs_idx + 1])
        weighted_sum = weighted_sum + part_sum
        hit_weight = hit_weight + part_hit
        kept.append((cleaned, in_scan, one_hot))
    sky_map = weighted_sum / (hit_weight + prior_weight)
    sky_b = sky_map.astype(jnp.bfloat16)
    outputs = []
    for obs_idx in range(OBS):
        cleaned, in_scan, one_hot = kept[obs_idx]
        residual = rescan_residual(cleaned, in_scan, sky_b, one_hot)
        outputs.append(adjoint_filter(residual, filter_taps[obs_idx:obs_idx + 1]))
    return (jnp.concatenate(outputs, axis=0), sky_map)
```

```python
import functools

import jax
import jax.numpy as jnp
from jax import lax
from jax.experimental import pallas as pl
from jax.experimental.pallas import tpu as pltpu
from jax.sharding import PartitionSpec as P

TAPS = 129
HALF = 64
BANDS = 8
TILE = 128
POLY = 6
TILES = 16
LANES = 128
prior_weight = 1.0
F32 = jnp.float32
BF16 = jnp.bfloat16


def lane_band(det):
    return lax.broadcasted_iota(jnp.int32, (HALF, LANES), 1) // det


def projector(pos_ref, wafer_ref, dets):
    x = pos_ref[0:1, :]
    y = pos_ref[1:2, :]
    rows = [jnp.ones_like(x), x, y, x * x, x * y, y * y]
    q = [r.astype(BF16).astype(F32) for r in rows]
    group = jnp.broadcast_to(wafer_ref[...].astype(F32), (dets, dets))
    same = group == group.T
    same_b = jnp.where(same, 1.0, 0.0).astype(BF16)
    pairs = [(i, j) for i in range(POLY) for j in range(i + 1)]
    products = jnp.concatenate(
        [q[i] * q[j] for i, j in pairs] + [jnp.zeros((32 - len(pairs), dets), F32)], axis=0
    )
    high = products.astype(BF16)
    low = (products - high.astype(F32)).astype(BF16)
    gram = jnp.dot(high, same_b, preferred_element_type=F32) + jnp.dot(
        low, same_b, preferred_element_type=F32
    )
    entry = {pair: gram[n : n + 1, :] for n, pair in enumerate(pairs)}
    factor, inv, white = {}, {}, []
    for i in range(POLY):
        for j in range(i + 1):
            value = entry[(i, j)]
            for k in range(j):
                value = value - factor[(i, k)] * factor[(j, k)]
            if i == j:
                factor[(i, i)] = jnp.sqrt(value)
                inv[i] = 1.0 / factor[(i, i)]
            else:
                factor[(i, j)] = value * inv[j]
        value = q[i]
        for k in range(i):
            value = value - factor[(i, k)] * white[k]
        white.append(value * inv[i])
    whitened = jnp.concatenate(white + [jnp.zeros((8 - POLY, dets), F32)], axis=0)
    columns = jnp.concatenate([whitened, jnp.zeros((LANES - 8, dets), F32)], axis=0).T
    outer = columns[:, 0:1] * white[0]
    for m in range(1, POLY):
        outer = outer + columns[:, m : m + 1] * white[m]
    outer = jnp.where(same, outer, 0.0)
    p_high = outer.astype(BF16)
    p_low = (outer - p_high.astype(F32)).astype(BF16)
    return p_high, p_low


def clean(p_high, p_low, gathered):
    fitted = jnp.dot(p_high, gathered, preferred_element_type=F32) + jnp.dot(
        p_low, gathered, preferred_element_type=F32
    )
    return (gathered.astype(F32) - fitted).astype(BF16)


def scan_mask(bounds_ref, length, n_bounds):
    sample = lax.broadcasted_iota(jnp.int32, (BANDS, length), 0) * length + lax.broadcasted_iota(
        jnp.int32, (BANDS, length), 1
    )
    count = jnp.zeros((BANDS, length), jnp.int32)
    for n in range(n_bounds):
        count = count + jnp.where(bounds_ref[0, n] <= sample, 1, 0)
    return (count & 1).astype(F32)


def spread_rows(mask, det):
    return jnp.broadcast_to(mask[:, None, :], (BANDS, det, TILE)).reshape(BANDS * det, TILE)


def pick_matrix(tiles_row, det):
    shape = (det * TILES, LANES)
    row = lax.broadcasted_iota(jnp.int32, shape, 0)
    lane = lax.broadcasted_iota(jnp.int32, shape, 1)
    return (row % det == lane % det) & ((row // det).astype(F32) == tiles_row)


def spread_matrix(tiles_column, det):
    shape = (LANES, det * TILES)
    row = lax.broadcasted_iota(jnp.int32, shape, 0)
    lane = lax.broadcasted_iota(jnp.int32, shape, 1)
    return (row % det == lane % det) & ((lane // det).astype(F32) == tiles_column)


def adjoint_body(pad_ref, taps_ref, ext_ref, out_ref, length, det):
    def chunk(c, _):
        base = pl.multiple_of(c * TILE, TILE)
        acc = jnp.zeros((TILE, LANES), F32)
        for k in range(TAPS):
            acc = acc + taps_ref[k : k + 1, :] * pad_ref[pl.ds(base + (TILE - k), TILE), :]
        ext_ref[pl.ds(base, TILE), :] = acc
        return 0

    lax.fori_loop(0, length // TILE + 1, chunk, 0)
    band = lane_band(det)
    head = ext_ref[0:HALF, :]
    tail = ext_ref[HALF + length : 2 * HALF + length, :]
    ext_ref[length : length + HALF, :] += jnp.where(
        band < BANDS - 1, pltpu.roll(head, LANES - det, 1), 0.0
    )
    ext_ref[HALF : 2 * HALF, :] += jnp.where(band > 0, pltpu.roll(tail, det, 1), 0.0)
    for c in range(length // TILE):
        piece = ext_ref[HALF + c * TILE : HALF + (c + 1) * TILE, :].T
        for b in range(BANDS):
            out_ref[:, b * length + c * TILE : b * length + (c + 1) * TILE] = piece[
                b * det : (b + 1) * det, :
            ]


MESH = pl.DeviceIdType.MESH
PIECES = 4


def load_signal(x_ref, ext_ref, length, det):
    for c in range(length // TILE):
        piece = jnp.concatenate(
            [x_ref[:, b * length + c * TILE : b * length + (c + 1) * TILE] for b in range(BANDS)],
            axis=0,
        )
        ext_ref[HALF + c * TILE : HALF + (c + 1) * TILE, :] = piece.astype(F32).T
    band = lane_band(det)
    last = ext_ref[length : length + HALF, :]
    first = ext_ref[HALF : 2 * HALF, :]
    ext_ref[0:HALF, :] = jnp.where(band > 0, pltpu.roll(last, det, 1), 0.0)
    ext_ref[HALF + length : 2 * HALF + length, :] = jnp.where(
        band < BANDS - 1, pltpu.roll(first, LANES - det, 1), 0.0
    )


def whole_kernel(
    dims, bounds_ref, index_ref, x_ref, taps_ref, weights_ref, pos_ref, wafer_ref,
    out_ref, skyout_ref,
    ext_ref, pad_ref, mask_ref, tiles_ref, fsend, frecv, csend, crecv, tsend, trecv,
    filt, spread, gsend, grecv, hsend, hrecv, sky_b, sky_f, skyb_recv, skyf_recv,
    f_s, f_r, c_s, c_r, t_s, t_r, g_s, g_r, h_s, h_r, b_s, b_r, k_s, k_r,
):
    n_obs, td, det, length, slab, n_bounds = dims
    dets = det * td
    split = td // BANDS
    blocks = slab // TILE
    width = slab // PIECES
    folds = dets // TILE
    per_fold = td // folds
    count = n_obs * td
    stride = count // TILES
    own_rows = TILE // count
    obs = lax.axis_index("obs")
    me = lax.axis_index("td")
    linear = obs * td + me
    mine = linear // stride
    owner = lax.rem(linear, stride) == 0

    def place(device):
        return (device // td, lax.rem(device, td))

    def td_peer(k):
        return lax.rem(me + k, td)

    def td_source(k):
        return lax.rem(me + td - k, td)

    def obs_peer(k):
        return lax.rem(obs + k, n_obs)

    def obs_source(k):
        return lax.rem(obs + n_obs - k, n_obs)

    barrier = pltpu.get_barrier_semaphore()
    for k in range(1, td):
        pl.semaphore_signal(barrier, 1, device_id=(obs, td_peer(k)), device_id_type=MESH)
    for k in range(1, n_obs):
        pl.semaphore_signal(barrier, 1, device_id=(obs_peer(k), me), device_id_type=MESH)

    row = lax.broadcasted_iota(jnp.int32, (blocks, LANES), 0)
    tile = jnp.zeros((blocks, LANES), jnp.int32)
    for n in range(blocks):
        tile = jnp.where(row == n, index_ref[0, n], tile)
    tsend[...] = tile.astype(F32)
    trecv[me] = tile.astype(F32)
    load_signal(x_ref, ext_ref, length, det)

    def tile_copy(k, slot):
        return pltpu.make_async_remote_copy(
            src_ref=tsend, dst_ref=trecv.at[slot], send_sem=t_s.at[k], recv_sem=t_r.at[k],
            device_id=(obs, td_peer(k)), device_id_type=MESH,
        )

    def signal_copy(h, k, slot):
        cols = pl.ds(pl.multiple_of(h * width, TILE), width)
        peer = td_peer(k)
        return pltpu.make_async_remote_copy(
            src_ref=fsend.at[peer, :, cols], dst_ref=frecv.at[slot, :, cols],
            send_sem=f_s.at[h, k], recv_sem=f_r.at[h, k],
            device_id=(obs, peer), device_id_type=MESH,
        )

    def clean_copy(h, k, slot):
        cols = pl.ds(pl.multiple_of(h * width, TILE), width)
        peer = td_peer(k)
        return pltpu.make_async_remote_copy(
            src_ref=csend.at[peer, :, cols], dst_ref=crecv.at[slot, :, cols],
            send_sem=c_s.at[h, k], recv_sem=c_r.at[h, k],
            device_id=(obs, peer), device_id_type=MESH,
        )

    def hit_copy(k, slot):
        peer = obs_peer(k)
        return pltpu.make_async_remote_copy(
            src_ref=hsend.at[(peer * td + me) // stride], dst_ref=hrecv.at[slot],
            send_sem=h_s.at[k], recv_sem=h_r.at[k],
            device_id=(peer, me), device_id_type=MESH,
        )

    def bin_copy(p, source):
        return pltpu.make_async_remote_copy(
            src_ref=gsend.at[p], dst_ref=grecv.at[source],
            send_sem=g_s.at[p], recv_sem=g_r.at[source],
            device_id=place(p * stride), device_id_type=MESH,
        )

    def rounded_copy(device, p):
        rows = pl.ds(pl.multiple_of(lax.rem(lax.rem(device, td), per_fold) * det, det), det)
        return pltpu.make_async_remote_copy(
            src_ref=sky_b.at[rows], dst_ref=skyb_recv.at[p],
            send_sem=b_s.at[device], recv_sem=b_r.at[p],
            device_id=place(device), device_id_type=MESH,
        )

    def row_copy(device, p):
        return pltpu.make_async_remote_copy(
            src_ref=sky_f.at[device], dst_ref=skyf_recv.at[p],
            send_sem=k_s.at[device], recv_sem=k_r.at[p],
            device_id=place(device), device_id_type=MESH,
        )

    def each(number, do):
        def step(k, _):
            do(k)
            return 0

        lax.fori_loop(1, number, step, 0)

    def each_tile(do):
        def step(k, _):
            p = lax.rem(mine + k, TILES)

            @pl.when(p * stride != linear)
            def _():
                do(p)

            return 0

        lax.fori_loop(0, TILES, step, 0)

    def each_device(do):
        each(count, lambda k: do(lax.rem(linear + k, count)))

    def compute(p):
        quarter = p // PIECES
        h = lax.rem(p, PIECES)

        def chunk(c, _):
            inside = pl.multiple_of(h * width + c * TILE, TILE)
            base = pl.multiple_of(quarter * slab + inside, TILE)
            acc = jnp.zeros((TILE, LANES), F32)
            for k in range(TAPS):
                acc = acc + taps_ref[k : k + 1, :] * ext_ref[pl.ds(base + k, TILE), :]
            block = acc.T.astype(BF16)
            filt[quarter * blocks + h * (width // TILE) + c] = block
            for b in range(BANDS):
                fsend[b * split + quarter, :, pl.ds(inside, TILE)] = block[b * det : (b + 1) * det, :]
            return 0

        lax.fori_loop(0, width // TILE, chunk, 0)

    def send_piece(p):
        quarter = p // PIECES
        h = lax.rem(p, PIECES)

        def send(k):
            if split == 1:
                signal_copy(h, k, me).start()
            else:

                @pl.when(lax.rem(td_peer(k), split) == quarter)
                def _():
                    signal_copy(h, k, me).start()

        each(td, send)

    compute(jnp.int32(0))
    pl.semaphore_wait(barrier, td - 1 + n_obs - 1)
    each(td, lambda k: tile_copy(k, me).start())
    send_piece(jnp.int32(0))

    def later(p, _):
        compute(p)
        send_piece(p)
        return 0

    lax.fori_loop(1, split * PIECES, later, 0)
    frecv[me] = fsend[me]

    mask_ref[...] = scan_mask(bounds_ref, length, n_bounds)
    each(td, lambda k: tile_copy(k, td_source(k)).wait_recv())
    lane = lax.broadcasted_iota(jnp.int32, (blocks, LANES), 1) // det
    for quarter in range(split):
        tile = trecv[quarter]
        for b in range(1, BANDS):
            tile = jnp.where(lane == b, trecv[b * split + quarter], tile)
        tiles_ref[quarter * blocks : (quarter + 1) * blocks, :] = tile
    first = lax.broadcasted_iota(jnp.int32, (TILES, LANES), 1) % det == 0
    which = lax.broadcasted_iota(jnp.int32, (TILES, LANES), 0).astype(F32)
    counts = jnp.zeros((TILES, TILE), F32)
    for n in range(length // TILE):
        mask = spread_rows(mask_ref[:, n * TILE : (n + 1) * TILE], det).astype(BF16)
        pick = jnp.where(first & (which == tiles_ref[n : n + 1, :]), 1.0, 0.0).astype(BF16)
        counts = counts + jnp.dot(pick, mask, preferred_element_type=F32)
    sums = jnp.zeros((det * TILES, TILE), F32)
    for n in range(length // TILE):
        mask = spread_rows(mask_ref[:, n * TILE : (n + 1) * TILE], det).astype(BF16)
        pick = jnp.where(pick_matrix(tiles_ref[n : n + 1, :], det), 1.0, 0.0).astype(BF16)
        sums = sums + jnp.dot(pick, filt[n] * mask, preferred_element_type=F32)
    gsend[...] = sums.reshape(TILES, det, TILE).astype(BF16)
    each_tile(lambda p: bin_copy(p, linear).start())

    @pl.when(owner)
    def _():
        grecv[linear] = gsend[mine]
        level = lax.broadcasted_iota(jnp.int32, (TILES, 8, TILE), 1)
        rows = jnp.broadcast_to(counts[:, None, :], (TILES, 8, TILE))
        weights = weights_ref[...].astype(F32)
        for q in range(folds):
            rows = jnp.where(level == q + 1, weights[:, None, q * TILE : (q + 1) * TILE], rows)
        hsend[...] = rows
        hrecv[obs] = hsend[mine]
        each(n_obs, lambda k: hit_copy(k, obs).start())

    p_high, p_low = projector(pos_ref, wafer_ref, dets)

    for h in range(PIECES):
        each(td, lambda k: signal_copy(h, k, td_source(k)).wait_recv())
        cols = slice(h * width, (h + 1) * width)
        cleaned = clean(p_high, p_low, frecv[:, :, cols].reshape(dets, width))
        csend[:, :, cols] = cleaned.reshape(td, det, width)
        each(td, lambda k: clean_copy(h, k, me).start())
    crecv[me] = csend[me]

    def band_rows(n):
        quarter, inside = n // blocks, n % blocks
        cols = slice(inside * TILE, (inside + 1) * TILE)
        return jnp.concatenate([crecv[b * split + quarter, :, cols] for b in range(BANDS)], axis=0)

    @pl.when(owner)
    def _():
        each(n_obs, lambda k: hit_copy(k, obs_source(k)).wait_recv())
        each_device(lambda d: bin_copy(mine, d).wait_recv())
        total = jnp.zeros((TILE, TILE), F32)
        hit = jnp.zeros((TILE, TILE), F32)
        for o in range(n_obs):
            binned = grecv[o * td : (o + 1) * td].reshape(dets, TILE)
            fitted = jnp.dot(p_high, binned, preferred_element_type=F32) + jnp.dot(
                p_low, binned, preferred_element_type=F32
            )
            left = binned.astype(F32) - fitted
            for q in range(folds):
                weight = jnp.broadcast_to(hrecv[o, q + 1 : q + 2, :], (TILE, TILE)).T
                total = total + weight * left[q * TILE : (q + 1) * TILE, :]
                hit = hit + weight * hrecv[o, 0:1, :]
        sky = total / (hit + prior_weight)
        sky_b[...] = sky.astype(BF16)
        for d in range(count):
            sky_f[d] = sky[d * own_rows : (d + 1) * own_rows, :]
        each_device(lambda d: rounded_copy(d, mine).start())
        each_device(lambda d: row_copy(d, mine).start())
        own = pl.ds(pl.multiple_of(lax.rem(me, per_fold) * det, det), det)
        skyb_recv[mine] = sky_b[own, :]
        skyf_recv[mine] = sky_f[linear]

    grid = jnp.concatenate(
        [tiles_ref[...], jnp.zeros((LANES - length // TILE, LANES), F32)], axis=0
    ).T
    for n in range(length // TILE):
        spread[n] = jnp.where(spread_matrix(grid[:, n : n + 1], det), 1.0, 0.0).astype(BF16)
    for h in range(PIECES):
        each(td, lambda k: clean_copy(h, k, td_source(k)).wait_recv())
    each_tile(lambda p: rounded_copy(linear, p).wait_recv())
    chosen_from = skyb_recv[...].reshape(TILES * det, TILE)
    zero = jnp.zeros((TILE, LANES), F32)
    pad_ref[0:TILE, :] = zero
    pad_ref[TILE + length : 2 * TILE + length, :] = zero
    for n in range(length // TILE):
        mask = spread_rows(mask_ref[:, n * TILE : (n + 1) * TILE], det)
        chosen = jnp.dot(spread[n], chosen_from, preferred_element_type=F32)
        residual = (mask * (band_rows(n).astype(F32) - chosen)).astype(BF16)
        pad_ref[TILE + n * TILE : 2 * TILE + n * TILE, :] = residual.astype(F32).T
    adjoint_body(pad_ref, taps_ref, ext_ref, out_ref, length, det)

    each_tile(lambda p: row_copy(linear, p).wait_recv())
    skyout_ref[...] = skyf_recv[...]
    each(td, lambda k: tile_copy(k, me).wait_send())
    for h in range(PIECES):
        each(td, lambda k: signal_copy(h, k, me).wait_send())
        each(td, lambda k: clean_copy(h, k, me).wait_send())
    each_tile(lambda p: bin_copy(p, linear).wait_send())

    @pl.when(owner)
    def _():
        each(n_obs, lambda k: hit_copy(k, obs).wait_send())
        each_device(lambda d: rounded_copy(d, mine).wait_send())
        each_device(lambda d: row_copy(d, mine).wait_send())


VM = pl.BlockSpec(memory_space=pltpu.VMEM)
SM = pl.BlockSpec(memory_space=pltpu.SMEM)


def local(timestreams, filter_taps, scan_bounds, tile_index, det_weights, positions, wafer_group):
    _, det, samples = timestreams.shape
    td = lax.axis_size("td")
    n_obs = lax.axis_size("obs")
    dets = det * td
    length = samples // BANDS
    slab = samples // td
    blocks = slab // TILE
    count = n_obs * td
    own_rows = TILE // count
    dims = (n_obs, td, det, length, slab, scan_bounds.shape[1])
    taps = jnp.transpose(filter_taps[0], (2, 1, 0)).reshape(TAPS, BANDS * det).astype(F32)
    dma = pltpu.SemaphoreType.DMA
    out, sky = pl.pallas_call(
        functools.partial(whole_kernel, dims),
        out_shape=(
            jax.ShapeDtypeStruct((det, samples), F32),
            jax.ShapeDtypeStruct((TILES, own_rows, TILE), F32),
        ),
        in_specs=[SM, SM, VM, VM, VM, VM, VM],
        out_specs=(VM, VM),
        scratch_shapes=[
            pltpu.VMEM((length + 2 * HALF, LANES), F32),
            pltpu.VMEM((length + 2 * TILE, LANES), F32),
            pltpu.VMEM((BANDS, length), F32),
            pltpu.VMEM((length // TILE, LANES), F32),
            pltpu.VMEM((td, det, slab), BF16),
            pltpu.VMEM((td, det, slab), BF16),
            pltpu.VMEM((td, det, slab), BF16),
            pltpu.VMEM((td, det, slab), BF16),
            pltpu.VMEM((blocks, LANES), F32),
            pltpu.VMEM((td, blocks, LANES), F32),
            pltpu.VMEM((length // TILE, LANES, TILE), BF16),
            pltpu.VMEM((length // TILE, LANES, det * TILES), BF16),
            pltpu.VMEM((TILES, det, TILE), BF16),
            pltpu.VMEM((count, det, TILE), BF16),
            pltpu.VMEM((TILES, 8, TILE), F32),
            pltpu.VMEM((n_obs, 8, TILE), F32),
            pltpu.VMEM((TILE, TILE), BF16),
            pltpu.VMEM((count, own_rows, TILE), F32),
            pltpu.VMEM((TILES, det, TILE), BF16),
            pltpu.VMEM((TILES, own_rows, TILE), F32),
            dma((PIECES, td)), dma((PIECES, td)), dma((PIECES, td)), dma((PIECES, td)),
            dma((td,)), dma((td,)), dma((TILES,)), dma((count,)),
            dma((n_obs,)), dma((n_obs,)), dma((count,)), dma((TILES,)),
            dma((count,)), dma((TILES,)),
        ],
        compiler_params=pltpu.CompilerParams(
            collective_id=0, has_side_effects=True, vmem_limit_bytes=48 << 20
        ),
    )(
        scan_bounds, tile_index, timestreams[0], taps, det_weights, positions,
        wafer_group.reshape(1, dets),
    )
    return out[None], sky


def solution(mesh):
    placed = (
        P("obs", "td", None),
        P("obs", "td", None, None),
        P("obs", None),
        P("obs", "td"),
        P("obs", None),
        P(),
        P(),
    )
    return jax.shard_map(
        local,
        mesh=mesh,
        in_specs=placed,
        out_specs=(P("obs", "td", None), P(None, ("obs", "td"), None)),
        check_vma=False,
    )
```

```python
import functools

import jax
import jax.numpy as jnp
from jax import lax
from jax.experimental import pallas as pl
from jax.experimental.pallas import tpu as pltpu
from jax.sharding import PartitionSpec as P

TAPS = 129
HALF = 64
BANDS = 8
TILE = 128
POLY = 6
TILES = 16
LANES = 128
prior_weight = 1.0
F32 = jnp.float32
BF16 = jnp.bfloat16


def lane_band(det):
    return lax.broadcasted_iota(jnp.int32, (HALF, LANES), 1) // det


def projector(pos_ref, wafer_ref, dets):
    x = pos_ref[0:1, :]
    y = pos_ref[1:2, :]
    rows = [jnp.ones_like(x), x, y, x * x, x * y, y * y]
    q = [r.astype(BF16).astype(F32) for r in rows]
    group = jnp.broadcast_to(wafer_ref[...].astype(F32), (dets, dets))
    same = group == group.T
    same_b = jnp.where(same, 1.0, 0.0).astype(BF16)
    pairs = [(i, j) for i in range(POLY) for j in range(i + 1)]
    products = jnp.concatenate(
        [q[i] * q[j] for i, j in pairs] + [jnp.zeros((32 - len(pairs), dets), F32)], axis=0
    )
    high = products.astype(BF16)
    low = (products - high.astype(F32)).astype(BF16)
    gram = jnp.dot(high, same_b, preferred_element_type=F32) + jnp.dot(
        low, same_b, preferred_element_type=F32
    )
    entry = {pair: gram[n : n + 1, :] for n, pair in enumerate(pairs)}
    factor, inv, white = {}, {}, []
    for i in range(POLY):
        for j in range(i + 1):
            value = entry[(i, j)]
            for k in range(j):
                value = value - factor[(i, k)] * factor[(j, k)]
            if i == j:
                factor[(i, i)] = jnp.sqrt(value)
                inv[i] = 1.0 / factor[(i, i)]
            else:
                factor[(i, j)] = value * inv[j]
        value = q[i]
        for k in range(i):
            value = value - factor[(i, k)] * white[k]
        white.append(value * inv[i])
    whitened = jnp.concatenate(white + [jnp.zeros((8 - POLY, dets), F32)], axis=0)
    columns = jnp.concatenate([whitened, jnp.zeros((LANES - 8, dets), F32)], axis=0).T
    outer = columns[:, 0:1] * white[0]
    for m in range(1, POLY):
        outer = outer + columns[:, m : m + 1] * white[m]
    outer = jnp.where(same, outer, 0.0)
    p_high = outer.astype(BF16)
    p_low = (outer - p_high.astype(F32)).astype(BF16)
    return p_high, p_low


def clean(p_high, p_low, gathered):
    fitted = jnp.dot(p_high, gathered, preferred_element_type=F32) + jnp.dot(
        p_low, gathered, preferred_element_type=F32
    )
    return (gathered.astype(F32) - fitted).astype(BF16)


def scan_mask(bounds_ref, length, n_bounds):
    sample = lax.broadcasted_iota(jnp.int32, (BANDS, length), 0) * length + lax.broadcasted_iota(
        jnp.int32, (BANDS, length), 1
    )
    count = jnp.zeros((BANDS, length), jnp.int32)
    for n in range(n_bounds):
        count = count + jnp.where(bounds_ref[0, n] <= sample, 1, 0)
    return (count & 1).astype(F32)


def spread_rows(mask, det):
    return jnp.broadcast_to(mask[:, None, :], (BANDS, det, TILE)).reshape(BANDS * det, TILE)


def pick_matrix(tiles_row, det):
    shape = (det * TILES, LANES)
    row = lax.broadcasted_iota(jnp.int32, shape, 0)
    lane = lax.broadcasted_iota(jnp.int32, shape, 1)
    return (row % det == lane % det) & ((row // det).astype(F32) == tiles_row)


def spread_matrix(tiles_column, det):
    shape = (LANES, det * TILES)
    row = lax.broadcasted_iota(jnp.int32, shape, 0)
    lane = lax.broadcasted_iota(jnp.int32, shape, 1)
    return (row % det == lane % det) & ((lane // det).astype(F32) == tiles_column)


def load_taps(raw_ref, rows_ref, last_ref, taps_ref, det):
    rows_ref[...] = raw_ref[...].reshape(det * BANDS, TAPS)[:, 0:TILE].astype(F32)
    last = raw_ref[...].reshape(det * BANDS, TAPS)[:, TILE:TAPS].astype(F32)
    last_ref[...] = jnp.broadcast_to(last, (det * BANDS, LANES))
    by_band = [rows_ref[pl.ds(b, det, stride=BANDS), :] for b in range(BANDS)]
    taps_ref[0:TILE, :] = jnp.concatenate(by_band, axis=0).T
    by_band = [last_ref[pl.ds(b, det, stride=BANDS), :] for b in range(BANDS)]
    taps_ref[TILE : TILE + 8, :] = jnp.concatenate(by_band, axis=0).T[0:8, :]


def build_bands(rows_ref, bands_ref):
    j = lax.broadcasted_iota(jnp.int32, (HALF, LANES), 0)
    m = lax.broadcasted_iota(jnp.int32, (HALF, LANES), 1)
    keep = jnp.where(m >= j, 1.0, 0.0).astype(BF16)

    def one(pair, _):
        row = jnp.broadcast_to(rows_ref[pl.ds(pair, 1), :], (HALF, LANES))
        turned = pltpu.roll(row, 0, 1, stride=1, stride_axis=0).astype(BF16)
        near = turned * keep
        bands_ref[pair, :, 0:LANES] = near
        bands_ref[pair, :, LANES : 2 * LANES] = turned - near
        return 0

    lax.fori_loop(0, rows_ref.shape[0], one, 0, unroll=8)


def adjoint_body(rest_ref, bands_ref, last_ref, sums, out_ref, length, det, finish):
    per_band = length // TILE
    per_det = BANDS * per_band + 8
    near_ref, far_ref, near_half, far_half = sums

    def one(d, _):
        base = pl.multiple_of(d * per_det, 8)
        for far in (far_ref, far_half):
            far[pl.ds(base, 8), :] = jnp.zeros((8, LANES), F32)
        for near in (near_ref, near_half):
            near[pl.ds(base + per_det - 8, 8), :] = jnp.zeros((8, LANES), F32)
        for b in range(BANDS):
            pair = b * det + d
            rest = rest_ref[pl.ds(pl.multiple_of(pair * 2 * per_band, 8), 2 * per_band), :]
            both = jnp.dot(
                rest[:, 0:HALF].astype(BF16), bands_ref[d * BANDS + b], preferred_element_type=F32
            )
            end = last_ref[pl.ds(d * BANDS + b, 1), :] * rest[0:per_band, :]
            here = pl.ds(base + b * per_band, per_band)
            after = pl.ds(base + b * per_band + 1, per_band)
            near_ref[here, :] = both[0:per_band, 0:LANES]
            far_ref[after, :] = both[0:per_band, LANES:] + end
            near_half[here, :] = both[per_band:, 0:LANES]
            far_half[after, :] = both[per_band:, LANES:]
        return 0

    lax.fori_loop(0, det, one, 0, unroll=UNROLL)
    for d in range(det):
        rows = slice(d * per_det, (d + 1) * per_det)
        near_ref[rows, :] = near_ref[rows, :] + far_ref[rows, :]
        near_half[rows, :] = near_half[rows, :] + far_half[rows, :]
    low = lax.broadcasted_iota(jnp.int32, (det, LANES), 1) < HALF

    def turned(i):
        return pltpu.roll(near_ref[pl.ds(i, det, stride=per_det), :], HALF, 1)

    here = turned(0)
    for b in range(BANDS):
        for i in range(b * per_band, (b + 1) * per_band):
            after = turned(i + 1)
            out_ref[:, i * TILE : (i + 1) * TILE] = (
                jnp.where(low, here, after) + near_half[pl.ds(i, det, stride=per_det), :]
            )
            here = after
        finish(b)


MESH = pl.DeviceIdType.MESH
PIECES = 4
COPIES = 2
UNROLL = 4


def load_signal(x_ref, ext_ref, length, det):
    for c in range(length // TILE):
        piece = jnp.concatenate(
            [x_ref[:, b * length + c * TILE : b * length + (c + 1) * TILE] for b in range(BANDS)],
            axis=0,
        )
        ext_ref[HALF + c * TILE : HALF + (c + 1) * TILE, :] = piece.astype(F32).T
    band = lane_band(det)
    last = ext_ref[length : length + HALF, :]
    first = ext_ref[HALF : 2 * HALF, :]
    ext_ref[0:HALF, :] = jnp.where(band > 0, pltpu.roll(last, det, 1), 0.0)
    ext_ref[HALF + length : 2 * HALF + length, :] = jnp.where(
        band < BANDS - 1, pltpu.roll(first, LANES - det, 1), 0.0
    )


def whole_kernel(
    dims, bounds_hbm, index_hbm, x_hbm, taps_hbm, weights_hbm, pos_hbm, wafer_hbm,
    out_hbm, skyout_hbm, out_ref, give,
    bounds_ref, index_ref, x_ref, raw_ref, weights_ref, pos_ref, wafer_ref, load,
    rows_ref, last_ref, taps_ref, bands_ref, rest_ref, near_ref, far_ref, near_half, far_half,
    ext_ref, mask_ref, tiles_ref, fsend, frecv, csend, crecv, tsend, trecv,
    filt, spread, gsend, grecv, hsend, hrecv, sky_b, sky_f, skyb_recv, skyf_recv,
    f_s, f_r, c_s, c_r, t_s, t_r, g_s, g_r, h_s, h_r, b_s, b_r, k_s, k_r,
):
    n_obs, td, det, length, slab, n_bounds = dims
    dets = det * td
    split = td // BANDS
    blocks = slab // TILE
    width = slab // PIECES
    folds = dets // TILE
    per_fold = td // folds
    count = n_obs * td
    group = count // COPIES
    stride = group // TILES
    own_rows = TILE // count
    obs = lax.axis_index("obs")
    me = lax.axis_index("td")
    linear = obs * td + me
    mine = lax.rem(linear // stride, TILES)
    within = lax.rem(linear, group)
    start = linear - within
    owner = lax.rem(linear, stride) == 0

    def place(device):
        return (device // td, lax.rem(device, td))

    def td_peer(k):
        return lax.rem(me + k, td)

    def td_source(k):
        return lax.rem(me + td - k, td)

    def obs_peer(k):
        return lax.rem(obs + k, n_obs)

    def obs_source(k):
        return lax.rem(obs + n_obs - k, n_obs)

    barrier = pltpu.get_barrier_semaphore()
    for k in range(1, td):
        pl.semaphore_signal(barrier, 1, device_id=(obs, td_peer(k)), device_id_type=MESH)
    for k in range(1, n_obs):
        pl.semaphore_signal(barrier, 1, device_id=(obs_peer(k), me), device_id_type=MESH)

    loads = [
        pltpu.make_async_copy(source, target, load.at[n])
        for n, (source, target) in enumerate(
            [
                (taps_hbm, raw_ref), (x_hbm, x_ref), (index_hbm, index_ref),
                (bounds_hbm, bounds_ref), (weights_hbm, weights_ref), (pos_hbm, pos_ref),
                (wafer_hbm, wafer_ref),
            ]
        )
    ]
    for copy in loads:
        copy.start()
    loads[0].wait()
    load_taps(raw_ref, rows_ref, last_ref, taps_ref, det)
    for copy in loads[1:]:
        copy.wait()

    row = lax.broadcasted_iota(jnp.int32, (blocks, LANES), 0)
    tile = jnp.zeros((blocks, LANES), jnp.int32)
    for n in range(blocks):
        tile = jnp.where(row == n, index_ref[0, n], tile)
    tsend[...] = tile.astype(F32)
    trecv[me] = tile.astype(F32)
    load_signal(x_ref, ext_ref, length, det)

    def tile_copy(k, slot):
        return pltpu.make_async_remote_copy(
            src_ref=tsend, dst_ref=trecv.at[slot], send_sem=t_s.at[k], recv_sem=t_r.at[k],
            device_id=(obs, td_peer(k)), device_id_type=MESH,
        )

    def signal_copy(h, k, slot):
        cols = pl.ds(pl.multiple_of(h * width, TILE), width)
        peer = td_peer(k)
        return pltpu.make_async_remote_copy(
            src_ref=fsend.at[peer, :, cols], dst_ref=frecv.at[slot, :, cols],
            send_sem=f_s.at[h, k], recv_sem=f_r.at[h, k],
            device_id=(obs, peer), device_id_type=MESH,
        )

    def clean_copy(h, k, slot):
        cols = pl.ds(pl.multiple_of(h * width, TILE), width)
        peer = td_peer(k)
        return pltpu.make_async_remote_copy(
            src_ref=csend.at[peer, :, cols], dst_ref=crecv.at[slot, :, cols],
            send_sem=c_s.at[h, k], recv_sem=c_r.at[h, k],
            device_id=(obs, peer), device_id_type=MESH,
        )

    def hit_copy(k, slot):
        peer = obs_peer(k)
        return pltpu.make_async_remote_copy(
            src_ref=hsend.at[lax.rem((peer * td + me) // stride, TILES)], dst_ref=hrecv.at[slot],
            send_sem=h_s.at[k], recv_sem=h_r.at[k],
            device_id=(peer, me), device_id_type=MESH,
        )

    def bin_copy(q, source):
        return pltpu.make_async_remote_copy(
            src_ref=gsend.at[lax.rem(q, TILES)], dst_ref=grecv.at[source],
            send_sem=g_s.at[q], recv_sem=g_r.at[source],
            device_id=place(q * stride), device_id_type=MESH,
        )

    def rounded_copy(device, p):
        rows = pl.ds(pl.multiple_of(lax.rem(lax.rem(device, td), per_fold) * det, det), det)
        return pltpu.make_async_remote_copy(
            src_ref=sky_b.at[rows], dst_ref=skyb_recv.at[p],
            send_sem=b_s.at[device], recv_sem=b_r.at[p],
            device_id=place(device), device_id_type=MESH,
        )

    def row_copy(device, p):
        return pltpu.make_async_remote_copy(
            src_ref=sky_f.at[device], dst_ref=skyf_recv.at[p],
            send_sem=k_s.at[device], recv_sem=k_r.at[p],
            device_id=place(device), device_id_type=MESH,
        )

    def each(number, do):
        def step(k, _):
            do(k)
            return 0

        lax.fori_loop(1, number, step, 0)

    def each_tile(do):
        def step(k, _):
            p = lax.rem(mine + k, TILES)

            @pl.when(start + p * stride != linear)
            def _():
                do(p)

            return 0

        lax.fori_loop(0, TILES, step, 0)

    def each_owner(do):
        def step(k, _):
            q = lax.rem(linear // stride + TILES + k, COPIES * TILES)

            @pl.when(q * stride != linear)
            def _():
                do(q)

            return 0

        lax.fori_loop(0, COPIES * TILES, step, 0)

    def each_device(do):
        each(count, lambda k: do(lax.rem(linear + k, count)))

    def each_near(do):
        each(group, lambda k: do(start + lax.rem(within + k, group)))

    def compute(p):
        quarter = p // PIECES
        h = lax.rem(p, PIECES)

        def chunk(c, _):
            inside = pl.multiple_of(h * width + c * TILE, TILE)
            base = pl.multiple_of(quarter * slab + inside, TILE)
            acc = jnp.zeros((TILE, LANES), F32)
            for k in range(TAPS):
                acc = acc + taps_ref[k : k + 1, :] * ext_ref[pl.ds(base + k, TILE), :]
            block = acc.T.astype(BF16)
            filt[quarter * blocks + h * (width // TILE) + c] = block
            for b in range(BANDS):
                fsend[b * split + quarter, :, pl.ds(inside, TILE)] = block[b * det : (b + 1) * det, :]
            return 0

        lax.fori_loop(0, width // TILE, chunk, 0)

    def send_piece(p):
        quarter = p // PIECES
        h = lax.rem(p, PIECES)

        def send(k):
            if split == 1:
                signal_copy(h, k, me).start()
            else:

                @pl.when(lax.rem(td_peer(k), split) == quarter)
                def _():
                    signal_copy(h, k, me).start()

        each(td, send)

    ahead = PIECES // 2

    def late(p, _):
        send_piece(p)
        return 0

    def step(p, _):
        compute(p)

        @pl.when(p == ahead - 1)
        def _():
            pl.semaphore_wait(barrier, td - 1 + n_obs - 1)
            each(td, lambda k: tile_copy(k, me).start())
            lax.fori_loop(0, ahead, late, 0)

        @pl.when(p >= ahead)
        def _():
            send_piece(p)

        return 0

    lax.fori_loop(0, split * PIECES, step, 0)
    frecv[me] = fsend[me]

    mask_ref[...] = scan_mask(bounds_ref, length, n_bounds)
    for n in range(length // TILE):
        filt[n] = filt[n] * spread_rows(mask_ref[:, n * TILE : (n + 1) * TILE], det).astype(BF16)
    each(td, lambda k: tile_copy(k, td_source(k)).wait_recv())
    lane = lax.broadcasted_iota(jnp.int32, (blocks, LANES), 1) // det
    for quarter in range(split):
        tile = trecv[quarter]
        for b in range(1, BANDS):
            tile = jnp.where(lane == b, trecv[b * split + quarter], tile)
        tiles_ref[quarter * blocks : (quarter + 1) * blocks, :] = tile
    sums = jnp.zeros((det * TILES, TILE), F32)
    for n in range(length // TILE):
        pick = jnp.where(pick_matrix(tiles_ref[n : n + 1, :], det), 1.0, 0.0).astype(BF16)
        sums = sums + jnp.dot(pick, filt[n], preferred_element_type=F32)
    gsend[...] = sums.reshape(TILES, det, TILE).astype(BF16)
    each_owner(lambda q: bin_copy(q, linear).start())
    first = lax.broadcasted_iota(jnp.int32, (TILES, LANES), 1) % det == 0
    which = lax.broadcasted_iota(jnp.int32, (TILES, LANES), 0).astype(F32)
    counts = jnp.zeros((TILES, TILE), F32)
    for n in range(length // TILE):
        mask = spread_rows(mask_ref[:, n * TILE : (n + 1) * TILE], det).astype(BF16)
        pick = jnp.where(first & (which == tiles_ref[n : n + 1, :]), 1.0, 0.0).astype(BF16)
        counts = counts + jnp.dot(pick, mask, preferred_element_type=F32)

    @pl.when(owner)
    def _():
        grecv[linear] = gsend[mine]
        level = lax.broadcasted_iota(jnp.int32, (TILES, 8, TILE), 1)
        rows = jnp.broadcast_to(counts[:, None, :], (TILES, 8, TILE))
        weights = weights_ref[...].astype(F32)
        for q in range(folds):
            rows = jnp.where(level == q + 1, weights[:, None, q * TILE : (q + 1) * TILE], rows)
        hsend[...] = rows
        hrecv[obs] = hsend[mine]
        each(n_obs, lambda k: hit_copy(k, obs).start())

    p_high, p_low = projector(pos_ref, wafer_ref, dets)

    for h in range(PIECES):
        each(td, lambda k: signal_copy(h, k, td_source(k)).wait_recv())
        cols = slice(h * width, (h + 1) * width)
        cleaned = clean(p_high, p_low, frecv[:, :, cols].reshape(dets, width))
        csend[:, :, cols] = cleaned.reshape(td, det, width)
        each(td, lambda k: clean_copy(h, k, me).start())
    crecv[me] = csend[me]

    def band_rows(n):
        quarter, inside = n // blocks, n % blocks
        cols = slice(inside * TILE, (inside + 1) * TILE)
        return jnp.concatenate([crecv[b * split + quarter, :, cols] for b in range(BANDS)], axis=0)

    build_bands(rows_ref, bands_ref)
    @pl.when(owner)
    def _():
        each(n_obs, lambda k: hit_copy(k, obs_source(k)).wait_recv())
        each_device(lambda d: bin_copy(linear // stride, d).wait_recv())
        total = jnp.zeros((TILE, TILE), F32)
        hit = jnp.zeros((TILE, TILE), F32)
        for o in range(n_obs):
            binned = grecv[o * td : (o + 1) * td].reshape(dets, TILE)
            fitted = jnp.dot(p_high, binned, preferred_element_type=F32) + jnp.dot(
                p_low, binned, preferred_element_type=F32
            )
            left = binned.astype(F32) - fitted
            for q in range(folds):
                weight = jnp.broadcast_to(hrecv[o, q + 1 : q + 2, :], (TILE, TILE)).T
                total = total + weight * left[q * TILE : (q + 1) * TILE, :]
                hit = hit + weight * hrecv[o, 0:1, :]
        sky = total / (hit + prior_weight)
        sky_b[...] = sky.astype(BF16)
        for d in range(count):
            sky_f[d] = sky[d * own_rows : (d + 1) * own_rows, :]
        each_near(lambda d: rounded_copy(d, mine).start())
        each_near(lambda d: row_copy(d, mine).start())
        own = pl.ds(pl.multiple_of(lax.rem(me, per_fold) * det, det), det)
        skyb_recv[mine] = sky_b[own, :]
        skyf_recv[mine] = sky_f[linear]

    grid = jnp.concatenate(
        [tiles_ref[...], jnp.zeros((LANES - length // TILE, LANES), F32)], axis=0
    ).T
    for n in range(length // TILE):
        spread[n] = jnp.where(spread_matrix(grid[:, n : n + 1], det), 1.0, 0.0).astype(BF16)
    for h in range(PIECES):
        each(td, lambda k: clean_copy(h, k, td_source(k)).wait_recv())
    each_tile(lambda p: rounded_copy(linear, p).wait_recv())
    chosen_from = skyb_recv[...].reshape(TILES * det, TILE)
    for n in range(length // TILE):
        mask = spread_rows(mask_ref[:, n * TILE : (n + 1) * TILE], det)
        chosen = jnp.dot(spread[n], chosen_from, preferred_element_type=F32)
        residual = (mask * (band_rows(n).astype(F32) - chosen)).astype(BF16)
        rest = residual.astype(F32)
        rest_ref[pl.ds(n, LANES, stride=2 * length // TILE), :] = rest
        rest_ref[pl.ds(length // TILE + n, LANES, stride=2 * length // TILE), :] = pltpu.roll(
            rest, HALF, 1
        )

    def give_copy(b):
        cols = pl.ds(b * length, length)
        return pltpu.make_async_copy(out_ref.at[:, cols], out_hbm.at[:, cols], give.at[b])

    sky_copy = pltpu.make_async_copy(skyf_recv, skyout_hbm, give.at[BANDS])
    adjoint_body(
        rest_ref, bands_ref, last_ref, (near_ref, far_ref, near_half, far_half), out_ref, length, det,
        lambda b: give_copy(b).start(),
    )

    each_tile(lambda p: row_copy(linear, p).wait_recv())
    sky_copy.start()
    each(td, lambda k: tile_copy(k, me).wait_send())
    for h in range(PIECES):
        each(td, lambda k: signal_copy(h, k, me).wait_send())
        each(td, lambda k: clean_copy(h, k, me).wait_send())
    each_owner(lambda q: bin_copy(q, linear).wait_send())

    for b in range(BANDS):
        give_copy(b).wait()
    sky_copy.wait()

    @pl.when(owner)
    def _():
        each(n_obs, lambda k: hit_copy(k, obs).wait_send())
        each_near(lambda d: rounded_copy(d, mine).wait_send())
        each_near(lambda d: row_copy(d, mine).wait_send())


HB = pl.BlockSpec(memory_space=pltpu.HBM)
CUTS = 4


def hand_over(out_ref, sky_ref, out_hbm, sky_hbm, held, sky_held, taken, given):
    width = out_ref.shape[1] // CUTS
    pieces = [(sky_ref, sky_held, sky_hbm)]
    for n in range(CUTS):
        cols = pl.ds(n * width, width)
        pieces.append((out_ref.at[:, cols], held.at[:, cols], out_hbm.at[:, cols]))
    copies = []
    for n, (source, middle, target) in enumerate(pieces):
        take = pltpu.make_async_copy(source, middle, taken.at[n])
        take.start()
        copies.append((take, pltpu.make_async_copy(middle, target, given.at[n])))
    for take, give in copies:
        take.wait()
        give.start()
    for _, give in copies:
        give.wait()


def local(timestreams, filter_taps, scan_bounds, tile_index, det_weights, positions, wafer_group):
    _, det, samples = timestreams.shape
    td = lax.axis_size("td")
    n_obs = lax.axis_size("obs")
    dets = det * td
    length = samples // BANDS
    slab = samples // td
    blocks = slab // TILE
    count = n_obs * td
    own_rows = TILE // count
    dims = (n_obs, td, det, length, slab, scan_bounds.shape[1])
    dma = pltpu.SemaphoreType.DMA
    out, sky = pl.pallas_call(
        functools.partial(whole_kernel, dims),
        out_shape=(
            jax.ShapeDtypeStruct((det, samples), F32),
            jax.ShapeDtypeStruct((TILES, own_rows, TILE), F32),
        ),
        in_specs=[HB] * 7,
        out_specs=(HB, HB),
        scratch_shapes=[
            pltpu.VMEM((det, samples), F32),
            dma((BANDS + 1,)),
            pltpu.SMEM(scan_bounds.shape, jnp.int32),
            pltpu.SMEM(tile_index.shape, jnp.int32),
            pltpu.VMEM((det, samples), BF16),
            pltpu.VMEM((det, BANDS, TAPS), BF16),
            pltpu.VMEM((1, dets), BF16),
            pltpu.VMEM((2, dets), F32),
            pltpu.VMEM((1, dets), jnp.int32),
            dma((7,)),
            pltpu.VMEM((det * BANDS, LANES), F32),
            pltpu.VMEM((det * BANDS, LANES), F32),
            pltpu.VMEM((TILE + 8, LANES), F32),
            pltpu.VMEM((det * BANDS, HALF, 2 * LANES), BF16),
            pltpu.VMEM((2 * det * samples // TILE, LANES), F32),
            pltpu.VMEM((det * (samples // TILE + 8), LANES), F32),
            pltpu.VMEM((det * (samples // TILE + 8), LANES), F32),
            pltpu.VMEM((det * (samples // TILE + 8), LANES), F32),
            pltpu.VMEM((det * (samples // TILE + 8), LANES), F32),
            pltpu.VMEM((length + 2 * HALF, LANES), F32),
            pltpu.VMEM((BANDS, length), F32),
            pltpu.VMEM((length // TILE, LANES), F32),
            pltpu.VMEM((td, det, slab), BF16),
            pltpu.VMEM((td, det, slab), BF16),
            pltpu.VMEM((td, det, slab), BF16),
            pltpu.VMEM((td, det, slab), BF16),
            pltpu.VMEM((blocks, LANES), F32),
            pltpu.VMEM((td, blocks, LANES), F32),
            pltpu.VMEM((length // TILE, LANES, TILE), BF16),
            pltpu.VMEM((length // TILE, LANES, det * TILES), BF16),
            pltpu.VMEM((TILES, det, TILE), BF16),
            pltpu.VMEM((count, det, TILE), BF16),
            pltpu.VMEM((TILES, 8, TILE), F32),
            pltpu.VMEM((n_obs, 8, TILE), F32),
            pltpu.VMEM((TILE, TILE), BF16),
            pltpu.VMEM((count, own_rows, TILE), F32),
            pltpu.VMEM((TILES, det, TILE), BF16),
            pltpu.VMEM((TILES, own_rows, TILE), F32),
            dma((PIECES, td)), dma((PIECES, td)), dma((PIECES, td)), dma((PIECES, td)),
            dma((td,)), dma((td,)), dma((COPIES * TILES,)), dma((count,)),
            dma((n_obs,)), dma((n_obs,)), dma((count,)), dma((TILES,)),
            dma((count,)), dma((TILES,)),
        ],
        compiler_params=pltpu.CompilerParams(
            collective_id=0, has_side_effects=True, vmem_limit_bytes=63 << 20
        ),
    )(
        scan_bounds, tile_index, timestreams[0], filter_taps[0], det_weights, positions,
        wafer_group.reshape(1, dets),
    )
    out, sky = pl.pallas_call(
        hand_over,
        out_shape=(
            jax.ShapeDtypeStruct((det, samples), F32),
            jax.ShapeDtypeStruct((TILES, own_rows, TILE), F32),
        ),
        in_specs=[HB, HB],
        out_specs=(HB, HB),
        scratch_shapes=[
            pltpu.VMEM((det, samples), F32), pltpu.VMEM((TILES, own_rows, TILE), F32),
            dma((CUTS + 1,)), dma((CUTS + 1,)),
        ],
        compiler_params=pltpu.CompilerParams(vmem_limit_bytes=63 << 20),
    )(out, sky)
    return out[None], sky


def solution(mesh):
    placed = (
        P("obs", "td", None),
        P("obs", "td", None, None),
        P("obs", None),
        P("obs", "td"),
        P("obs", None),
        P(),
        P(),
    )
    return jax.shard_map(
        local,
        mesh=mesh,
        in_specs=placed,
        out_specs=(P("obs", "td", None), P(None, ("obs", "td"), None)),
        check_vma=False,
    )
```

```python
import functools

import jax
import jax.numpy as jnp
from jax import lax
from jax.experimental import pallas as pl
from jax.experimental.pallas import tpu as pltpu
from jax.sharding import PartitionSpec as P

TAPS = 129
HALF = 64
BANDS = 8
TILE = 128
POLY = 6
TILES = 16
LANES = 128
prior_weight = 1.0
F32 = jnp.float32
BF16 = jnp.bfloat16


def projector(pos_ref, wafer_ref, dets):
    x = pos_ref[0:1, :]
    y = pos_ref[1:2, :]
    rows = [jnp.ones_like(x), x, y, x * x, x * y, y * y]
    q = [r.astype(BF16).astype(F32) for r in rows]
    group = jnp.broadcast_to(wafer_ref[...].astype(F32), (dets, dets))
    same = group == group.T
    same_b = jnp.where(same, 1.0, 0.0).astype(BF16)
    pairs = [(i, j) for i in range(POLY) for j in range(i + 1)]
    products = jnp.concatenate(
        [q[i] * q[j] for i, j in pairs] + [jnp.zeros((32 - len(pairs), dets), F32)], axis=0
    )
    high = products.astype(BF16)
    low = (products - high.astype(F32)).astype(BF16)
    gram = jnp.dot(high, same_b, preferred_element_type=F32) + jnp.dot(
        low, same_b, preferred_element_type=F32
    )
    entry = {pair: gram[n : n + 1, :] for n, pair in enumerate(pairs)}
    factor, inv, white = {}, {}, []
    for i in range(POLY):
        for j in range(i + 1):
            value = entry[(i, j)]
            for k in range(j):
                value = value - factor[(i, k)] * factor[(j, k)]
            if i == j:
                factor[(i, i)] = jnp.sqrt(value)
                inv[i] = 1.0 / factor[(i, i)]
            else:
                factor[(i, j)] = value * inv[j]
        value = q[i]
        for k in range(i):
            value = value - factor[(i, k)] * white[k]
        white.append(value * inv[i])
    whitened = jnp.concatenate(white + [jnp.zeros((8 - POLY, dets), F32)], axis=0)
    columns = jnp.concatenate([whitened, jnp.zeros((LANES - 8, dets), F32)], axis=0).T
    outer = columns[:, 0:1] * white[0]
    for m in range(1, POLY):
        outer = outer + columns[:, m : m + 1] * white[m]
    outer = jnp.where(same, outer, 0.0)
    p_high = outer.astype(BF16)
    p_low = (outer - p_high.astype(F32)).astype(BF16)
    return p_high, p_low


def clean(p_high, p_low, gathered):
    fitted = jnp.dot(p_high, gathered, preferred_element_type=F32) + jnp.dot(
        p_low, gathered, preferred_element_type=F32
    )
    return (gathered.astype(F32) - fitted).astype(BF16)


def scan_mask(bounds_ref, length, n_bounds):
    sample = lax.broadcasted_iota(jnp.int32, (BANDS, length), 0) * length + lax.broadcasted_iota(
        jnp.int32, (BANDS, length), 1
    )
    count = jnp.zeros((BANDS, length), jnp.int32)
    for n in range(n_bounds):
        count = count + jnp.where(bounds_ref[0, n] <= sample, 1, 0)
    return (count & 1).astype(F32)


def spread_rows(mask, det):
    return jnp.broadcast_to(mask[:, None, :], (BANDS, det, TILE)).reshape(BANDS * det, TILE)


def pick_matrix(tiles_row, det):
    shape = (det * TILES, LANES)
    row = lax.broadcasted_iota(jnp.int32, shape, 0)
    lane = lax.broadcasted_iota(jnp.int32, shape, 1)
    return (row % det == lane % det) & ((row // det).astype(F32) == tiles_row)


def spread_matrix(tiles_column, det):
    shape = (LANES, det * TILES)
    row = lax.broadcasted_iota(jnp.int32, shape, 0)
    lane = lax.broadcasted_iota(jnp.int32, shape, 1)
    return (row % det == lane % det) & ((lane // det).astype(F32) == tiles_column)


def load_taps(raw_ref, rows_ref, last_ref, det):
    taps = raw_ref[...].reshape(det * BANDS, TAPS)
    rows_ref[...] = taps[:, 0:TILE].astype(F32)
    last_ref[...] = jnp.broadcast_to(taps[:, TILE:TAPS].astype(F32), (det * BANDS, LANES))


def build_bands(rows_ref, last_ref, bands_ref):
    j = lax.broadcasted_iota(jnp.int32, (HALF, LANES), 0)
    m = lax.broadcasted_iota(jnp.int32, (HALF, LANES), 1)
    keep = jnp.where(m >= j, 1.0, 0.0).astype(BF16)
    same = jnp.where(m == j, 1.0, 0.0).astype(BF16)

    def one(pair, _):
        row = jnp.broadcast_to(rows_ref[pl.ds(pair, 1), :], (HALF, LANES))
        last = jnp.broadcast_to(last_ref[pl.ds(pair, 1), :], (HALF, LANES)).astype(BF16)
        turned = pltpu.roll(row, 0, 1, stride=1, stride_axis=0).astype(BF16)
        near = turned * keep
        bands_ref[pair, :, 0:LANES] = near
        bands_ref[pair, :, LANES : 2 * LANES] = (turned - near) + last * same
        return 0

    lax.fori_loop(0, rows_ref.shape[0], one, 0, unroll=8)


def load_signal(x_ref, block_ref, shift_ref, det):
    total = x_ref.shape[1] // TILE
    low = lax.broadcasted_iota(jnp.int32, (det, LANES), 1) < HALF
    before = jnp.zeros((det, LANES), F32)
    for i in range(total + 1):
        rows = pl.ds(i, det, stride=total + 8)
        if i < total:
            block = x_ref[:, i * TILE : (i + 1) * TILE].astype(F32)
        else:
            block = jnp.zeros((det, LANES), F32)
        block_ref[rows, :] = block
        turned = pltpu.roll(block, HALF, 1)
        shift_ref[rows, :] = jnp.where(low, before, turned)
        before = turned


def forward_body(block_ref, shift_ref, bands_ref, halves_ref, length, det):
    per_band = length // TILE
    per_det = BANDS * per_band + 8

    def one(d, _):
        base = pl.multiple_of(d * per_det, 8)
        for b in range(BANDS):
            here = pl.ds(base + b * per_band, per_band)
            after = pl.ds(base + b * per_band + 1, per_band)
            window = jnp.concatenate(
                [
                    jnp.concatenate([source[here, :], source[after, :]], axis=1)
                    for source in (shift_ref, block_ref)
                ],
                axis=0,
            ).astype(BF16)
            rows = pl.ds(pl.multiple_of((b * det + d) * 2 * per_band, 8), 2 * per_band)
            halves_ref[rows, 0:HALF] = lax.dot_general(
                window, bands_ref[d * BANDS + b], (((1,), (1,)), ((), ())),
                preferred_element_type=F32,
            )
        return 0

    lax.fori_loop(0, det, one, 0, unroll=UNROLL)


def adjoint_body(rest_ref, bands_ref, sums, out_ref, length, det, finish):
    per_band = length // TILE
    per_det = BANDS * per_band + 8
    near_ref, far_ref, near_half, far_half = sums

    def one(d, _):
        base = pl.multiple_of(d * per_det, 8)
        for far in (far_ref, far_half):
            far[pl.ds(base, 8), :] = jnp.zeros((8, LANES), F32)
        for near in (near_ref, near_half):
            near[pl.ds(base + per_det - 8, 8), :] = jnp.zeros((8, LANES), F32)
        for b in range(BANDS):
            pair = b * det + d
            rest = rest_ref[pl.ds(pl.multiple_of(pair * 2 * per_band, 8), 2 * per_band), :]
            both = jnp.dot(
                rest[:, 0:HALF].astype(BF16), bands_ref[d * BANDS + b], preferred_element_type=F32
            )
            here = pl.ds(base + b * per_band, per_band)
            after = pl.ds(base + b * per_band + 1, per_band)
            near_ref[here, :] = both[0:per_band, 0:LANES]
            far_ref[after, :] = both[0:per_band, LANES:]
            near_half[here, :] = both[per_band:, 0:LANES]
            far_half[after, :] = both[per_band:, LANES:]
        return 0

    lax.fori_loop(0, det, one, 0, unroll=UNROLL)
    for d in range(det):
        rows = slice(d * per_det, (d + 1) * per_det)
        near_ref[rows, :] = near_ref[rows, :] + far_ref[rows, :]
        near_half[rows, :] = near_half[rows, :] + far_half[rows, :]
    low = lax.broadcasted_iota(jnp.int32, (det, LANES), 1) < HALF

    def turned(i):
        return pltpu.roll(near_ref[pl.ds(i, det, stride=per_det), :], HALF, 1)

    here = turned(0)
    for b in range(BANDS):
        for i in range(b * per_band, (b + 1) * per_band):
            after = turned(i + 1)
            out_ref[:, i * TILE : (i + 1) * TILE] = (
                jnp.where(low, here, after) + near_half[pl.ds(i, det, stride=per_det), :]
            )
            here = after
        finish(b)


MESH = pl.DeviceIdType.MESH
PIECES = 4
COPIES = 2
UNROLL = 4


def whole_kernel(
    dims, bounds_hbm, index_hbm, x_hbm, taps_hbm, weights_hbm, pos_hbm, wafer_hbm,
    out_hbm, skyout_hbm, out_ref, give,
    bounds_ref, index_ref, x_ref, raw_ref, weights_ref, pos_ref, wafer_ref, load,
    rows_ref, last_ref, bands_ref, rest_ref, near_ref, far_ref, near_half, far_half,
    mask_ref, tiles_ref, fsend, frecv, csend, crecv, tsend, trecv,
    filt, spread, gsend, grecv, hsend, hrecv, sky_b, sky_f, skyb_recv, skyf_recv,
    f_s, f_r, c_s, c_r, t_s, t_r, g_s, g_r, h_s, h_r, b_s, b_r, k_s, k_r,
):
    n_obs, td, det, length, slab, n_bounds = dims
    dets = det * td
    split = td // BANDS
    blocks = slab // TILE
    width = slab // PIECES
    folds = dets // TILE
    per_fold = td // folds
    count = n_obs * td
    group = count // COPIES
    stride = group // TILES
    own_rows = TILE // count
    obs = lax.axis_index("obs")
    me = lax.axis_index("td")
    linear = obs * td + me
    mine = lax.rem(linear // stride, TILES)
    within = lax.rem(linear, group)
    start = linear - within
    owner = lax.rem(linear, stride) == 0

    def place(device):
        return (device // td, lax.rem(device, td))

    def td_peer(k):
        return lax.rem(me + k, td)

    def td_source(k):
        return lax.rem(me + td - k, td)

    def obs_peer(k):
        return lax.rem(obs + k, n_obs)

    def obs_source(k):
        return lax.rem(obs + n_obs - k, n_obs)

    barrier = pltpu.get_barrier_semaphore()
    for k in range(1, td):
        pl.semaphore_signal(barrier, 1, device_id=(obs, td_peer(k)), device_id_type=MESH)
    for k in range(1, n_obs):
        pl.semaphore_signal(barrier, 1, device_id=(obs_peer(k), me), device_id_type=MESH)

    loads = [
        pltpu.make_async_copy(source, target, load.at[n])
        for n, (source, target) in enumerate(
            [
                (taps_hbm, raw_ref), (x_hbm, x_ref), (index_hbm, index_ref),
                (bounds_hbm, bounds_ref), (weights_hbm, weights_ref), (pos_hbm, pos_ref),
                (wafer_hbm, wafer_ref),
            ]
        )
    ]
    for copy in loads:
        copy.start()
    def tile_copy(k, slot):
        return pltpu.make_async_remote_copy(
            src_ref=tsend, dst_ref=trecv.at[slot], send_sem=t_s.at[k], recv_sem=t_r.at[k],
            device_id=(obs, td_peer(k)), device_id_type=MESH,
        )

    def each(number, do):
        def step(k, _):
            do(k)
            return 0

        lax.fori_loop(1, number, step, 0)

    loads[0].wait()
    load_taps(raw_ref, rows_ref, last_ref, det)
    build_bands(rows_ref, last_ref, bands_ref)
    loads[2].wait()
    row = lax.broadcasted_iota(jnp.int32, (blocks, LANES), 0)
    tile = jnp.zeros((blocks, LANES), jnp.int32)
    for n in range(blocks):
        tile = jnp.where(row == n, index_ref[0, n], tile)
    tsend[...] = tile.astype(F32)
    trecv[me] = tile.astype(F32)
    pl.semaphore_wait(barrier, td - 1 + n_obs - 1)
    each(td, lambda k: tile_copy(k, me).start())
    for n in (1, 3, 4, 5, 6):
        loads[n].wait()
    load_signal(x_ref, near_ref, far_ref, det)
    forward_body(near_ref, far_ref, bands_ref, rest_ref, length, det)

    def signal_copy(h, k, slot):
        cols = pl.ds(pl.multiple_of(h * width, TILE), width)
        peer = td_peer(k)
        return pltpu.make_async_remote_copy(
            src_ref=fsend.at[peer, :, cols], dst_ref=frecv.at[slot, :, cols],
            send_sem=f_s.at[h, k], recv_sem=f_r.at[h, k],
            device_id=(obs, peer), device_id_type=MESH,
        )

    def clean_copy(h, k, slot):
        cols = pl.ds(pl.multiple_of(h * width, TILE), width)
        peer = td_peer(k)
        return pltpu.make_async_remote_copy(
            src_ref=csend.at[peer, :, cols], dst_ref=crecv.at[slot, :, cols],
            send_sem=c_s.at[h, k], recv_sem=c_r.at[h, k],
            device_id=(obs, peer), device_id_type=MESH,
        )

    def hit_copy(k, slot):
        peer = obs_peer(k)
        return pltpu.make_async_remote_copy(
            src_ref=hsend.at[lax.rem((peer * td + me) // stride, TILES)], dst_ref=hrecv.at[slot],
            send_sem=h_s.at[k], recv_sem=h_r.at[k],
            device_id=(peer, me), device_id_type=MESH,
        )

    def bin_copy(q, source):
        return pltpu.make_async_remote_copy(
            src_ref=gsend.at[lax.rem(q, TILES)], dst_ref=grecv.at[source],
            send_sem=g_s.at[q], recv_sem=g_r.at[source],
            device_id=place(q * stride), device_id_type=MESH,
        )

    def rounded_copy(device, p):
        rows = pl.ds(pl.multiple_of(lax.rem(lax.rem(device, td), per_fold) * det, det), det)
        return pltpu.make_async_remote_copy(
            src_ref=sky_b.at[rows], dst_ref=skyb_recv.at[p],
            send_sem=b_s.at[device], recv_sem=b_r.at[p],
            device_id=place(device), device_id_type=MESH,
        )

    def row_copy(device, p):
        return pltpu.make_async_remote_copy(
            src_ref=sky_f.at[device], dst_ref=skyf_recv.at[p],
            send_sem=k_s.at[device], recv_sem=k_r.at[p],
            device_id=place(device), device_id_type=MESH,
        )

    def each_tile(do):
        def step(k, _):
            p = lax.rem(mine + k, TILES)

            @pl.when(start + p * stride != linear)
            def _():
                do(p)

            return 0

        lax.fori_loop(0, TILES, step, 0)

    def each_owner(do):
        def step(k, _):
            q = lax.rem(linear // stride + TILES + k, COPIES * TILES)

            @pl.when(q * stride != linear)
            def _():
                do(q)

            return 0

        lax.fori_loop(0, COPIES * TILES, step, 0)

    def each_device(do):
        each(count, lambda k: do(lax.rem(linear + k, count)))

    def each_near(do):
        each(group, lambda k: do(start + lax.rem(within + k, group)))

    per_band = length // TILE
    low = lax.broadcasted_iota(jnp.int32, (LANES, LANES), 1) < HALF

    def finish_block(n):
        early = rest_ref[pl.ds(n, LANES, stride=2 * per_band), :]
        late = rest_ref[pl.ds(per_band + n, LANES, stride=2 * per_band), :]
        block = jnp.where(low, early, pltpu.roll(late, HALF, 1)).astype(BF16)
        filt[n] = block
        quarter, inside = n // blocks, n % blocks
        for b in range(BANDS):
            fsend[b * split + quarter, :, inside * TILE : (inside + 1) * TILE] = block[
                b * det : (b + 1) * det, :
            ]

    def send_piece(p):
        quarter, h = p // PIECES, p % PIECES

        def send(k):
            if split == 1:
                signal_copy(h, k, me).start()
            else:

                @pl.when(lax.rem(td_peer(k), split) == quarter)
                def _():
                    signal_copy(h, k, me).start()

        each(td, send)

    for p in range(split * PIECES):
        for c in range(width // TILE):
            finish_block(p * (width // TILE) + c)
        send_piece(p)
    frecv[me] = fsend[me]

    mask_ref[...] = scan_mask(bounds_ref, length, n_bounds)
    for n in range(length // TILE):
        filt[n] = filt[n] * spread_rows(mask_ref[:, n * TILE : (n + 1) * TILE], det).astype(BF16)
    each(td, lambda k: tile_copy(k, td_source(k)).wait_recv())
    lane = lax.broadcasted_iota(jnp.int32, (blocks, LANES), 1) // det
    for quarter in range(split):
        tile = trecv[quarter]
        for b in range(1, BANDS):
            tile = jnp.where(lane == b, trecv[b * split + quarter], tile)
        tiles_ref[quarter * blocks : (quarter + 1) * blocks, :] = tile
    sums = jnp.zeros((det * TILES, TILE), F32)
    for n in range(length // TILE):
        pick = jnp.where(pick_matrix(tiles_ref[n : n + 1, :], det), 1.0, 0.0).astype(BF16)
        sums = sums + jnp.dot(pick, filt[n], preferred_element_type=F32)
    gsend[...] = sums.reshape(TILES, det, TILE).astype(BF16)
    each_owner(lambda q: bin_copy(q, linear).start())
    first = lax.broadcasted_iota(jnp.int32, (TILES, LANES), 1) % det == 0
    which = lax.broadcasted_iota(jnp.int32, (TILES, LANES), 0).astype(F32)
    counts = jnp.zeros((TILES, TILE), F32)
    for n in range(length // TILE):
        mask = spread_rows(mask_ref[:, n * TILE : (n + 1) * TILE], det).astype(BF16)
        pick = jnp.where(first & (which == tiles_ref[n : n + 1, :]), 1.0, 0.0).astype(BF16)
        counts = counts + jnp.dot(pick, mask, preferred_element_type=F32)

    @pl.when(owner)
    def _():
        grecv[linear] = gsend[mine]
        level = lax.broadcasted_iota(jnp.int32, (TILES, 8, TILE), 1)
        rows = jnp.broadcast_to(counts[:, None, :], (TILES, 8, TILE))
        weights = weights_ref[...].astype(F32)
        for q in range(folds):
            rows = jnp.where(level == q + 1, weights[:, None, q * TILE : (q + 1) * TILE], rows)
        hsend[...] = rows
        hrecv[obs] = hsend[mine]
        each(n_obs, lambda k: hit_copy(k, obs).start())

    p_high, p_low = projector(pos_ref, wafer_ref, dets)

    for h in range(PIECES):
        each(td, lambda k: signal_copy(h, k, td_source(k)).wait_recv())
        cols = slice(h * width, (h + 1) * width)
        cleaned = clean(p_high, p_low, frecv[:, :, cols].reshape(dets, width))
        csend[:, :, cols] = cleaned.reshape(td, det, width)
        each(td, lambda k: clean_copy(h, k, me).start())
    crecv[me] = csend[me]

    def band_rows(n):
        quarter, inside = n // blocks, n % blocks
        cols = slice(inside * TILE, (inside + 1) * TILE)
        return jnp.concatenate([crecv[b * split + quarter, :, cols] for b in range(BANDS)], axis=0)

    @pl.when(owner)
    def _():
        each(n_obs, lambda k: hit_copy(k, obs_source(k)).wait_recv())
        each_device(lambda d: bin_copy(linear // stride, d).wait_recv())
        total = jnp.zeros((TILE, TILE), F32)
        hit = jnp.zeros((TILE, TILE), F32)
        for o in range(n_obs):
            binned = grecv[o * td : (o + 1) * td].reshape(dets, TILE)
            fitted = jnp.dot(p_high, binned, preferred_element_type=F32) + jnp.dot(
                p_low, binned, preferred_element_type=F32
            )
            left = binned.astype(F32) - fitted
            for q in range(folds):
                weight = jnp.broadcast_to(hrecv[o, q + 1 : q + 2, :], (TILE, TILE)).T
                total = total + weight * left[q * TILE : (q + 1) * TILE, :]
                hit = hit + weight * hrecv[o, 0:1, :]
        sky = total / (hit + prior_weight)
        sky_b[...] = sky.astype(BF16)
        for d in range(count):
            sky_f[d] = sky[d * own_rows : (d + 1) * own_rows, :]
        each_near(lambda d: rounded_copy(d, mine).start())
        each_near(lambda d: row_copy(d, mine).start())
        own = pl.ds(pl.multiple_of(lax.rem(me, per_fold) * det, det), det)
        skyb_recv[mine] = sky_b[own, :]
        skyf_recv[mine] = sky_f[linear]

    grid = jnp.concatenate(
        [tiles_ref[...], jnp.zeros((LANES - length // TILE, LANES), F32)], axis=0
    ).T
    for n in range(length // TILE):
        spread[n] = jnp.where(spread_matrix(grid[:, n : n + 1], det), 1.0, 0.0).astype(BF16)
    for h in range(PIECES):
        each(td, lambda k: clean_copy(h, k, td_source(k)).wait_recv())
    each_tile(lambda p: rounded_copy(linear, p).wait_recv())
    chosen_from = skyb_recv[...].reshape(TILES * det, TILE)
    for n in range(length // TILE):
        mask = spread_rows(mask_ref[:, n * TILE : (n + 1) * TILE], det)
        chosen = jnp.dot(spread[n], chosen_from, preferred_element_type=F32)
        residual = (mask * (band_rows(n).astype(F32) - chosen)).astype(BF16)
        rest = residual.astype(F32)
        rest_ref[pl.ds(n, LANES, stride=2 * length // TILE), :] = rest
        rest_ref[pl.ds(length // TILE + n, LANES, stride=2 * length // TILE), :] = pltpu.roll(
            rest, HALF, 1
        )

    def give_copy(b):
        cols = pl.ds(b * length, length)
        return pltpu.make_async_copy(out_ref.at[:, cols], out_hbm.at[:, cols], give.at[b])

    sky_copy = pltpu.make_async_copy(skyf_recv, skyout_hbm, give.at[BANDS])
    adjoint_body(
        rest_ref, bands_ref, (near_ref, far_ref, near_half, far_half), out_ref, length, det,
        lambda b: give_copy(b).start(),
    )

    each_tile(lambda p: row_copy(linear, p).wait_recv())
    sky_copy.start()
    each(td, lambda k: tile_copy(k, me).wait_send())
    for h in range(PIECES):
        each(td, lambda k: signal_copy(h, k, me).wait_send())
        each(td, lambda k: clean_copy(h, k, me).wait_send())
    each_owner(lambda q: bin_copy(q, linear).wait_send())

    for b in range(BANDS):
        give_copy(b).wait()
    sky_copy.wait()

    @pl.when(owner)
    def _():
        each(n_obs, lambda k: hit_copy(k, obs).wait_send())
        each_near(lambda d: rounded_copy(d, mine).wait_send())
        each_near(lambda d: row_copy(d, mine).wait_send())


HB = pl.BlockSpec(memory_space=pltpu.HBM)
CUTS = 4


def hand_over(out_ref, sky_ref, out_hbm, sky_hbm, held, sky_held, taken, given):
    width = out_ref.shape[1] // CUTS
    pieces = [(sky_ref, sky_held, sky_hbm)]
    for n in range(CUTS):
        cols = pl.ds(n * width, width)
        pieces.append((out_ref.at[:, cols], held.at[:, cols], out_hbm.at[:, cols]))
    copies = []
    for n, (source, middle, target) in enumerate(pieces):
        take = pltpu.make_async_copy(source, middle, taken.at[n])
        take.start()
        copies.append((take, pltpu.make_async_copy(middle, target, given.at[n])))
    for take, give in copies:
        take.wait()
        give.start()
    for _, give in copies:
        give.wait()


def local(timestreams, filter_taps, scan_bounds, tile_index, det_weights, positions, wafer_group):
    _, det, samples = timestreams.shape
    td = lax.axis_size("td")
    n_obs = lax.axis_size("obs")
    dets = det * td
    length = samples // BANDS
    slab = samples // td
    blocks = slab // TILE
    count = n_obs * td
    own_rows = TILE // count
    dims = (n_obs, td, det, length, slab, scan_bounds.shape[1])
    dma = pltpu.SemaphoreType.DMA
    out, sky = pl.pallas_call(
        functools.partial(whole_kernel, dims),
        out_shape=(
            jax.ShapeDtypeStruct((det, samples), F32),
            jax.ShapeDtypeStruct((TILES, own_rows, TILE), F32),
        ),
        in_specs=[HB] * 7,
        out_specs=(HB, HB),
        scratch_shapes=[
            pltpu.VMEM((det, samples), F32),
            dma((BANDS + 1,)),
            pltpu.SMEM(scan_bounds.shape, jnp.int32),
            pltpu.SMEM(tile_index.shape, jnp.int32),
            pltpu.VMEM((det, samples), BF16),
            pltpu.VMEM((det, BANDS, TAPS), BF16),
            pltpu.VMEM((1, dets), BF16),
            pltpu.VMEM((2, dets), F32),
            pltpu.VMEM((1, dets), jnp.int32),
            dma((7,)),
            pltpu.VMEM((det * BANDS, LANES), F32),
            pltpu.VMEM((det * BANDS, LANES), F32),
            pltpu.VMEM((det * BANDS, HALF, 2 * LANES), BF16),
            pltpu.VMEM((2 * det * samples // TILE, LANES), F32),
            pltpu.VMEM((det * (samples // TILE + 8), LANES), F32),
            pltpu.VMEM((det * (samples // TILE + 8), LANES), F32),
            pltpu.VMEM((det * (samples // TILE + 8), LANES), F32),
            pltpu.VMEM((det * (samples // TILE + 8), LANES), F32),
            pltpu.VMEM((BANDS, length), F32),
            pltpu.VMEM((length // TILE, LANES), F32),
            pltpu.VMEM((td, det, slab), BF16),
            pltpu.VMEM((td, det, slab), BF16),
            pltpu.VMEM((td, det, slab), BF16),
            pltpu.VMEM((td, det, slab), BF16),
            pltpu.VMEM((blocks, LANES), F32),
            pltpu.VMEM((td, blocks, LANES), F32),
            pltpu.VMEM((length // TILE, LANES, TILE), BF16),
            pltpu.VMEM((length // TILE, LANES, det * TILES), BF16),
            pltpu.VMEM((TILES, det, TILE), BF16),
            pltpu.VMEM((count, det, TILE), BF16),
            pltpu.VMEM((TILES, 8, TILE), F32),
            pltpu.VMEM((n_obs, 8, TILE), F32),
            pltpu.VMEM((TILE, TILE), BF16),
            pltpu.VMEM((count, own_rows, TILE), F32),
            pltpu.VMEM((TILES, det, TILE), BF16),
            pltpu.VMEM((TILES, own_rows, TILE), F32),
            dma((PIECES, td)), dma((PIECES, td)), dma((PIECES, td)), dma((PIECES, td)),
            dma((td,)), dma((td,)), dma((COPIES * TILES,)), dma((count,)),
            dma((n_obs,)), dma((n_obs,)), dma((count,)), dma((TILES,)),
            dma((count,)), dma((TILES,)),
        ],
        compiler_params=pltpu.CompilerParams(
            collective_id=0, has_side_effects=True, vmem_limit_bytes=63 << 20
        ),
    )(
        scan_bounds, tile_index, timestreams[0], filter_taps[0], det_weights, positions,
        wafer_group.reshape(1, dets),
    )
    out, sky = pl.pallas_call(
        hand_over,
        out_shape=(
            jax.ShapeDtypeStruct((det, samples), F32),
            jax.ShapeDtypeStruct((TILES, own_rows, TILE), F32),
        ),
        in_specs=[HB, HB],
        out_specs=(HB, HB),
        scratch_shapes=[
            pltpu.VMEM((det, samples), F32), pltpu.VMEM((TILES, own_rows, TILE), F32),
            dma((CUTS + 1,)), dma((CUTS + 1,)),
        ],
        compiler_params=pltpu.CompilerParams(vmem_limit_bytes=63 << 20),
    )(out, sky)
    return out[None], sky


def solution(mesh):
    placed = (
        P("obs", "td", None),
        P("obs", "td", None, None),
        P("obs", None),
        P("obs", "td"),
        P("obs", None),
        P(),
        P(),
    )
    return jax.shard_map(
        local,
        mesh=mesh,
        in_specs=placed,
        out_specs=(P("obs", "td", None), P(None, ("obs", "td"), None)),
        check_vma=False,
    )
```

```python
import functools

import jax
import jax.numpy as jnp
from jax import lax
from jax.experimental import pallas as pl
from jax.experimental.pallas import tpu as pltpu
from jax.sharding import PartitionSpec as P

TAPS = 129
HALF = 64
BANDS = 8
TILE = 128
POLY = 6
TILES = 16
LANES = 128
prior_weight = 1.0
F32 = jnp.float32
BF16 = jnp.bfloat16


def projector(pos_ref, wafer_ref, dets):
    x = pos_ref[0:1, :]
    y = pos_ref[1:2, :]
    rows = [jnp.ones_like(x), x, y, x * x, x * y, y * y]
    q = [r.astype(BF16).astype(F32) for r in rows]
    group = jnp.broadcast_to(wafer_ref[...].astype(F32), (dets, dets))
    same = group == group.T
    same_b = jnp.where(same, 1.0, 0.0).astype(BF16)
    pairs = [(i, j) for i in range(POLY) for j in range(i + 1)]
    products = jnp.concatenate(
        [q[i] * q[j] for i, j in pairs] + [jnp.zeros((32 - len(pairs), dets), F32)], axis=0
    )
    high = products.astype(BF16)
    low = (products - high.astype(F32)).astype(BF16)
    gram = jnp.dot(high, same_b, preferred_element_type=F32) + jnp.dot(
        low, same_b, preferred_element_type=F32
    )
    entry = {pair: gram[n : n + 1, :] for n, pair in enumerate(pairs)}
    factor, inv, white = {}, {}, []
    for i in range(POLY):
        for j in range(i + 1):
            value = entry[(i, j)]
            for k in range(j):
                value = value - factor[(i, k)] * factor[(j, k)]
            if i == j:
                factor[(i, i)] = jnp.sqrt(value)
                inv[i] = 1.0 / factor[(i, i)]
            else:
                factor[(i, j)] = value * inv[j]
        value = q[i]
        for k in range(i):
            value = value - factor[(i, k)] * white[k]
        white.append(value * inv[i])
    whitened = jnp.concatenate(white + [jnp.zeros((8 - POLY, dets), F32)], axis=0)
    columns = jnp.concatenate([whitened, jnp.zeros((LANES - 8, dets), F32)], axis=0).T
    outer = columns[:, 0:1] * white[0]
    for m in range(1, POLY):
        outer = outer + columns[:, m : m + 1] * white[m]
    outer = jnp.where(same, outer, 0.0)
    p_high = outer.astype(BF16)
    p_low = (outer - p_high.astype(F32)).astype(BF16)
    return p_high, p_low


def clean(p_high, p_low, gathered):
    fitted = jnp.dot(p_high, gathered, preferred_element_type=F32) + jnp.dot(
        p_low, gathered, preferred_element_type=F32
    )
    return (gathered.astype(F32) - fitted).astype(BF16)


def scan_mask(bounds_ref, length, n_bounds):
    sample = lax.broadcasted_iota(jnp.int32, (BANDS, length), 0) * length + lax.broadcasted_iota(
        jnp.int32, (BANDS, length), 1
    )
    count = jnp.zeros((BANDS, length), jnp.int32)
    for n in range(n_bounds):
        count = count + jnp.where(bounds_ref[0, n] <= sample, 1, 0)
    return (count & 1).astype(F32)


def spread_rows(mask, det):
    return jnp.broadcast_to(mask[:, None, :], (BANDS, det, TILE)).reshape(BANDS * det, TILE)


def pick_matrix(tiles_row, det):
    shape = (det * TILES, LANES)
    row = lax.broadcasted_iota(jnp.int32, shape, 0)
    lane = lax.broadcasted_iota(jnp.int32, shape, 1)
    return (row % det == lane % det) & ((row // det).astype(F32) == tiles_row)


def spread_matrix(tiles_column, det):
    shape = (LANES, det * TILES)
    row = lax.broadcasted_iota(jnp.int32, shape, 0)
    lane = lax.broadcasted_iota(jnp.int32, shape, 1)
    return (row % det == lane % det) & ((lane // det).astype(F32) == tiles_column)


def load_taps(raw_ref, rows_ref, last_ref, det):
    taps = raw_ref[...].reshape(det * BANDS, TAPS)
    rows_ref[...] = taps[:, 0:TILE].astype(F32)
    last_ref[...] = jnp.broadcast_to(taps[:, TILE:TAPS].astype(F32), (det * BANDS, LANES))


def build_bands(rows_ref, last_ref, bands_ref):
    j = lax.broadcasted_iota(jnp.int32, (HALF, LANES), 0)
    m = lax.broadcasted_iota(jnp.int32, (HALF, LANES), 1)
    keep = jnp.where(m >= j, 1.0, 0.0).astype(BF16)
    same = jnp.where(m == j, 1.0, 0.0).astype(BF16)

    def one(pair, _):
        row = jnp.broadcast_to(rows_ref[pl.ds(pair, 1), :], (HALF, LANES))
        last = jnp.broadcast_to(last_ref[pl.ds(pair, 1), :], (HALF, LANES)).astype(BF16)
        turned = pltpu.roll(row, 0, 1, stride=1, stride_axis=0).astype(BF16)
        near = turned * keep
        bands_ref[pair, :, 0:LANES] = near
        bands_ref[pair, :, LANES : 2 * LANES] = (turned - near) + last * same
        return 0

    lax.fori_loop(0, rows_ref.shape[0], one, 0, unroll=64)


def load_signal(x_ref, block_ref, shift_ref, det):
    total = x_ref.shape[1] // TILE
    low = lax.broadcasted_iota(jnp.int32, (det, LANES), 1) < HALF
    before = jnp.zeros((det, LANES), F32)
    for i in range(total + 1):
        rows = pl.ds(i, det, stride=total + 8)
        if i < total:
            block = x_ref[:, i * TILE : (i + 1) * TILE].astype(F32)
        else:
            block = jnp.zeros((det, LANES), F32)
        block_ref[rows, :] = block
        turned = pltpu.roll(block, HALF, 1)
        shift_ref[rows, :] = jnp.where(low, before, turned)
        before = turned


def forward_body(block_ref, shift_ref, bands_ref, halves_ref, length, det):
    per_band = length // TILE
    per_det = BANDS * per_band + 8

    def one(d, _):
        base = pl.multiple_of(d * per_det, 8)
        for b in range(BANDS):
            here = pl.ds(base + b * per_band, per_band)
            after = pl.ds(base + b * per_band + 1, per_band)
            window = jnp.concatenate(
                [
                    jnp.concatenate([source[here, :], source[after, :]], axis=1)
                    for source in (shift_ref, block_ref)
                ],
                axis=0,
            ).astype(BF16)
            rows = pl.ds(pl.multiple_of((b * det + d) * 2 * per_band, 8), 2 * per_band)
            halves_ref[rows, 0:HALF] = lax.dot_general(
                window, bands_ref[d * BANDS + b], (((1,), (1,)), ((), ())),
                preferred_element_type=F32,
            )
        return 0

    lax.fori_loop(0, det, one, 0, unroll=UNROLL)


def adjoint_body(rest_ref, bands_ref, sums, out_ref, length, det, finish):
    per_band = length // TILE
    per_det = BANDS * per_band + 8
    near_ref, far_ref, near_half, far_half = sums

    def one(d, _):
        base = pl.multiple_of(d * per_det, 8)
        for far in (far_ref, far_half):
            far[pl.ds(base, 8), :] = jnp.zeros((8, LANES), F32)
        for near in (near_ref, near_half):
            near[pl.ds(base + per_det - 8, 8), :] = jnp.zeros((8, LANES), F32)
        for b in range(BANDS):
            pair = b * det + d
            rest = rest_ref[pl.ds(pl.multiple_of(pair * 2 * per_band, 8), 2 * per_band), :]
            both = jnp.dot(
                rest[:, 0:HALF].astype(BF16), bands_ref[d * BANDS + b], preferred_element_type=F32
            )
            here = pl.ds(base + b * per_band, per_band)
            after = pl.ds(base + b * per_band + 1, per_band)
            near_ref[here, :] = both[0:per_band, 0:LANES]
            far_ref[after, :] = both[0:per_band, LANES:]
            near_half[here, :] = both[per_band:, 0:LANES]
            far_half[after, :] = both[per_band:, LANES:]
        return 0

    lax.fori_loop(0, det, one, 0, unroll=UNROLL)
    for d in range(det):
        rows = slice(d * per_det, (d + 1) * per_det)
        near_ref[rows, :] = near_ref[rows, :] + far_ref[rows, :]
        near_half[rows, :] = near_half[rows, :] + far_half[rows, :]
    low = lax.broadcasted_iota(jnp.int32, (det, LANES), 1) < HALF

    def turned(i):
        return pltpu.roll(near_ref[pl.ds(i, det, stride=per_det), :], HALF, 1)

    here = turned(0)
    for b in range(BANDS):
        for i in range(b * per_band, (b + 1) * per_band):
            after = turned(i + 1)
            out_ref[:, i * TILE : (i + 1) * TILE] = (
                jnp.where(low, here, after) + near_half[pl.ds(i, det, stride=per_det), :]
            )
            here = after
        finish(b)


MESH = pl.DeviceIdType.MESH
PIECES = 4
COPIES = 2
UNROLL = 16


def whole_kernel(
    dims, bounds_hbm, index_hbm, x_hbm, taps_hbm, weights_hbm, pos_hbm, wafer_hbm,
    out_hbm, skyout_hbm, out_ref, give,
    bounds_ref, index_ref, x_ref, raw_ref, weights_ref, pos_ref, wafer_ref, load,
    rows_ref, last_ref, bands_ref, rest_ref, near_ref, far_ref, near_half, far_half,
    mask_ref, tiles_ref, fsend, frecv, csend, crecv, tsend, trecv,
    filt, spread, gsend, grecv, hsend, hrecv, sky_b, sky_f, skyb_recv, skyf_recv, spread_w, hits_ref,
    f_s, f_r, c_s, c_r, t_s, t_r, g_s, g_r, h_s, h_r, b_s, b_r, k_s, k_r,
):
    n_obs, td, det, length, slab, n_bounds = dims
    dets = det * td
    split = td // BANDS
    blocks = slab // TILE
    width = slab // PIECES
    folds = dets // TILE
    per_fold = td // folds
    count = n_obs * td
    group = count // COPIES
    stride = group // TILES
    own_rows = TILE // count
    obs = lax.axis_index("obs")
    me = lax.axis_index("td")
    linear = obs * td + me
    mine = lax.rem(linear // stride, TILES)
    within = lax.rem(linear, group)
    start = linear - within
    owner = lax.rem(linear, stride) == 0

    def place(device):
        return (device // td, lax.rem(device, td))

    def td_peer(k):
        return lax.rem(me + k, td)

    def td_source(k):
        return lax.rem(me + td - k, td)

    def obs_peer(k):
        return lax.rem(obs + k, n_obs)

    def obs_source(k):
        return lax.rem(obs + n_obs - k, n_obs)

    barrier = pltpu.get_barrier_semaphore()
    for k in range(1, td):
        pl.semaphore_signal(barrier, 1, device_id=(obs, td_peer(k)), device_id_type=MESH)
    for k in range(1, n_obs):
        pl.semaphore_signal(barrier, 1, device_id=(obs_peer(k), me), device_id_type=MESH)

    loads = [
        pltpu.make_async_copy(source, target, load.at[n])
        for n, (source, target) in enumerate(
            [
                (taps_hbm, raw_ref), (x_hbm, x_ref), (index_hbm, index_ref),
                (bounds_hbm, bounds_ref), (weights_hbm, weights_ref), (pos_hbm, pos_ref),
                (wafer_hbm, wafer_ref),
            ]
        )
    ]
    for copy in loads:
        copy.start()
    def tile_copy(k, slot):
        return pltpu.make_async_remote_copy(
            src_ref=tsend, dst_ref=trecv.at[slot], send_sem=t_s.at[k], recv_sem=t_r.at[k],
            device_id=(obs, td_peer(k)), device_id_type=MESH,
        )

    def each(number, do):
        def step(k, _):
            do(k)
            return 0

        lax.fori_loop(1, number, step, 0)

    loads[0].wait()
    load_taps(raw_ref, rows_ref, last_ref, det)
    build_bands(rows_ref, last_ref, bands_ref)
    loads[2].wait()
    row = lax.broadcasted_iota(jnp.int32, (blocks, LANES), 0)
    tile = jnp.zeros((blocks, LANES), jnp.int32)
    for n in range(blocks):
        tile = jnp.where(row == n, index_ref[0, n], tile)
    tsend[...] = tile.astype(F32)
    trecv[me] = tile.astype(F32)
    pl.semaphore_wait(barrier, td - 1 + n_obs - 1)
    each(td, lambda k: tile_copy(k, me).start())
    for n in (1, 3, 4, 5, 6):
        loads[n].wait()
    load_signal(x_ref, near_ref, far_ref, det)
    forward_body(near_ref, far_ref, bands_ref, rest_ref, length, det)

    def signal_copy(h, k, slot):
        cols = pl.ds(pl.multiple_of(h * width, TILE), width)
        peer = td_peer(k)
        return pltpu.make_async_remote_copy(
            src_ref=fsend.at[peer, :, cols], dst_ref=frecv.at[slot, :, cols],
            send_sem=f_s.at[h, k], recv_sem=f_r.at[h, k],
            device_id=(obs, peer), device_id_type=MESH,
        )

    def clean_copy(h, k, slot):
        cols = pl.ds(pl.multiple_of(h * width, TILE), width)
        peer = td_peer(k)
        return pltpu.make_async_remote_copy(
            src_ref=csend.at[peer, :, cols], dst_ref=crecv.at[slot, :, cols],
            send_sem=c_s.at[h, k], recv_sem=c_r.at[h, k],
            device_id=(obs, peer), device_id_type=MESH,
        )

    def hit_copy(k, slot):
        peer = obs_peer(k)
        return pltpu.make_async_remote_copy(
            src_ref=hsend.at[lax.rem((peer * td + me) // stride, TILES)], dst_ref=hrecv.at[slot],
            send_sem=h_s.at[k], recv_sem=h_r.at[k],
            device_id=(peer, me), device_id_type=MESH,
        )

    def bin_copy(q, source):
        return pltpu.make_async_remote_copy(
            src_ref=gsend.at[lax.rem(q, TILES)], dst_ref=grecv.at[source],
            send_sem=g_s.at[q], recv_sem=g_r.at[source],
            device_id=place(q * stride), device_id_type=MESH,
        )

    def rounded_copy(device, p):
        rows = pl.ds(pl.multiple_of(lax.rem(lax.rem(device, td), per_fold) * det, det), det)
        return pltpu.make_async_remote_copy(
            src_ref=sky_b.at[rows], dst_ref=skyb_recv.at[p],
            send_sem=b_s.at[device], recv_sem=b_r.at[p],
            device_id=place(device), device_id_type=MESH,
        )

    def row_copy(device, p):
        return pltpu.make_async_remote_copy(
            src_ref=sky_f.at[device], dst_ref=skyf_recv.at[p],
            send_sem=k_s.at[device], recv_sem=k_r.at[p],
            device_id=place(device), device_id_type=MESH,
        )

    def each_tile(do):
        def step(k, _):
            p = lax.rem(mine + k, TILES)

            @pl.when(start + p * stride != linear)
            def _():
                do(p)

            return 0

        lax.fori_loop(0, TILES, step, 0)

    def each_owner(do):
        def step(k, _):
            q = lax.rem(linear // stride + TILES + k, COPIES * TILES)

            @pl.when(q * stride != linear)
            def _():
                do(q)

            return 0

        lax.fori_loop(0, COPIES * TILES, step, 0)

    def each_device(do):
        each(count, lambda k: do(lax.rem(linear + k, count)))

    def each_near(do):
        each(group, lambda k: do(start + lax.rem(within + k, group)))

    per_band = length // TILE
    low = lax.broadcasted_iota(jnp.int32, (LANES, LANES), 1) < HALF

    def finish_block(n):
        early = rest_ref[pl.ds(n, LANES, stride=2 * per_band), :]
        late = rest_ref[pl.ds(per_band + n, LANES, stride=2 * per_band), :]
        block = jnp.where(low, early, pltpu.roll(late, HALF, 1)).astype(BF16)
        filt[n] = block
        quarter, inside = n // blocks, n % blocks
        for b in range(BANDS):
            fsend[b * split + quarter, :, inside * TILE : (inside + 1) * TILE] = block[
                b * det : (b + 1) * det, :
            ]

    def send_piece(p):
        quarter, h = p // PIECES, p % PIECES

        def send(k):
            if split == 1:
                signal_copy(h, k, me).start()
            else:

                @pl.when(lax.rem(td_peer(k), split) == quarter)
                def _():
                    signal_copy(h, k, me).start()

        each(td, send)

    for p in range(split * PIECES):
        for c in range(width // TILE):
            finish_block(p * (width // TILE) + c)
        send_piece(p)
    frecv[me] = fsend[me]

    mask_ref[...] = scan_mask(bounds_ref, length, n_bounds)
    for n in range(length // TILE):
        filt[n] = filt[n] * spread_rows(mask_ref[:, n * TILE : (n + 1) * TILE], det).astype(BF16)
    each(td, lambda k: tile_copy(k, td_source(k)).wait_recv())
    lane = lax.broadcasted_iota(jnp.int32, (blocks, LANES), 1) // det
    for quarter in range(split):
        tile = trecv[quarter]
        for b in range(1, BANDS):
            tile = jnp.where(lane == b, trecv[b * split + quarter], tile)
        tiles_ref[quarter * blocks : (quarter + 1) * blocks, :] = tile
    sums = jnp.zeros((det * TILES, TILE), F32)
    for n in range(length // TILE):
        pick = jnp.where(pick_matrix(tiles_ref[n : n + 1, :], det), 1.0, 0.0).astype(BF16)
        sums = sums + jnp.dot(pick, filt[n], preferred_element_type=F32)
    gsend[...] = sums.reshape(TILES, det, TILE).astype(BF16)
    each_owner(lambda q: bin_copy(q, linear).start())
    first = lax.broadcasted_iota(jnp.int32, (TILES, LANES), 1) % det == 0
    which = lax.broadcasted_iota(jnp.int32, (TILES, LANES), 0).astype(F32)
    counts = jnp.zeros((TILES, TILE), F32)
    for n in range(length // TILE):
        mask = spread_rows(mask_ref[:, n * TILE : (n + 1) * TILE], det).astype(BF16)
        pick = jnp.where(first & (which == tiles_ref[n : n + 1, :]), 1.0, 0.0).astype(BF16)
        counts = counts + jnp.dot(pick, mask, preferred_element_type=F32)

    @pl.when(owner)
    def _():
        grecv[linear] = gsend[mine]
        level = lax.broadcasted_iota(jnp.int32, (TILES, 8, TILE), 1)
        rows = jnp.broadcast_to(counts[:, None, :], (TILES, 8, TILE))
        weights = weights_ref[...].astype(F32)
        for q in range(folds):
            rows = jnp.where(level == q + 1, weights[:, None, q * TILE : (q + 1) * TILE], rows)
        hsend[...] = rows
        hrecv[obs] = hsend[mine]
        each(n_obs, lambda k: hit_copy(k, obs).start())

    p_high, p_low = projector(pos_ref, wafer_ref, dets)

    for h in range(PIECES):
        each(td, lambda k: signal_copy(h, k, td_source(k)).wait_recv())
        cols = slice(h * width, (h + 1) * width)
        cleaned = clean(p_high, p_low, frecv[:, :, cols].reshape(dets, width))
        csend[:, :, cols] = cleaned.reshape(td, det, width)
        each(td, lambda k: clean_copy(h, k, me).start())
    crecv[me] = csend[me]

    def band_rows(n):
        quarter, inside = n // blocks, n % blocks
        cols = slice(inside * TILE, (inside + 1) * TILE)
        return jnp.concatenate([crecv[b * split + quarter, :, cols] for b in range(BANDS)], axis=0)

    @pl.when(owner)
    def _():
        each(n_obs, lambda k: hit_copy(k, obs_source(k)).wait_recv())
        hit = jnp.zeros((TILE, TILE), F32)
        for o in range(n_obs):
            for q in range(folds):
                weight = jnp.broadcast_to(hrecv[o, q + 1 : q + 2, :], (TILE, TILE)).T
                hit = hit + weight * hrecv[o, 0:1, :]
                spread_w[o * folds + q] = weight
        hits_ref[...] = hit + prior_weight
        each_device(lambda d: bin_copy(linear // stride, d).wait_recv())
        total = jnp.zeros((TILE, TILE), F32)
        for o in range(n_obs):
            binned = grecv[o * td : (o + 1) * td].reshape(dets, TILE)
            fitted = jnp.dot(p_high, binned, preferred_element_type=F32) + jnp.dot(
                p_low, binned, preferred_element_type=F32
            )
            left = binned.astype(F32) - fitted
            for q in range(folds):
                total = total + spread_w[o * folds + q] * left[q * TILE : (q + 1) * TILE, :]
        sky = total / hits_ref[...]
        sky_b[...] = sky.astype(BF16)
        for d in range(count):
            sky_f[d] = sky[d * own_rows : (d + 1) * own_rows, :]
        each_near(lambda d: rounded_copy(d, mine).start())
        each_near(lambda d: row_copy(d, mine).start())
        own = pl.ds(pl.multiple_of(lax.rem(me, per_fold) * det, det), det)
        skyb_recv[mine] = sky_b[own, :]
        skyf_recv[mine] = sky_f[linear]

    grid = jnp.concatenate(
        [tiles_ref[...], jnp.zeros((LANES - length // TILE, LANES), F32)], axis=0
    ).T
    for n in range(length // TILE):
        spread[n] = jnp.where(spread_matrix(grid[:, n : n + 1], det), 1.0, 0.0).astype(BF16)
    for h in range(PIECES):
        each(td, lambda k: clean_copy(h, k, td_source(k)).wait_recv())
    each(td, lambda k: tile_copy(k, me).wait_send())
    for h in range(PIECES):
        each(td, lambda k: signal_copy(h, k, me).wait_send())
        each(td, lambda k: clean_copy(h, k, me).wait_send())
    each_owner(lambda q: bin_copy(q, linear).wait_send())


    @pl.when(owner)
    def _():
        each(n_obs, lambda k: hit_copy(k, obs).wait_send())

    each_tile(lambda p: rounded_copy(linear, p).wait_recv())
    chosen_from = skyb_recv[...].reshape(TILES * det, TILE)
    for n in range(length // TILE):
        mask = spread_rows(mask_ref[:, n * TILE : (n + 1) * TILE], det)
        chosen = jnp.dot(spread[n], chosen_from, preferred_element_type=F32)
        residual = (mask * (band_rows(n).astype(F32) - chosen)).astype(BF16)
        rest = residual.astype(F32)
        rest_ref[pl.ds(n, LANES, stride=2 * length // TILE), :] = rest
        rest_ref[pl.ds(length // TILE + n, LANES, stride=2 * length // TILE), :] = pltpu.roll(
            rest, HALF, 1
        )

    def give_copy(b):
        cols = pl.ds(b * length, length)
        return pltpu.make_async_copy(out_ref.at[:, cols], out_hbm.at[:, cols], give.at[b])

    sky_copy = pltpu.make_async_copy(skyf_recv, skyout_hbm, give.at[BANDS])
    adjoint_body(
        rest_ref, bands_ref, (near_ref, far_ref, near_half, far_half), out_ref, length, det,
        lambda b: give_copy(b).start(),
    )

    each_tile(lambda p: row_copy(linear, p).wait_recv())
    sky_copy.start()
    for b in range(BANDS):
        give_copy(b).wait()
    sky_copy.wait()

    @pl.when(owner)
    def _():
        each_near(lambda d: rounded_copy(d, mine).wait_send())
        each_near(lambda d: row_copy(d, mine).wait_send())


HB = pl.BlockSpec(memory_space=pltpu.HBM)
CUTS = 4


def hand_over(out_ref, sky_ref, out_hbm, sky_hbm, held, sky_held, taken, given):
    width = out_ref.shape[1] // CUTS
    pieces = [(sky_ref, sky_held, sky_hbm)]
    for n in range(CUTS):
        cols = pl.ds(n * width, width)
        pieces.append((out_ref.at[:, cols], held.at[:, cols], out_hbm.at[:, cols]))
    copies = []
    for n, (source, middle, target) in enumerate(pieces):
        take = pltpu.make_async_copy(source, middle, taken.at[n])
        take.start()
        copies.append((take, pltpu.make_async_copy(middle, target, given.at[n])))
    for take, give in copies:
        take.wait()
        give.start()
    for _, give in copies:
        give.wait()


def local(timestreams, filter_taps, scan_bounds, tile_index, det_weights, positions, wafer_group):
    _, det, samples = timestreams.shape
    td = lax.axis_size("td")
    n_obs = lax.axis_size("obs")
    dets = det * td
    length = samples // BANDS
    slab = samples // td
    blocks = slab // TILE
    count = n_obs * td
    own_rows = TILE // count
    dims = (n_obs, td, det, length, slab, scan_bounds.shape[1])
    dma = pltpu.SemaphoreType.DMA
    out, sky = pl.pallas_call(
        functools.partial(whole_kernel, dims),
        out_shape=(
            jax.ShapeDtypeStruct((det, samples), F32),
            jax.ShapeDtypeStruct((TILES, own_rows, TILE), F32),
        ),
        in_specs=[HB] * 7,
        out_specs=(HB, HB),
        scratch_shapes=[
            pltpu.VMEM((det, samples), F32),
            dma((BANDS + 1,)),
            pltpu.SMEM(scan_bounds.shape, jnp.int32),
            pltpu.SMEM(tile_index.shape, jnp.int32),
            pltpu.VMEM((det, samples), BF16),
            pltpu.VMEM((det, BANDS, TAPS), BF16),
            pltpu.VMEM((1, dets), BF16),
            pltpu.VMEM((2, dets), F32),
            pltpu.VMEM((1, dets), jnp.int32),
            dma((7,)),
            pltpu.VMEM((det * BANDS, LANES), F32),
            pltpu.VMEM((det * BANDS, LANES), F32),
            pltpu.VMEM((det * BANDS, HALF, 2 * LANES), BF16),
            pltpu.VMEM((2 * det * samples // TILE, LANES), F32),
            pltpu.VMEM((det * (samples // TILE + 8), LANES), F32),
            pltpu.VMEM((det * (samples // TILE + 8), LANES), F32),
            pltpu.VMEM((det * (samples // TILE + 8), LANES), F32),
            pltpu.VMEM((det * (samples // TILE + 8), LANES), F32),
            pltpu.VMEM((BANDS, length), F32),
            pltpu.VMEM((length // TILE, LANES), F32),
            pltpu.VMEM((td, det, slab), BF16),
            pltpu.VMEM((td, det, slab), BF16),
            pltpu.VMEM((td, det, slab), BF16),
            pltpu.VMEM((td, det, slab), BF16),
            pltpu.VMEM((blocks, LANES), F32),
            pltpu.VMEM((td, blocks, LANES), F32),
            pltpu.VMEM((length // TILE, LANES, TILE), BF16),
            pltpu.VMEM((length // TILE, LANES, det * TILES), BF16),
            pltpu.VMEM((TILES, det, TILE), BF16),
            pltpu.VMEM((count, det, TILE), BF16),
            pltpu.VMEM((TILES, 8, TILE), F32),
            pltpu.VMEM((n_obs, 8, TILE), F32),
            pltpu.VMEM((TILE, TILE), BF16),
            pltpu.VMEM((count, own_rows, TILE), F32),
            pltpu.VMEM((TILES, det, TILE), BF16),
            pltpu.VMEM((TILES, own_rows, TILE), F32),
            pltpu.VMEM((n_obs * dets // TILE, TILE, TILE), F32),
            pltpu.VMEM((TILE, TILE), F32),
            dma((PIECES, td)), dma((PIECES, td)), dma((PIECES, td)), dma((PIECES, td)),
            dma((td,)), dma((td,)), dma((COPIES * TILES,)), dma((count,)),
            dma((n_obs,)), dma((n_obs,)), dma((count,)), dma((TILES,)),
            dma((count,)), dma((TILES,)),
        ],
        compiler_params=pltpu.CompilerParams(
            collective_id=0, has_side_effects=True, vmem_limit_bytes=63 << 20
        ),
    )(
        scan_bounds, tile_index, timestreams[0], filter_taps[0], det_weights, positions,
        wafer_group.reshape(1, dets),
    )
    out, sky = pl.pallas_call(
        hand_over,
        out_shape=(
            jax.ShapeDtypeStruct((det, samples), F32),
            jax.ShapeDtypeStruct((TILES, own_rows, TILE), F32),
        ),
        in_specs=[HB, HB],
        out_specs=(HB, HB),
        scratch_shapes=[
            pltpu.VMEM((det, samples), F32), pltpu.VMEM((TILES, own_rows, TILE), F32),
            dma((CUTS + 1,)), dma((CUTS + 1,)),
        ],
        compiler_params=pltpu.CompilerParams(vmem_limit_bytes=63 << 20),
    )(out, sky)
    return out[None], sky


def solution(mesh):
    placed = (
        P("obs", "td", None),
        P("obs", "td", None, None),
        P("obs", None),
        P("obs", "td"),
        P("obs", None),
        P(),
        P(),
    )
    return jax.shard_map(
        local,
        mesh=mesh,
        in_specs=placed,
        out_specs=(P("obs", "td", None), P(None, ("obs", "td"), None)),
        check_vma=False,
    )
```

```python
import functools

import jax
import jax.numpy as jnp
from jax import lax
from jax.experimental import pallas as pl
from jax.experimental.pallas import tpu as pltpu
from jax.sharding import PartitionSpec as P

TAPS = 129
HALF = 64
BANDS = 8
TILE = 128
POLY = 6
TILES = 16
LANES = 128
prior_weight = 1.0
F32 = jnp.float32
BF16 = jnp.bfloat16


def projector(pos_ref, wafer_ref, dets):
    x = pos_ref[0:1, :]
    y = pos_ref[1:2, :]
    rows = [jnp.ones_like(x), x, y, x * x, x * y, y * y]
    q = [r.astype(BF16).astype(F32) for r in rows]
    group = jnp.broadcast_to(wafer_ref[...].astype(F32), (dets, dets))
    same = group == group.T
    same_b = jnp.where(same, 1.0, 0.0).astype(BF16)
    pairs = [(i, j) for i in range(POLY) for j in range(i + 1)]
    products = jnp.concatenate(
        [q[i] * q[j] for i, j in pairs] + [jnp.zeros((32 - len(pairs), dets), F32)], axis=0
    )
    high = products.astype(BF16)
    low = (products - high.astype(F32)).astype(BF16)
    gram = jnp.dot(high, same_b, preferred_element_type=F32) + jnp.dot(
        low, same_b, preferred_element_type=F32
    )
    entry = {pair: gram[n : n + 1, :] for n, pair in enumerate(pairs)}
    factor, inv, white = {}, {}, []
    for i in range(POLY):
        for j in range(i + 1):
            value = entry[(i, j)]
            for k in range(j):
                value = value - factor[(i, k)] * factor[(j, k)]
            if i == j:
                factor[(i, i)] = jnp.sqrt(value)
                inv[i] = 1.0 / factor[(i, i)]
            else:
                factor[(i, j)] = value * inv[j]
        value = q[i]
        for k in range(i):
            value = value - factor[(i, k)] * white[k]
        white.append(value * inv[i])
    whitened = jnp.concatenate(white + [jnp.zeros((8 - POLY, dets), F32)], axis=0)
    columns = jnp.concatenate([whitened, jnp.zeros((LANES - 8, dets), F32)], axis=0).T
    outer = columns[:, 0:1] * white[0]
    for m in range(1, POLY):
        outer = outer + columns[:, m : m + 1] * white[m]
    outer = jnp.where(same, outer, 0.0)
    p_high = outer.astype(BF16)
    p_low = (outer - p_high.astype(F32)).astype(BF16)
    return p_high, p_low


def clean(p_high, p_low, gathered):
    fitted = jnp.dot(p_high, gathered, preferred_element_type=F32) + jnp.dot(
        p_low, gathered, preferred_element_type=F32
    )
    return (gathered.astype(F32) - fitted).astype(BF16)


def scan_mask(bounds_ref, length, n_bounds):
    sample = lax.broadcasted_iota(jnp.int32, (BANDS, length), 0) * length + lax.broadcasted_iota(
        jnp.int32, (BANDS, length), 1
    )
    count = jnp.zeros((BANDS, length), jnp.int32)
    for n in range(n_bounds):
        count = count + jnp.where(bounds_ref[0, n] <= sample, 1, 0)
    return (count & 1).astype(F32)


def spread_rows(mask, det):
    return jnp.broadcast_to(mask[:, None, :], (BANDS, det, TILE)).reshape(BANDS * det, TILE)


def pick_matrix(tiles_row, det):
    shape = (det * TILES, LANES)
    row = lax.broadcasted_iota(jnp.int32, shape, 0)
    lane = lax.broadcasted_iota(jnp.int32, shape, 1)
    return (row % det == lane % det) & ((row // det).astype(F32) == tiles_row)


def spread_matrix(tiles_column, det):
    shape = (LANES, det * TILES)
    row = lax.broadcasted_iota(jnp.int32, shape, 0)
    lane = lax.broadcasted_iota(jnp.int32, shape, 1)
    return (row % det == lane % det) & ((lane // det).astype(F32) == tiles_column)


def load_taps(raw_ref, rows_ref, last_ref, det):
    taps = raw_ref[...].reshape(det * BANDS, TAPS)
    rows_ref[...] = taps[:, 0:TILE].astype(F32)
    last_ref[...] = jnp.broadcast_to(taps[:, TILE:TAPS].astype(F32), (det * BANDS, LANES))


def build_bands(rows_ref, last_ref, bands_ref):
    j = lax.broadcasted_iota(jnp.int32, (HALF, LANES), 0)
    m = lax.broadcasted_iota(jnp.int32, (HALF, LANES), 1)
    keep = jnp.where(m >= j, 1.0, 0.0).astype(BF16)
    same = jnp.where(m == j, 1.0, 0.0).astype(BF16)

    def one(pair, _):
        row = jnp.broadcast_to(rows_ref[pl.ds(pair, 1), :], (HALF, LANES))
        last = jnp.broadcast_to(last_ref[pl.ds(pair, 1), :], (HALF, LANES)).astype(BF16)
        turned = pltpu.roll(row, 0, 1, stride=1, stride_axis=0).astype(BF16)
        near = turned * keep
        bands_ref[pair, :, 0:LANES] = near
        bands_ref[pair, :, LANES : 2 * LANES] = (turned - near) + last * same
        return 0

    lax.fori_loop(0, rows_ref.shape[0], one, 0, unroll=64)


def load_signal(x_ref, block_ref, shift_ref, det):
    total = x_ref.shape[1] // TILE
    low = lax.broadcasted_iota(jnp.int32, (det, LANES), 1) < HALF
    before = jnp.zeros((det, LANES), F32)
    for i in range(total + 1):
        rows = pl.ds(i, det, stride=total + 8)
        if i < total:
            block = x_ref[:, i * TILE : (i + 1) * TILE].astype(F32)
        else:
            block = jnp.zeros((det, LANES), F32)
        block_ref[rows, :] = block
        turned = pltpu.roll(block, HALF, 1)
        shift_ref[rows, :] = jnp.where(low, before, turned)
        before = turned


def forward_body(block_ref, shift_ref, bands_ref, halves_ref, length, det):
    per_band = length // TILE
    per_det = BANDS * per_band + 8

    def one(d, _):
        base = pl.multiple_of(d * per_det, 8)
        for b in range(BANDS):
            here = pl.ds(base + b * per_band, per_band)
            after = pl.ds(base + b * per_band + 1, per_band)
            window = jnp.concatenate(
                [
                    jnp.concatenate([source[here, :], source[after, :]], axis=1)
                    for source in (shift_ref, block_ref)
                ],
                axis=0,
            ).astype(BF16)
            rows = pl.ds(pl.multiple_of((b * det + d) * 2 * per_band, 8), 2 * per_band)
            halves_ref[rows, 0:HALF] = lax.dot_general(
                window, bands_ref[d * BANDS + b], (((1,), (1,)), ((), ())),
                preferred_element_type=F32,
            )
        return 0

    lax.fori_loop(0, det, one, 0, unroll=UNROLL)


def adjoint_body(rest_ref, bands_ref, sums, out_ref, length, det, finish):
    per_band = length // TILE
    per_det = BANDS * per_band + 8
    near_ref, far_ref, near_half, far_half = sums

    def one(d, _):
        base = pl.multiple_of(d * per_det, 8)
        for far in (far_ref, far_half):
            far[pl.ds(base, 8), :] = jnp.zeros((8, LANES), F32)
        for near in (near_ref, near_half):
            near[pl.ds(base + per_det - 8, 8), :] = jnp.zeros((8, LANES), F32)
        for b in range(BANDS):
            pair = b * det + d
            rest = rest_ref[pl.ds(pl.multiple_of(pair * 2 * per_band, 8), 2 * per_band), :]
            both = jnp.dot(
                rest[:, 0:HALF].astype(BF16), bands_ref[d * BANDS + b], preferred_element_type=F32
            )
            here = pl.ds(base + b * per_band, per_band)
            after = pl.ds(base + b * per_band + 1, per_band)
            near_ref[here, :] = both[0:per_band, 0:LANES]
            far_ref[after, :] = both[0:per_band, LANES:]
            near_half[here, :] = both[per_band:, 0:LANES]
            far_half[after, :] = both[per_band:, LANES:]
        return 0

    lax.fori_loop(0, det, one, 0, unroll=UNROLL)
    for d in range(det):
        rows = slice(d * per_det, (d + 1) * per_det)
        near_ref[rows, :] = near_ref[rows, :] + far_ref[rows, :]
        near_half[rows, :] = near_half[rows, :] + far_half[rows, :]
    low = lax.broadcasted_iota(jnp.int32, (det, LANES), 1) < HALF

    def turned(i):
        return pltpu.roll(near_ref[pl.ds(i, det, stride=per_det), :], HALF, 1)

    here = turned(0)
    for b in range(BANDS):
        for i in range(b * per_band, (b + 1) * per_band):
            after = turned(i + 1)
            out_ref[:, i * TILE : (i + 1) * TILE] = (
                jnp.where(low, here, after) + near_half[pl.ds(i, det, stride=per_det), :]
            )
            here = after
        finish(b)


MESH = pl.DeviceIdType.MESH
PIECES = 1
COPIES = 2
UNROLL = 16


def whole_kernel(
    dims, bounds_hbm, index_hbm, x_hbm, taps_hbm, weights_hbm, pos_hbm, wafer_hbm,
    out_hbm, skyout_hbm, out_ref, give,
    bounds_ref, index_ref, x_ref, raw_ref, weights_ref, pos_ref, wafer_ref, load,
    rows_ref, last_ref, bands_ref, rest_ref, near_ref, far_ref, near_half, far_half,
    mask_ref, tiles_ref, fsend, frecv, csend, crecv, tsend, trecv,
    filt, spread, gsend, grecv, hsend, hrecv, sky_b, sky_f, skyb_recv, skyf_recv, spread_w, hits_ref,
    f_s, f_r, c_s, c_r, t_s, t_r, g_s, g_r, h_s, h_r, b_s, b_r, k_s, k_r,
):
    n_obs, td, det, length, slab, n_bounds = dims
    dets = det * td
    split = td // BANDS
    blocks = slab // TILE
    width = slab // PIECES
    folds = dets // TILE
    per_fold = td // folds
    count = n_obs * td
    group = count // COPIES
    stride = group // TILES
    own_rows = TILE // count
    obs = lax.axis_index("obs")
    me = lax.axis_index("td")
    linear = obs * td + me
    mine = lax.rem(linear // stride, TILES)
    within = lax.rem(linear, group)
    start = linear - within
    owner = lax.rem(linear, stride) == 0

    def place(device):
        return (device // td, lax.rem(device, td))

    def td_peer(k):
        return lax.rem(me + k, td)

    def td_source(k):
        return lax.rem(me + td - k, td)

    def obs_peer(k):
        return lax.rem(obs + k, n_obs)

    def obs_source(k):
        return lax.rem(obs + n_obs - k, n_obs)

    barrier = pltpu.get_barrier_semaphore()
    for k in range(1, td):
        pl.semaphore_signal(barrier, 1, device_id=(obs, td_peer(k)), device_id_type=MESH)
    for k in range(1, n_obs):
        pl.semaphore_signal(barrier, 1, device_id=(obs_peer(k), me), device_id_type=MESH)

    loads = [
        pltpu.make_async_copy(source, target, load.at[n])
        for n, (source, target) in enumerate(
            [
                (taps_hbm, raw_ref), (x_hbm, x_ref), (index_hbm, index_ref),
                (bounds_hbm, bounds_ref), (weights_hbm, weights_ref), (pos_hbm, pos_ref),
                (wafer_hbm, wafer_ref),
            ]
        )
    ]
    for copy in loads:
        copy.start()
    def tile_copy(k, slot):
        return pltpu.make_async_remote_copy(
            src_ref=tsend, dst_ref=trecv.at[slot], send_sem=t_s.at[k], recv_sem=t_r.at[k],
            device_id=(obs, td_peer(k)), device_id_type=MESH,
        )

    def each(number, do):
        def step(k, _):
            do(k)
            return 0

        lax.fori_loop(1, number, step, 0)

    loads[0].wait()
    load_taps(raw_ref, rows_ref, last_ref, det)
    build_bands(rows_ref, last_ref, bands_ref)
    loads[2].wait()
    row = lax.broadcasted_iota(jnp.int32, (blocks, LANES), 0)
    tile = jnp.zeros((blocks, LANES), jnp.int32)
    for n in range(blocks):
        tile = jnp.where(row == n, index_ref[0, n], tile)
    tsend[...] = tile.astype(F32)
    trecv[me] = tile.astype(F32)
    pl.semaphore_wait(barrier, td - 1 + n_obs - 1)
    each(td, lambda k: tile_copy(k, me).start())
    for n in (1, 3, 4, 5, 6):
        loads[n].wait()
    load_signal(x_ref, near_ref, far_ref, det)
    forward_body(near_ref, far_ref, bands_ref, rest_ref, length, det)

    def signal_copy(h, k, slot):
        cols = pl.ds(pl.multiple_of(h * width, TILE), width)
        peer = td_peer(k)
        return pltpu.make_async_remote_copy(
            src_ref=fsend.at[peer, :, cols], dst_ref=frecv.at[slot, :, cols],
            send_sem=f_s.at[h, k], recv_sem=f_r.at[h, k],
            device_id=(obs, peer), device_id_type=MESH,
        )

    def clean_copy(h, k, slot):
        cols = pl.ds(pl.multiple_of(h * width, TILE), width)
        peer = td_peer(k)
        return pltpu.make_async_remote_copy(
            src_ref=csend.at[peer, :, cols], dst_ref=crecv.at[slot, :, cols],
            send_sem=c_s.at[h, k], recv_sem=c_r.at[h, k],
            device_id=(obs, peer), device_id_type=MESH,
        )

    def hit_copy(k, slot):
        peer = obs_peer(k)
        return pltpu.make_async_remote_copy(
            src_ref=hsend.at[lax.rem((peer * td + me) // stride, TILES)], dst_ref=hrecv.at[slot],
            send_sem=h_s.at[k], recv_sem=h_r.at[k],
            device_id=(peer, me), device_id_type=MESH,
        )

    def bin_copy(q, source):
        return pltpu.make_async_remote_copy(
            src_ref=gsend.at[lax.rem(q, TILES)], dst_ref=grecv.at[source],
            send_sem=g_s.at[q], recv_sem=g_r.at[source],
            device_id=place(q * stride), device_id_type=MESH,
        )

    def rounded_copy(device, p):
        rows = pl.ds(pl.multiple_of(lax.rem(lax.rem(device, td), per_fold) * det, det), det)
        return pltpu.make_async_remote_copy(
            src_ref=sky_b.at[rows], dst_ref=skyb_recv.at[p],
            send_sem=b_s.at[device], recv_sem=b_r.at[p],
            device_id=place(device), device_id_type=MESH,
        )

    def row_copy(device, p):
        return pltpu.make_async_remote_copy(
            src_ref=sky_f.at[device], dst_ref=skyf_recv.at[p],
            send_sem=k_s.at[device], recv_sem=k_r.at[p],
            device_id=place(device), device_id_type=MESH,
        )

    def each_tile(do):
        def step(k, _):
            p = lax.rem(mine + k, TILES)

            @pl.when(start + p * stride != linear)
            def _():
                do(p)

            return 0

        lax.fori_loop(0, TILES, step, 0)

    def each_owner(do):
        def step(k, _):
            q = lax.rem(linear // stride + TILES + k, COPIES * TILES)

            @pl.when(q * stride != linear)
            def _():
                do(q)

            return 0

        lax.fori_loop(0, COPIES * TILES, step, 0)

    def each_device(do):
        each(count, lambda k: do(lax.rem(linear + k, count)))

    def each_near(do):
        each(group, lambda k: do(start + lax.rem(within + k, group)))

    per_band = length // TILE
    low = lax.broadcasted_iota(jnp.int32, (LANES, LANES), 1) < HALF

    def finish_block(n):
        early = rest_ref[pl.ds(n, LANES, stride=2 * per_band), :]
        late = rest_ref[pl.ds(per_band + n, LANES, stride=2 * per_band), :]
        block = jnp.where(low, early, pltpu.roll(late, HALF, 1)).astype(BF16)
        filt[n] = block
        quarter, inside = n // blocks, n % blocks
        for b in range(BANDS):
            fsend[b * split + quarter, :, inside * TILE : (inside + 1) * TILE] = block[
                b * det : (b + 1) * det, :
            ]

    def send_piece(p):
        quarter, h = p // PIECES, p % PIECES

        def send(k):
            if split == 1:
                signal_copy(h, k, me).start()
            else:

                @pl.when(lax.rem(td_peer(k), split) == quarter)
                def _():
                    signal_copy(h, k, me).start()

        each(td, send)

    for p in range(split * PIECES):
        for c in range(width // TILE):
            finish_block(p * (width // TILE) + c)
        send_piece(p)
    frecv[me] = fsend[me]

    mask_ref[...] = scan_mask(bounds_ref, length, n_bounds)
    for n in range(length // TILE):
        filt[n] = filt[n] * spread_rows(mask_ref[:, n * TILE : (n + 1) * TILE], det).astype(BF16)
    each(td, lambda k: tile_copy(k, td_source(k)).wait_recv())
    lane = lax.broadcasted_iota(jnp.int32, (blocks, LANES), 1) // det
    for quarter in range(split):
        tile = trecv[quarter]
        for b in range(1, BANDS):
            tile = jnp.where(lane == b, trecv[b * split + quarter], tile)
        tiles_ref[quarter * blocks : (quarter + 1) * blocks, :] = tile
    sums = jnp.zeros((det * TILES, TILE), F32)
    for n in range(length // TILE):
        pick = jnp.where(pick_matrix(tiles_ref[n : n + 1, :], det), 1.0, 0.0).astype(BF16)
        sums = sums + jnp.dot(pick, filt[n], preferred_element_type=F32)
    gsend[...] = sums.reshape(TILES, det, TILE).astype(BF16)
    each_owner(lambda q: bin_copy(q, linear).start())
    first = lax.broadcasted_iota(jnp.int32, (TILES, LANES), 1) % det == 0
    which = lax.broadcasted_iota(jnp.int32, (TILES, LANES), 0).astype(F32)
    counts = jnp.zeros((TILES, TILE), F32)
    for n in range(length // TILE):
        mask = spread_rows(mask_ref[:, n * TILE : (n + 1) * TILE], det).astype(BF16)
        pick = jnp.where(first & (which == tiles_ref[n : n + 1, :]), 1.0, 0.0).astype(BF16)
        counts = counts + jnp.dot(pick, mask, preferred_element_type=F32)

    @pl.when(owner)
    def _():
        grecv[linear] = gsend[mine]
        level = lax.broadcasted_iota(jnp.int32, (TILES, 8, TILE), 1)
        rows = jnp.broadcast_to(counts[:, None, :], (TILES, 8, TILE))
        weights = weights_ref[...].astype(F32)
        for q in range(folds):
            rows = jnp.where(level == q + 1, weights[:, None, q * TILE : (q + 1) * TILE], rows)
        hsend[...] = rows
        hrecv[obs] = hsend[mine]
        each(n_obs, lambda k: hit_copy(k, obs).start())

    p_high, p_low = projector(pos_ref, wafer_ref, dets)

    for h in range(PIECES):
        each(td, lambda k: signal_copy(h, k, td_source(k)).wait_recv())
        cols = slice(h * width, (h + 1) * width)
        cleaned = clean(p_high, p_low, frecv[:, :, cols].reshape(dets, width))
        csend[:, :, cols] = cleaned.reshape(td, det, width)
        each(td, lambda k: clean_copy(h, k, me).start())
    crecv[me] = csend[me]

    def band_rows(n):
        quarter, inside = n // blocks, n % blocks
        cols = slice(inside * TILE, (inside + 1) * TILE)
        return jnp.concatenate([crecv[b * split + quarter, :, cols] for b in range(BANDS)], axis=0)

    @pl.when(owner)
    def _():
        each(n_obs, lambda k: hit_copy(k, obs_source(k)).wait_recv())
        hit = jnp.zeros((TILE, TILE), F32)
        for o in range(n_obs):
            for q in range(folds):
                weight = jnp.broadcast_to(hrecv[o, q + 1 : q + 2, :], (TILE, TILE)).T
                hit = hit + weight * hrecv[o, 0:1, :]
                spread_w[o * folds + q] = weight
        hits_ref[...] = hit + prior_weight
        each_device(lambda d: bin_copy(linear // stride, d).wait_recv())
        total = jnp.zeros((TILE, TILE), F32)
        for o in range(n_obs):
            binned = grecv[o * td : (o + 1) * td].reshape(dets, TILE)
            fitted = jnp.dot(p_high, binned, preferred_element_type=F32) + jnp.dot(
                p_low, binned, preferred_element_type=F32
            )
            left = binned.astype(F32) - fitted
            for q in range(folds):
                total = total + spread_w[o * folds + q] * left[q * TILE : (q + 1) * TILE, :]
        sky = total / hits_ref[...]
        sky_b[...] = sky.astype(BF16)
        for d in range(count):
            sky_f[d] = sky[d * own_rows : (d + 1) * own_rows, :]
        each_near(lambda d: rounded_copy(d, mine).start())
        each_near(lambda d: row_copy(d, mine).start())
        own = pl.ds(pl.multiple_of(lax.rem(me, per_fold) * det, det), det)
        skyb_recv[mine] = sky_b[own, :]
        skyf_recv[mine] = sky_f[linear]

    grid = jnp.concatenate(
        [tiles_ref[...], jnp.zeros((LANES - length // TILE, LANES), F32)], axis=0
    ).T
    for n in range(length // TILE):
        spread[n] = jnp.where(spread_matrix(grid[:, n : n + 1], det), 1.0, 0.0).astype(BF16)
    for h in range(PIECES):
        each(td, lambda k: clean_copy(h, k, td_source(k)).wait_recv())
    each(td, lambda k: tile_copy(k, me).wait_send())
    for h in range(PIECES):
        each(td, lambda k: signal_copy(h, k, me).wait_send())
        each(td, lambda k: clean_copy(h, k, me).wait_send())
    each_owner(lambda q: bin_copy(q, linear).wait_send())


    @pl.when(owner)
    def _():
        each(n_obs, lambda k: hit_copy(k, obs).wait_send())

    each_tile(lambda p: rounded_copy(linear, p).wait_recv())
    chosen_from = skyb_recv[...].reshape(TILES * det, TILE)
    for n in range(length // TILE):
        mask = spread_rows(mask_ref[:, n * TILE : (n + 1) * TILE], det)
        chosen = jnp.dot(spread[n], chosen_from, preferred_element_type=F32)
        residual = (mask * (band_rows(n).astype(F32) - chosen)).astype(BF16)
        rest = residual.astype(F32)
        rest_ref[pl.ds(n, LANES, stride=2 * length // TILE), :] = rest
        rest_ref[pl.ds(length // TILE + n, LANES, stride=2 * length // TILE), :] = pltpu.roll(
            rest, HALF, 1
        )

    def give_copy(b):
        cols = pl.ds(b * length, length)
        return pltpu.make_async_copy(out_ref.at[:, cols], out_hbm.at[:, cols], give.at[b])

    sky_copy = pltpu.make_async_copy(skyf_recv, skyout_hbm, give.at[BANDS])
    adjoint_body(
        rest_ref, bands_ref, (near_ref, far_ref, near_half, far_half), out_ref, length, det,
        lambda b: give_copy(b).start(),
    )

    each_tile(lambda p: row_copy(linear, p).wait_recv())
    sky_copy.start()
    for b in range(BANDS):
        give_copy(b).wait()
    sky_copy.wait()

    @pl.when(owner)
    def _():
        each_near(lambda d: rounded_copy(d, mine).wait_send())
        each_near(lambda d: row_copy(d, mine).wait_send())


HB = pl.BlockSpec(memory_space=pltpu.HBM)
CUTS = 2


def hand_over(out_ref, sky_ref, out_hbm, sky_hbm, held, sky_held, taken, given):
    width = out_ref.shape[1] // CUTS
    pieces = [(sky_ref, sky_held, sky_hbm)]
    for n in range(CUTS):
        cols = pl.ds(n * width, width)
        pieces.append((out_ref.at[:, cols], held.at[:, cols], out_hbm.at[:, cols]))
    copies = []
    for n, (source, middle, target) in enumerate(pieces):
        take = pltpu.make_async_copy(source, middle, taken.at[n])
        take.start()
        copies.append((take, pltpu.make_async_copy(middle, target, given.at[n])))
    for take, give in copies:
        take.wait()
        give.start()
    for _, give in copies:
        give.wait()


def local(timestreams, filter_taps, scan_bounds, tile_index, det_weights, positions, wafer_group):
    _, det, samples = timestreams.shape
    td = lax.axis_size("td")
    n_obs = lax.axis_size("obs")
    dets = det * td
    length = samples // BANDS
    slab = samples // td
    blocks = slab // TILE
    count = n_obs * td
    own_rows = TILE // count
    dims = (n_obs, td, det, length, slab, scan_bounds.shape[1])
    dma = pltpu.SemaphoreType.DMA
    out, sky = pl.pallas_call(
        functools.partial(whole_kernel, dims),
        out_shape=(
            jax.ShapeDtypeStruct((det, samples), F32),
            jax.ShapeDtypeStruct((TILES, own_rows, TILE), F32),
        ),
        in_specs=[HB] * 7,
        out_specs=(HB, HB),
        scratch_shapes=[
            pltpu.VMEM((det, samples), F32),
            dma((BANDS + 1,)),
            pltpu.SMEM(scan_bounds.shape, jnp.int32),
            pltpu.SMEM(tile_index.shape, jnp.int32),
            pltpu.VMEM((det, samples), BF16),
            pltpu.VMEM((det, BANDS, TAPS), BF16),
            pltpu.VMEM((1, dets), BF16),
            pltpu.VMEM((2, dets), F32),
            pltpu.VMEM((1, dets), jnp.int32),
            dma((7,)),
            pltpu.VMEM((det * BANDS, LANES), F32),
            pltpu.VMEM((det * BANDS, LANES), F32),
            pltpu.VMEM((det * BANDS, HALF, 2 * LANES), BF16),
            pltpu.VMEM((2 * det * samples // TILE, LANES), F32),
            pltpu.VMEM((det * (samples // TILE + 8), LANES), F32),
            pltpu.VMEM((det * (samples // TILE + 8), LANES), F32),
            pltpu.VMEM((det * (samples // TILE + 8), LANES), F32),
            pltpu.VMEM((det * (samples // TILE + 8), LANES), F32),
            pltpu.VMEM((BANDS, length), F32),
            pltpu.VMEM((length // TILE, LANES), F32),
            pltpu.VMEM((td, det, slab), BF16),
            pltpu.VMEM((td, det, slab), BF16),
            pltpu.VMEM((td, det, slab), BF16),
            pltpu.VMEM((td, det, slab), BF16),
            pltpu.VMEM((blocks, LANES), F32),
            pltpu.VMEM((td, blocks, LANES), F32),
            pltpu.VMEM((length // TILE, LANES, TILE), BF16),
            pltpu.VMEM((length // TILE, LANES, det * TILES), BF16),
            pltpu.VMEM((TILES, det, TILE), BF16),
            pltpu.VMEM((count, det, TILE), BF16),
            pltpu.VMEM((TILES, 8, TILE), F32),
            pltpu.VMEM((n_obs, 8, TILE), F32),
            pltpu.VMEM((TILE, TILE), BF16),
            pltpu.VMEM((count, own_rows, TILE), F32),
            pltpu.VMEM((TILES, det, TILE), BF16),
            pltpu.VMEM((TILES, own_rows, TILE), F32),
            pltpu.VMEM((n_obs * dets // TILE, TILE, TILE), F32),
            pltpu.VMEM((TILE, TILE), F32),
            dma((PIECES, td)), dma((PIECES, td)), dma((PIECES, td)), dma((PIECES, td)),
            dma((td,)), dma((td,)), dma((COPIES * TILES,)), dma((count,)),
            dma((n_obs,)), dma((n_obs,)), dma((count,)), dma((TILES,)),
            dma((count,)), dma((TILES,)),
        ],
        compiler_params=pltpu.CompilerParams(
            collective_id=0, has_side_effects=True, vmem_limit_bytes=63 << 20
        ),
    )(
        scan_bounds, tile_index, timestreams[0], filter_taps[0], det_weights, positions,
        wafer_group.reshape(1, dets),
    )
    out, sky = pl.pallas_call(
        hand_over,
        out_shape=(
            jax.ShapeDtypeStruct((det, samples), F32),
            jax.ShapeDtypeStruct((TILES, own_rows, TILE), F32),
        ),
        in_specs=[HB, HB],
        out_specs=(HB, HB),
        scratch_shapes=[
            pltpu.VMEM((det, samples), F32), pltpu.VMEM((TILES, own_rows, TILE), F32),
            dma((CUTS + 1,)), dma((CUTS + 1,)),
        ],
        compiler_params=pltpu.CompilerParams(vmem_limit_bytes=63 << 20),
    )(out, sky)
    return out[None], sky


def solution(mesh):
    placed = (
        P("obs", "td", None),
        P("obs", "td", None, None),
        P("obs", None),
        P("obs", "td"),
        P("obs", None),
        P(),
        P(),
    )
    return jax.shard_map(
        local,
        mesh=mesh,
        in_specs=placed,
        out_specs=(P("obs", "td", None), P(None, ("obs", "td"), None)),
        check_vma=False,
    )
```

```python
import functools

import jax
import jax.numpy as jnp
from jax import lax
from jax.experimental import pallas as pl
from jax.experimental.pallas import tpu as pltpu
from jax.sharding import PartitionSpec as P

TAPS = 129
HALF = 64
BANDS = 8
TILE = 128
POLY = 6
TILES = 16
LANES = 128
prior_weight = 1.0
F32 = jnp.float32
BF16 = jnp.bfloat16


def projector(pos_ref, wafer_ref, dets):
    x = pos_ref[0:1, :]
    y = pos_ref[1:2, :]
    rows = [jnp.ones_like(x), x, y, x * x, x * y, y * y]
    q = [r.astype(BF16).astype(F32) for r in rows]
    group = jnp.broadcast_to(wafer_ref[...].astype(F32), (dets, dets))
    same = group == group.T
    same_b = jnp.where(same, 1.0, 0.0).astype(BF16)
    pairs = [(i, j) for i in range(POLY) for j in range(i + 1)]
    products = jnp.concatenate(
        [q[i] * q[j] for i, j in pairs] + [jnp.zeros((32 - len(pairs), dets), F32)], axis=0
    )
    high = products.astype(BF16)
    low = (products - high.astype(F32)).astype(BF16)
    gram = jnp.dot(high, same_b, preferred_element_type=F32) + jnp.dot(
        low, same_b, preferred_element_type=F32
    )
    entry = {pair: gram[n : n + 1, :] for n, pair in enumerate(pairs)}
    factor, inv, white = {}, {}, []
    for i in range(POLY):
        for j in range(i + 1):
            value = entry[(i, j)]
            for k in range(j):
                value = value - factor[(i, k)] * factor[(j, k)]
            if i == j:
                factor[(i, i)] = jnp.sqrt(value)
                inv[i] = 1.0 / factor[(i, i)]
            else:
                factor[(i, j)] = value * inv[j]
        value = q[i]
        for k in range(i):
            value = value - factor[(i, k)] * white[k]
        white.append(value * inv[i])
    whitened = jnp.concatenate(white + [jnp.zeros((8 - POLY, dets), F32)], axis=0)
    columns = jnp.concatenate([whitened, jnp.zeros((LANES - 8, dets), F32)], axis=0).T
    outer = columns[:, 0:1] * white[0]
    for m in range(1, POLY):
        outer = outer + columns[:, m : m + 1] * white[m]
    outer = jnp.where(same, outer, 0.0)
    p_high = outer.astype(BF16)
    p_low = (outer - p_high.astype(F32)).astype(BF16)
    return p_high, p_low


def clean(p_high, p_low, gathered):
    fitted = jnp.dot(p_high, gathered, preferred_element_type=F32) + jnp.dot(
        p_low, gathered, preferred_element_type=F32
    )
    return (gathered.astype(F32) - fitted).astype(BF16)


def scan_mask(bounds_ref, length, n_bounds):
    sample = lax.broadcasted_iota(jnp.int32, (BANDS, length), 0) * length + lax.broadcasted_iota(
        jnp.int32, (BANDS, length), 1
    )
    count = jnp.zeros((BANDS, length), jnp.int32)
    for n in range(n_bounds):
        count = count + jnp.where(bounds_ref[0, n] <= sample, 1, 0)
    return (count & 1).astype(F32)


def spread_rows(mask, det):
    return jnp.broadcast_to(mask[:, None, :], (BANDS, det, TILE)).reshape(BANDS * det, TILE)


def pick_matrix(tiles_row, det):
    shape = (det * TILES, LANES)
    row = lax.broadcasted_iota(jnp.int32, shape, 0)
    lane = lax.broadcasted_iota(jnp.int32, shape, 1)
    return (row % det == lane % det) & ((row // det).astype(F32) == tiles_row)


def spread_matrix(tiles_column, det):
    shape = (LANES, det * TILES)
    row = lax.broadcasted_iota(jnp.int32, shape, 0)
    lane = lax.broadcasted_iota(jnp.int32, shape, 1)
    return (row % det == lane % det) & ((lane // det).astype(F32) == tiles_column)


def load_taps(raw_ref, rows_ref, last_ref, det):
    taps = raw_ref[...].reshape(det * BANDS, TAPS)
    rows_ref[...] = taps[:, 0:TILE].astype(F32)
    last_ref[...] = jnp.broadcast_to(taps[:, TILE:TAPS].astype(F32), (det * BANDS, LANES))


def build_bands(rows_ref, last_ref, bands_ref):
    j = lax.broadcasted_iota(jnp.int32, (HALF, LANES), 0)
    m = lax.broadcasted_iota(jnp.int32, (HALF, LANES), 1)
    keep = jnp.where(m >= j, 1.0, 0.0).astype(BF16)
    same = jnp.where(m == j, 1.0, 0.0).astype(BF16)

    def one(pair, _):
        row = jnp.broadcast_to(rows_ref[pl.ds(pair, 1), :], (HALF, LANES))
        last = jnp.broadcast_to(last_ref[pl.ds(pair, 1), :], (HALF, LANES)).astype(BF16)
        turned = pltpu.roll(row, 0, 1, stride=1, stride_axis=0).astype(BF16)
        near = turned * keep
        bands_ref[pair, :, 0:LANES] = near
        bands_ref[pair, :, LANES : 2 * LANES] = (turned - near) + last * same
        return 0

    lax.fori_loop(0, rows_ref.shape[0], one, 0, unroll=64)


def load_signal(x_ref, block_ref, shift_ref, det):
    total = x_ref.shape[1] // TILE
    low = lax.broadcasted_iota(jnp.int32, (det, LANES), 1) < HALF
    before = jnp.zeros((det, LANES), F32)
    for i in range(total + 1):
        rows = pl.ds(i, det, stride=total + 8)
        if i < total:
            block = x_ref[:, i * TILE : (i + 1) * TILE].astype(F32)
        else:
            block = jnp.zeros((det, LANES), F32)
        block_ref[rows, :] = block
        turned = pltpu.roll(block, HALF, 1)
        shift_ref[rows, :] = jnp.where(low, before, turned)
        before = turned


def forward_body(block_ref, shift_ref, bands_ref, halves_ref, length, det):
    per_band = length // TILE
    per_det = BANDS * per_band + 8

    def one(d, _):
        base = pl.multiple_of(d * per_det, 8)
        for b in range(BANDS):
            here = pl.ds(base + b * per_band, per_band)
            after = pl.ds(base + b * per_band + 1, per_band)
            window = jnp.concatenate(
                [
                    jnp.concatenate([source[here, :], source[after, :]], axis=1)
                    for source in (shift_ref, block_ref)
                ],
                axis=0,
            ).astype(BF16)
            rows = pl.ds(pl.multiple_of((b * det + d) * 2 * per_band, 8), 2 * per_band)
            halves_ref[rows, 0:HALF] = lax.dot_general(
                window, bands_ref[d * BANDS + b], (((1,), (1,)), ((), ())),
                preferred_element_type=F32,
            )
        return 0

    lax.fori_loop(0, det, one, 0, unroll=UNROLL)


def adjoint_body(rest_ref, bands_ref, sums, out_ref, length, det, finish):
    per_band = length // TILE
    per_det = BANDS * per_band + 8
    near_ref, far_ref, near_half, far_half = sums

    def one(d, _):
        base = pl.multiple_of(d * per_det, 8)
        for far in (far_ref, far_half):
            far[pl.ds(base, 8), :] = jnp.zeros((8, LANES), F32)
        for near in (near_ref, near_half):
            near[pl.ds(base + per_det - 8, 8), :] = jnp.zeros((8, LANES), F32)
        for b in range(BANDS):
            pair = b * det + d
            rest = rest_ref[pl.ds(pl.multiple_of(pair * 2 * per_band, 8), 2 * per_band), :]
            both = jnp.dot(
                rest[:, 0:HALF].astype(BF16), bands_ref[d * BANDS + b], preferred_element_type=F32
            )
            here = pl.ds(base + b * per_band, per_band)
            after = pl.ds(base + b * per_band + 1, per_band)
            near_ref[here, :] = both[0:per_band, 0:LANES]
            far_ref[after, :] = both[0:per_band, LANES:]
            near_half[here, :] = both[per_band:, 0:LANES]
            far_half[after, :] = both[per_band:, LANES:]
        return 0

    lax.fori_loop(0, det, one, 0, unroll=UNROLL)
    for d in range(det):
        rows = slice(d * per_det, (d + 1) * per_det)
        near_ref[rows, :] = near_ref[rows, :] + far_ref[rows, :]
        near_half[rows, :] = near_half[rows, :] + far_half[rows, :]
    low = lax.broadcasted_iota(jnp.int32, (det, LANES), 1) < HALF

    def turned(i):
        return pltpu.roll(near_ref[pl.ds(i, det, stride=per_det), :], HALF, 1)

    here = turned(0)
    for b in range(BANDS):
        for i in range(b * per_band, (b + 1) * per_band):
            after = turned(i + 1)
            out_ref[:, i * TILE : (i + 1) * TILE] = (
                jnp.where(low, here, after) + near_half[pl.ds(i, det, stride=per_det), :]
            )
            here = after
        finish(b)


MESH = pl.DeviceIdType.MESH
PIECES = 1
COPIES = 2
UNROLL = 16


def whole_kernel(
    dims, bounds_hbm, index_hbm, x_hbm, taps_hbm, weights_hbm, pos_hbm, wafer_hbm,
    out_hbm, skyout_hbm, out_ref, give,
    bounds_ref, index_ref, x_ref, raw_ref, weights_ref, pos_ref, wafer_ref, load,
    rows_ref, last_ref, bands_ref, rest_ref, near_ref, far_ref, near_half, far_half,
    mask_ref, tiles_ref, fsend, frecv, csend, crecv, tsend, trecv,
    filt, spread, gsend, grecv, hsend, hrecv, sky_b, sky_f, skyb_recv, skyf_recv, spread_w, hits_ref,
    f_s, f_r, c_s, c_r, t_s, t_r, g_s, g_r, h_s, h_r, b_s, b_r, k_s, k_r,
):
    n_obs, td, det, length, slab, n_bounds = dims
    dets = det * td
    split = td // BANDS
    blocks = slab // TILE
    width = slab // PIECES
    folds = dets // TILE
    per_fold = td // folds
    count = n_obs * td
    group = count // COPIES
    stride = group // TILES
    own_rows = TILE // count
    obs = lax.axis_index("obs")
    me = lax.axis_index("td")
    linear = obs * td + me
    mine = lax.rem(linear // stride, TILES)
    within = lax.rem(linear, group)
    start = linear - within
    owner = lax.rem(linear, stride) == 0

    def place(device):
        return (device // td, lax.rem(device, td))

    def td_peer(k):
        return lax.rem(me + k, td)

    def td_source(k):
        return lax.rem(me + td - k, td)

    def obs_peer(k):
        return lax.rem(obs + k, n_obs)

    def obs_source(k):
        return lax.rem(obs + n_obs - k, n_obs)

    barrier = pltpu.get_barrier_semaphore()
    for k in range(1, td):
        pl.semaphore_signal(barrier, 1, device_id=(obs, td_peer(k)), device_id_type=MESH)
    for k in range(1, n_obs):
        pl.semaphore_signal(barrier, 1, device_id=(obs_peer(k), me), device_id_type=MESH)

    loads = [
        pltpu.make_async_copy(source, target, load.at[n])
        for n, (source, target) in enumerate(
            [
                (taps_hbm, raw_ref), (x_hbm, x_ref), (index_hbm, index_ref),
                (bounds_hbm, bounds_ref), (weights_hbm, weights_ref), (pos_hbm, pos_ref),
                (wafer_hbm, wafer_ref),
            ]
        )
    ]
    for copy in loads:
        copy.start()
    def tile_copy(k, slot):
        return pltpu.make_async_remote_copy(
            src_ref=tsend, dst_ref=trecv.at[slot], send_sem=t_s.at[k], recv_sem=t_r.at[k],
            device_id=(obs, td_peer(k)), device_id_type=MESH,
        )

    def each(number, do):
        def step(k, _):
            do(k)
            return 0

        lax.fori_loop(1, number, step, 0, unroll=min(number - 1, 8))

    loads[0].wait()
    load_taps(raw_ref, rows_ref, last_ref, det)
    build_bands(rows_ref, last_ref, bands_ref)
    loads[2].wait()
    row = lax.broadcasted_iota(jnp.int32, (blocks, LANES), 0)
    tile = jnp.zeros((blocks, LANES), jnp.int32)
    for n in range(blocks):
        tile = jnp.where(row == n, index_ref[0, n], tile)
    tsend[...] = tile.astype(F32)
    trecv[me] = tile.astype(F32)
    pl.semaphore_wait(barrier, td - 1 + n_obs - 1)
    each(td, lambda k: tile_copy(k, me).start())
    for n in (1, 3, 4, 5, 6):
        loads[n].wait()
    load_signal(x_ref, near_ref, far_ref, det)
    forward_body(near_ref, far_ref, bands_ref, rest_ref, length, det)

    def signal_copy(h, k, slot):
        cols = pl.ds(pl.multiple_of(h * width, TILE), width)
        peer = td_peer(k)
        return pltpu.make_async_remote_copy(
            src_ref=fsend.at[peer, :, cols], dst_ref=frecv.at[slot, :, cols],
            send_sem=f_s.at[h, k], recv_sem=f_r.at[h, k],
            device_id=(obs, peer), device_id_type=MESH,
        )

    def clean_copy(h, k, slot):
        cols = pl.ds(pl.multiple_of(h * width, TILE), width)
        peer = td_peer(k)
        return pltpu.make_async_remote_copy(
            src_ref=csend.at[peer, :, cols], dst_ref=crecv.at[slot, :, cols],
            send_sem=c_s.at[h, k], recv_sem=c_r.at[h, k],
            device_id=(obs, peer), device_id_type=MESH,
        )

    def hit_copy(k, slot):
        peer = obs_peer(k)
        return pltpu.make_async_remote_copy(
            src_ref=hsend.at[lax.rem((peer * td + me) // stride, TILES)], dst_ref=hrecv.at[slot],
            send_sem=h_s.at[k], recv_sem=h_r.at[k],
            device_id=(peer, me), device_id_type=MESH,
        )

    def bin_copy(q, source):
        return pltpu.make_async_remote_copy(
            src_ref=gsend.at[lax.rem(q, TILES)], dst_ref=grecv.at[source],
            send_sem=g_s.at[q], recv_sem=g_r.at[source],
            device_id=place(q * stride), device_id_type=MESH,
        )

    def rounded_copy(device, p):
        rows = pl.ds(pl.multiple_of(lax.rem(lax.rem(device, td), per_fold) * det, det), det)
        return pltpu.make_async_remote_copy(
            src_ref=sky_b.at[rows], dst_ref=skyb_recv.at[p],
            send_sem=b_s.at[device], recv_sem=b_r.at[p],
            device_id=place(device), device_id_type=MESH,
        )

    def row_copy(device, p):
        return pltpu.make_async_remote_copy(
            src_ref=sky_f.at[device], dst_ref=skyf_recv.at[p],
            send_sem=k_s.at[device], recv_sem=k_r.at[p],
            device_id=place(device), device_id_type=MESH,
        )

    def each_tile(do):
        def step(k, _):
            p = lax.rem(mine + k, TILES)

            @pl.when(start + p * stride != linear)
            def _():
                do(p)

            return 0

        lax.fori_loop(0, TILES, step, 0, unroll=8)

    def each_owner(do):
        def step(k, _):
            q = lax.rem(linear // stride + TILES + k, COPIES * TILES)

            @pl.when(q * stride != linear)
            def _():
                do(q)

            return 0

        lax.fori_loop(0, COPIES * TILES, step, 0, unroll=8)

    def each_device(do):
        each(count, lambda k: do(lax.rem(linear + k, count)))

    def each_near(do):
        each(group, lambda k: do(start + lax.rem(within + k, group)))

    per_band = length // TILE
    low = lax.broadcasted_iota(jnp.int32, (LANES, LANES), 1) < HALF

    def finish_block(n):
        early = rest_ref[pl.ds(n, LANES, stride=2 * per_band), :]
        late = rest_ref[pl.ds(per_band + n, LANES, stride=2 * per_band), :]
        block = jnp.where(low, early, pltpu.roll(late, HALF, 1)).astype(BF16)
        filt[n] = block
        quarter, inside = n // blocks, n % blocks
        for b in range(BANDS):
            fsend[b * split + quarter, :, inside * TILE : (inside + 1) * TILE] = block[
                b * det : (b + 1) * det, :
            ]

    def send_piece(p):
        quarter, h = p // PIECES, p % PIECES

        def send(k):
            if split == 1:
                signal_copy(h, k, me).start()
            else:

                @pl.when(lax.rem(td_peer(k), split) == quarter)
                def _():
                    signal_copy(h, k, me).start()

        each(td, send)

    for p in range(split * PIECES):
        for c in range(width // TILE):
            finish_block(p * (width // TILE) + c)
        send_piece(p)
    frecv[me] = fsend[me]

    mask_ref[...] = scan_mask(bounds_ref, length, n_bounds)
    for n in range(length // TILE):
        filt[n] = filt[n] * spread_rows(mask_ref[:, n * TILE : (n + 1) * TILE], det).astype(BF16)
    each(td, lambda k: tile_copy(k, td_source(k)).wait_recv())
    lane = lax.broadcasted_iota(jnp.int32, (blocks, LANES), 1) // det
    for quarter in range(split):
        tile = trecv[quarter]
        for b in range(1, BANDS):
            tile = jnp.where(lane == b, trecv[b * split + quarter], tile)
        tiles_ref[quarter * blocks : (quarter + 1) * blocks, :] = tile
    sums = jnp.zeros((det * TILES, TILE), F32)
    for n in range(length // TILE):
        pick = jnp.where(pick_matrix(tiles_ref[n : n + 1, :], det), 1.0, 0.0).astype(BF16)
        sums = sums + jnp.dot(pick, filt[n], preferred_element_type=F32)
    gsend[...] = sums.reshape(TILES, det, TILE).astype(BF16)
    each_owner(lambda q: bin_copy(q, linear).start())
    first = lax.broadcasted_iota(jnp.int32, (TILES, LANES), 1) % det == 0
    which = lax.broadcasted_iota(jnp.int32, (TILES, LANES), 0).astype(F32)
    counts = jnp.zeros((TILES, TILE), F32)
    for n in range(length // TILE):
        mask = spread_rows(mask_ref[:, n * TILE : (n + 1) * TILE], det).astype(BF16)
        pick = jnp.where(first & (which == tiles_ref[n : n + 1, :]), 1.0, 0.0).astype(BF16)
        counts = counts + jnp.dot(pick, mask, preferred_element_type=F32)

    @pl.when(owner)
    def _():
        grecv[linear] = gsend[mine]
        level = lax.broadcasted_iota(jnp.int32, (TILES, 8, TILE), 1)
        rows = jnp.broadcast_to(counts[:, None, :], (TILES, 8, TILE))
        weights = weights_ref[...].astype(F32)
        for q in range(folds):
            rows = jnp.where(level == q + 1, weights[:, None, q * TILE : (q + 1) * TILE], rows)
        hsend[...] = rows
        hrecv[obs] = hsend[mine]
        each(n_obs, lambda k: hit_copy(k, obs).start())

    p_high, p_low = projector(pos_ref, wafer_ref, dets)

    for h in range(PIECES):
        each(td, lambda k: signal_copy(h, k, td_source(k)).wait_recv())
        cols = slice(h * width, (h + 1) * width)
        cleaned = clean(p_high, p_low, frecv[:, :, cols].reshape(dets, width))
        csend[:, :, cols] = cleaned.reshape(td, det, width)
        each(td, lambda k: clean_copy(h, k, me).start())
    crecv[me] = csend[me]

    def band_rows(n):
        quarter, inside = n // blocks, n % blocks
        cols = slice(inside * TILE, (inside + 1) * TILE)
        return jnp.concatenate([crecv[b * split + quarter, :, cols] for b in range(BANDS)], axis=0)

    @pl.when(owner)
    def _():
        each(n_obs, lambda k: hit_copy(k, obs_source(k)).wait_recv())
        hit = jnp.zeros((TILE, TILE), F32)
        for o in range(n_obs):
            for q in range(folds):
                weight = jnp.broadcast_to(hrecv[o, q + 1 : q + 2, :], (TILE, TILE)).T
                hit = hit + weight * hrecv[o, 0:1, :]
                spread_w[o * folds + q] = weight
        hits_ref[...] = hit + prior_weight
        each_device(lambda d: bin_copy(linear // stride, d).wait_recv())
        total = jnp.zeros((TILE, TILE), F32)
        for o in range(n_obs):
            binned = grecv[o * td : (o + 1) * td].reshape(dets, TILE)
            fitted = jnp.dot(p_high, binned, preferred_element_type=F32) + jnp.dot(
                p_low, binned, preferred_element_type=F32
            )
            left = binned.astype(F32) - fitted
            for q in range(folds):
                total = total + spread_w[o * folds + q] * left[q * TILE : (q + 1) * TILE, :]
        sky = total / hits_ref[...]
        sky_b[...] = sky.astype(BF16)
        for d in range(count):
            sky_f[d] = sky[d * own_rows : (d + 1) * own_rows, :]
        each_near(lambda d: rounded_copy(d, mine).start())
        each_near(lambda d: row_copy(d, mine).start())
        own = pl.ds(pl.multiple_of(lax.rem(me, per_fold) * det, det), det)
        skyb_recv[mine] = sky_b[own, :]
        skyf_recv[mine] = sky_f[linear]

    grid = jnp.concatenate(
        [tiles_ref[...], jnp.zeros((LANES - length // TILE, LANES), F32)], axis=0
    ).T
    for n in range(length // TILE):
        spread[n] = jnp.where(spread_matrix(grid[:, n : n + 1], det), 1.0, 0.0).astype(BF16)
    for h in range(PIECES):
        each(td, lambda k: clean_copy(h, k, td_source(k)).wait_recv())
    each(td, lambda k: tile_copy(k, me).wait_send())
    for h in range(PIECES):
        each(td, lambda k: signal_copy(h, k, me).wait_send())
        each(td, lambda k: clean_copy(h, k, me).wait_send())
    each_owner(lambda q: bin_copy(q, linear).wait_send())


    @pl.when(owner)
    def _():
        each(n_obs, lambda k: hit_copy(k, obs).wait_send())

    each_tile(lambda p: rounded_copy(linear, p).wait_recv())
    chosen_from = skyb_recv[...].reshape(TILES * det, TILE)
    for n in range(length // TILE):
        mask = spread_rows(mask_ref[:, n * TILE : (n + 1) * TILE], det)
        chosen = jnp.dot(spread[n], chosen_from, preferred_element_type=F32)
        residual = (mask * (band_rows(n).astype(F32) - chosen)).astype(BF16)
        rest = residual.astype(F32)
        rest_ref[pl.ds(n, LANES, stride=2 * length // TILE), :] = rest
        rest_ref[pl.ds(length // TILE + n, LANES, stride=2 * length // TILE), :] = pltpu.roll(
            rest, HALF, 1
        )

    def give_copy(b):
        cols = pl.ds(b * length, length)
        return pltpu.make_async_copy(out_ref.at[:, cols], out_hbm.at[:, cols], give.at[b])

    sky_copy = pltpu.make_async_copy(skyf_recv, skyout_hbm, give.at[BANDS])
    adjoint_body(
        rest_ref, bands_ref, (near_ref, far_ref, near_half, far_half), out_ref, length, det,
        lambda b: give_copy(b).start(),
    )

    each_tile(lambda p: row_copy(linear, p).wait_recv())
    sky_copy.start()
    for b in range(BANDS):
        give_copy(b).wait()
    sky_copy.wait()

    @pl.when(owner)
    def _():
        each_near(lambda d: rounded_copy(d, mine).wait_send())
        each_near(lambda d: row_copy(d, mine).wait_send())


HB = pl.BlockSpec(memory_space=pltpu.HBM)
CUTS = 2


def hand_over(out_ref, sky_ref, out_hbm, sky_hbm, held, sky_held, taken, given):
    width = out_ref.shape[1] // CUTS
    pieces = [(sky_ref, sky_held, sky_hbm)]
    for n in range(CUTS):
        cols = pl.ds(n * width, width)
        pieces.append((out_ref.at[:, cols], held.at[:, cols], out_hbm.at[:, cols]))
    copies = []
    for n, (source, middle, target) in enumerate(pieces):
        take = pltpu.make_async_copy(source, middle, taken.at[n])
        take.start()
        copies.append((take, pltpu.make_async_copy(middle, target, given.at[n])))
    for take, give in copies:
        take.wait()
        give.start()
    for _, give in copies:
        give.wait()


def local(timestreams, filter_taps, scan_bounds, tile_index, det_weights, positions, wafer_group):
    _, det, samples = timestreams.shape
    td = lax.axis_size("td")
    n_obs = lax.axis_size("obs")
    dets = det * td
    length = samples // BANDS
    slab = samples // td
    blocks = slab // TILE
    count = n_obs * td
    own_rows = TILE // count
    dims = (n_obs, td, det, length, slab, scan_bounds.shape[1])
    dma = pltpu.SemaphoreType.DMA
    out, sky = pl.pallas_call(
        functools.partial(whole_kernel, dims),
        out_shape=(
            jax.ShapeDtypeStruct((det, samples), F32),
            jax.ShapeDtypeStruct((TILES, own_rows, TILE), F32),
        ),
        in_specs=[HB] * 7,
        out_specs=(HB, HB),
        scratch_shapes=[
            pltpu.VMEM((det, samples), F32),
            dma((BANDS + 1,)),
            pltpu.SMEM(scan_bounds.shape, jnp.int32),
            pltpu.SMEM(tile_index.shape, jnp.int32),
            pltpu.VMEM((det, samples), BF16),
            pltpu.VMEM((det, BANDS, TAPS), BF16),
            pltpu.VMEM((1, dets), BF16),
            pltpu.VMEM((2, dets), F32),
            pltpu.VMEM((1, dets), jnp.int32),
            dma((7,)),
            pltpu.VMEM((det * BANDS, LANES), F32),
            pltpu.VMEM((det * BANDS, LANES), F32),
            pltpu.VMEM((det * BANDS, HALF, 2 * LANES), BF16),
            pltpu.VMEM((2 * det * samples // TILE, LANES), F32),
            pltpu.VMEM((det * (samples // TILE + 8), LANES), F32),
            pltpu.VMEM((det * (samples // TILE + 8), LANES), F32),
            pltpu.VMEM((det * (samples // TILE + 8), LANES), F32),
            pltpu.VMEM((det * (samples // TILE + 8), LANES), F32),
            pltpu.VMEM((BANDS, length), F32),
            pltpu.VMEM((length // TILE, LANES), F32),
            pltpu.VMEM((td, det, slab), BF16),
            pltpu.VMEM((td, det, slab), BF16),
            pltpu.VMEM((td, det, slab), BF16),
            pltpu.VMEM((td, det, slab), BF16),
            pltpu.VMEM((blocks, LANES), F32),
            pltpu.VMEM((td, blocks, LANES), F32),
            pltpu.VMEM((length // TILE, LANES, TILE), BF16),
            pltpu.VMEM((length // TILE, LANES, det * TILES), BF16),
            pltpu.VMEM((TILES, det, TILE), BF16),
            pltpu.VMEM((count, det, TILE), BF16),
            pltpu.VMEM((TILES, 8, TILE), F32),
            pltpu.VMEM((n_obs, 8, TILE), F32),
            pltpu.VMEM((TILE, TILE), BF16),
            pltpu.VMEM((count, own_rows, TILE), F32),
            pltpu.VMEM((TILES, det, TILE), BF16),
            pltpu.VMEM((TILES, own_rows, TILE), F32),
            pltpu.VMEM((n_obs * dets // TILE, TILE, TILE), F32),
            pltpu.VMEM((TILE, TILE), F32),
            dma((PIECES, td)), dma((PIECES, td)), dma((PIECES, td)), dma((PIECES, td)),
            dma((td,)), dma((td,)), dma((COPIES * TILES,)), dma((count,)),
            dma((n_obs,)), dma((n_obs,)), dma((count,)), dma((TILES,)),
            dma((count,)), dma((TILES,)),
        ],
        compiler_params=pltpu.CompilerParams(
            collective_id=0, has_side_effects=True, vmem_limit_bytes=63 << 20
        ),
    )(
        scan_bounds, tile_index, timestreams[0], filter_taps[0], det_weights, positions,
        wafer_group.reshape(1, dets),
    )
    out, sky = pl.pallas_call(
        hand_over,
        out_shape=(
            jax.ShapeDtypeStruct((det, samples), F32),
            jax.ShapeDtypeStruct((TILES, own_rows, TILE), F32),
        ),
        in_specs=[HB, HB],
        out_specs=(HB, HB),
        scratch_shapes=[
            pltpu.VMEM((det, samples), F32), pltpu.VMEM((TILES, own_rows, TILE), F32),
            dma((CUTS + 1,)), dma((CUTS + 1,)),
        ],
        compiler_params=pltpu.CompilerParams(vmem_limit_bytes=63 << 20),
    )(out, sky)
    return out[None], sky


def solution(mesh):
    placed = (
        P("obs", "td", None),
        P("obs", "td", None, None),
        P("obs", None),
        P("obs", "td"),
        P("obs", None),
        P(),
        P(),
    )
    return jax.shard_map(
        local,
        mesh=mesh,
        in_specs=placed,
        out_specs=(P("obs", "td", None), P(None, ("obs", "td"), None)),
        check_vma=False,
    )
```

```python
import functools

import jax
import jax.numpy as jnp
from jax import lax
from jax.experimental import pallas as pl
from jax.experimental.pallas import tpu as pltpu
from jax.sharding import PartitionSpec as P

TAPS = 129
HALF = 64
BANDS = 8
TILE = 128
POLY = 6
TILES = 16
LANES = 128
prior_weight = 1.0
F32 = jnp.float32
BF16 = jnp.bfloat16


def projector(pos_ref, wafer_ref, dets):
    x = pos_ref[0:1, :]
    y = pos_ref[1:2, :]
    rows = [jnp.ones_like(x), x, y, x * x, x * y, y * y]
    q = [r.astype(BF16).astype(F32) for r in rows]
    group = jnp.broadcast_to(wafer_ref[...].astype(F32), (dets, dets))
    same = group == group.T
    same_b = jnp.where(same, 1.0, 0.0).astype(BF16)
    pairs = [(i, j) for i in range(POLY) for j in range(i + 1)]
    products = jnp.concatenate(
        [q[i] * q[j] for i, j in pairs] + [jnp.zeros((32 - len(pairs), dets), F32)], axis=0
    )
    high = products.astype(BF16)
    low = (products - high.astype(F32)).astype(BF16)
    gram = jnp.dot(high, same_b, preferred_element_type=F32) + jnp.dot(
        low, same_b, preferred_element_type=F32
    )
    entry = {pair: gram[n : n + 1, :] for n, pair in enumerate(pairs)}
    factor, inv, white = {}, {}, []
    for i in range(POLY):
        for j in range(i + 1):
            value = entry[(i, j)]
            for k in range(j):
                value = value - factor[(i, k)] * factor[(j, k)]
            if i == j:
                factor[(i, i)] = jnp.sqrt(value)
                inv[i] = 1.0 / factor[(i, i)]
            else:
                factor[(i, j)] = value * inv[j]
        value = q[i]
        for k in range(i):
            value = value - factor[(i, k)] * white[k]
        white.append(value * inv[i])
    whitened = jnp.concatenate(white + [jnp.zeros((8 - POLY, dets), F32)], axis=0)
    columns = jnp.concatenate([whitened, jnp.zeros((LANES - 8, dets), F32)], axis=0).T
    outer = columns[:, 0:1] * white[0]
    for m in range(1, POLY):
        outer = outer + columns[:, m : m + 1] * white[m]
    outer = jnp.where(same, outer, 0.0)
    p_high = outer.astype(BF16)
    p_low = (outer - p_high.astype(F32)).astype(BF16)
    return p_high, p_low


def clean(p_high, p_low, gathered):
    fitted = jnp.dot(p_high, gathered, preferred_element_type=F32) + jnp.dot(
        p_low, gathered, preferred_element_type=F32
    )
    return (gathered.astype(F32) - fitted).astype(BF16)


def scan_mask(bounds_ref, length, n_bounds):
    sample = lax.broadcasted_iota(jnp.int32, (BANDS, length), 0) * length + lax.broadcasted_iota(
        jnp.int32, (BANDS, length), 1
    )
    count = jnp.zeros((BANDS, length), jnp.int32)
    for n in range(n_bounds):
        count = count + jnp.where(bounds_ref[0, n] <= sample, 1, 0)
    return (count & 1).astype(F32)


def spread_rows(mask, det):
    return jnp.broadcast_to(mask[:, None, :], (BANDS, det, TILE)).reshape(BANDS * det, TILE)


def pick_matrix(tiles_row, det):
    shape = (det * TILES, LANES)
    row = lax.broadcasted_iota(jnp.int32, shape, 0)
    lane = lax.broadcasted_iota(jnp.int32, shape, 1)
    return (row % det == lane % det) & ((row // det).astype(F32) == tiles_row)


def spread_matrix(tiles_column, det):
    shape = (LANES, det * TILES)
    row = lax.broadcasted_iota(jnp.int32, shape, 0)
    lane = lax.broadcasted_iota(jnp.int32, shape, 1)
    return (row % det == lane % det) & ((lane // det).astype(F32) == tiles_column)


def load_taps(raw_ref, rows_ref, last_ref, det):
    taps = raw_ref[...].reshape(det * BANDS, TAPS)
    rows_ref[...] = taps[:, 0:TILE].astype(F32)
    last_ref[...] = jnp.broadcast_to(taps[:, TILE:TAPS].astype(F32), (det * BANDS, LANES))


def build_bands(rows_ref, last_ref, bands_ref):
    j = lax.broadcasted_iota(jnp.int32, (HALF, LANES), 0)
    m = lax.broadcasted_iota(jnp.int32, (HALF, LANES), 1)
    keep = jnp.where(m >= j, 1.0, 0.0).astype(BF16)
    same = jnp.where(m == j, 1.0, 0.0).astype(BF16)

    def one(pair, _):
        row = jnp.broadcast_to(rows_ref[pl.ds(pair, 1), :], (HALF, LANES))
        last = jnp.broadcast_to(last_ref[pl.ds(pair, 1), :], (HALF, LANES)).astype(BF16)
        turned = pltpu.roll(row, 0, 1, stride=1, stride_axis=0).astype(BF16)
        near = turned * keep
        bands_ref[pair, :, 0:LANES] = near
        bands_ref[pair, :, LANES : 2 * LANES] = (turned - near) + last * same
        return 0

    lax.fori_loop(0, rows_ref.shape[0], one, 0, unroll=64)


def load_signal(x_ref, block_ref, shift_ref, det):
    total = x_ref.shape[1] // TILE
    low = lax.broadcasted_iota(jnp.int32, (det, LANES), 1) < HALF
    before = jnp.zeros((det, LANES), F32)
    for i in range(total + 1):
        rows = pl.ds(i, det, stride=total + 8)
        if i < total:
            block = x_ref[:, i * TILE : (i + 1) * TILE].astype(F32)
        else:
            block = jnp.zeros((det, LANES), F32)
        block_ref[rows, :] = block
        turned = pltpu.roll(block, HALF, 1)
        shift_ref[rows, :] = jnp.where(low, before, turned)
        before = turned


def forward_body(block_ref, shift_ref, bands_ref, halves_ref, length, det):
    per_band = length // TILE
    per_det = BANDS * per_band + 8

    def one(d, _):
        base = pl.multiple_of(d * per_det, 8)
        for b in range(BANDS):
            here = pl.ds(base + b * per_band, per_band)
            after = pl.ds(base + b * per_band + 1, per_band)
            window = jnp.concatenate(
                [
                    jnp.concatenate([source[here, :], source[after, :]], axis=1)
                    for source in (shift_ref, block_ref)
                ],
                axis=0,
            ).astype(BF16)
            rows = pl.ds(pl.multiple_of((b * det + d) * 2 * per_band, 8), 2 * per_band)
            halves_ref[rows, 0:HALF] = lax.dot_general(
                window, bands_ref[d * BANDS + b], (((1,), (1,)), ((), ())),
                preferred_element_type=F32,
            )
        return 0

    lax.fori_loop(0, det, one, 0, unroll=UNROLL)


def adjoint_body(rest_ref, bands_ref, sums, out_ref, length, det, finish):
    per_band = length // TILE
    per_det = BANDS * per_band + 8
    near_ref, far_ref, near_half, far_half = sums

    def one(d, _):
        base = pl.multiple_of(d * per_det, 8)
        for far in (far_ref, far_half):
            far[pl.ds(base, 8), :] = jnp.zeros((8, LANES), F32)
        for near in (near_ref, near_half):
            near[pl.ds(base + per_det - 8, 8), :] = jnp.zeros((8, LANES), F32)
        for b in range(BANDS):
            pair = b * det + d
            rest = rest_ref[pl.ds(pl.multiple_of(pair * 2 * per_band, 8), 2 * per_band), :]
            both = jnp.dot(
                rest[:, 0:HALF].astype(BF16), bands_ref[d * BANDS + b], preferred_element_type=F32
            )
            here = pl.ds(base + b * per_band, per_band)
            after = pl.ds(base + b * per_band + 1, per_band)
            near_ref[here, :] = both[0:per_band, 0:LANES]
            far_ref[after, :] = both[0:per_band, LANES:]
            near_half[here, :] = both[per_band:, 0:LANES]
            far_half[after, :] = both[per_band:, LANES:]
        return 0

    lax.fori_loop(0, det, one, 0, unroll=UNROLL)
    for d in range(det):
        rows = slice(d * per_det, (d + 1) * per_det)
        near_ref[rows, :] = near_ref[rows, :] + far_ref[rows, :]
        near_half[rows, :] = near_half[rows, :] + far_half[rows, :]
    low = lax.broadcasted_iota(jnp.int32, (det, LANES), 1) < HALF

    def turned(i):
        return pltpu.roll(near_ref[pl.ds(i, det, stride=per_det), :], HALF, 1)

    here = turned(0)
    for b in range(BANDS):
        for i in range(b * per_band, (b + 1) * per_band):
            after = turned(i + 1)
            out_ref[:, i * TILE : (i + 1) * TILE] = (
                jnp.where(low, here, after) + near_half[pl.ds(i, det, stride=per_det), :]
            )
            here = after
        finish(b)


MESH = pl.DeviceIdType.MESH
PIECES = 1
COPIES = 2
UNROLL = 16


def whole_kernel(
    dims, bounds_hbm, index_hbm, x_hbm, taps_hbm, weights_hbm, pos_hbm, wafer_hbm,
    out_hbm, skyout_hbm, out_ref, give,
    bounds_ref, index_ref, x_ref, raw_ref, weights_ref, pos_ref, wafer_ref, load,
    rows_ref, last_ref, bands_ref, rest_ref, near_ref, far_ref, near_half, far_half,
    mask_ref, tiles_ref, fsend, frecv, csend, crecv, tsend, trecv,
    filt, spread, gsend, grecv, hsend, hrecv, sky_b, sky_f, skyb_recv, skyf_recv, spread_w, hits_ref,
    f_s, f_r, c_s, c_r, t_s, t_r, g_s, g_r, h_s, h_r, b_s, b_r, k_s, k_r,
):
    n_obs, td, det, length, slab, n_bounds = dims
    dets = det * td
    split = td // BANDS
    blocks = slab // TILE
    width = slab // PIECES
    folds = dets // TILE
    per_fold = td // folds
    count = n_obs * td
    group = count // COPIES
    stride = group // TILES
    own_rows = TILE // count
    obs = lax.axis_index("obs")
    me = lax.axis_index("td")
    linear = obs * td + me
    mine = lax.rem(linear // stride, TILES)
    within = lax.rem(linear, group)
    start = linear - within
    owner = lax.rem(linear, stride) == 0

    def place(device):
        return (device // td, lax.rem(device, td))

    def td_peer(k):
        return lax.rem(me + k, td)

    def td_source(k):
        return lax.rem(me + td - k, td)

    def obs_peer(k):
        return lax.rem(obs + k, n_obs)

    def obs_source(k):
        return lax.rem(obs + n_obs - k, n_obs)

    barrier = pltpu.get_barrier_semaphore()
    for k in range(1, td):
        pl.semaphore_signal(barrier, 1, device_id=(obs, td_peer(k)), device_id_type=MESH)
    for k in range(1, n_obs):
        pl.semaphore_signal(barrier, 1, device_id=(obs_peer(k), me), device_id_type=MESH)

    loads = [
        pltpu.make_async_copy(source, target, load.at[n])
        for n, (source, target) in enumerate(
            [
                (taps_hbm, raw_ref), (x_hbm, x_ref), (index_hbm, index_ref),
                (bounds_hbm, bounds_ref), (weights_hbm, weights_ref), (pos_hbm, pos_ref),
                (wafer_hbm, wafer_ref),
            ]
        )
    ]
    for n in (2, 0, 1, 3, 4, 5, 6):
        loads[n].start()
    def tile_copy(k, slot):
        return pltpu.make_async_remote_copy(
            src_ref=tsend, dst_ref=trecv.at[slot], send_sem=t_s.at[k], recv_sem=t_r.at[k],
            device_id=(obs, td_peer(k)), device_id_type=MESH,
        )

    def each(number, do):
        def step(k, _):
            do(k)
            return 0

        lax.fori_loop(1, number, step, 0, unroll=min(number - 1, 16))

    loads[0].wait()
    load_taps(raw_ref, rows_ref, last_ref, det)
    build_bands(rows_ref, last_ref, bands_ref)
    loads[2].wait()
    row = lax.broadcasted_iota(jnp.int32, (blocks, LANES), 0)
    tile = jnp.zeros((blocks, LANES), jnp.int32)
    for n in range(blocks):
        tile = jnp.where(row == n, index_ref[0, n], tile)
    tsend[...] = tile.astype(F32)
    trecv[me] = tile.astype(F32)
    pl.semaphore_wait(barrier, td - 1 + n_obs - 1)
    each(td, lambda k: tile_copy(k, me).start())
    for n in (1, 3, 4, 5, 6):
        loads[n].wait()
    load_signal(x_ref, near_ref, far_ref, det)
    forward_body(near_ref, far_ref, bands_ref, rest_ref, length, det)

    def signal_copy(h, k, slot):
        cols = pl.ds(pl.multiple_of(h * width, TILE), width)
        peer = td_peer(k)
        return pltpu.make_async_remote_copy(
            src_ref=fsend.at[peer, :, cols], dst_ref=frecv.at[slot, :, cols],
            send_sem=f_s.at[h, k], recv_sem=f_r.at[h, k],
            device_id=(obs, peer), device_id_type=MESH,
        )

    def clean_copy(h, k, slot):
        cols = pl.ds(pl.multiple_of(h * width, TILE), width)
        peer = td_peer(k)
        return pltpu.make_async_remote_copy(
            src_ref=csend.at[peer, :, cols], dst_ref=crecv.at[slot, :, cols],
            send_sem=c_s.at[h, k], recv_sem=c_r.at[h, k],
            device_id=(obs, peer), device_id_type=MESH,
        )

    def hit_copy(k, slot):
        peer = obs_peer(k)
        return pltpu.make_async_remote_copy(
            src_ref=hsend.at[lax.rem((peer * td + me) // stride, TILES)], dst_ref=hrecv.at[slot],
            send_sem=h_s.at[k], recv_sem=h_r.at[k],
            device_id=(peer, me), device_id_type=MESH,
        )

    def bin_copy(q, source):
        return pltpu.make_async_remote_copy(
            src_ref=gsend.at[lax.rem(q, TILES)], dst_ref=grecv.at[source],
            send_sem=g_s.at[q], recv_sem=g_r.at[source],
            device_id=place(q * stride), device_id_type=MESH,
        )

    def rounded_copy(device, p):
        rows = pl.ds(pl.multiple_of(lax.rem(lax.rem(device, td), per_fold) * det, det), det)
        return pltpu.make_async_remote_copy(
            src_ref=sky_b.at[rows], dst_ref=skyb_recv.at[p],
            send_sem=b_s.at[device], recv_sem=b_r.at[p],
            device_id=place(device), device_id_type=MESH,
        )

    def row_copy(device, p):
        return pltpu.make_async_remote_copy(
            src_ref=sky_f.at[device], dst_ref=skyf_recv.at[p],
            send_sem=k_s.at[device], recv_sem=k_r.at[p],
            device_id=place(device), device_id_type=MESH,
        )

    def each_tile(do):
        def step(k, _):
            p = lax.rem(mine + k, TILES)

            @pl.when(start + p * stride != linear)
            def _():
                do(p)

            return 0

        lax.fori_loop(0, TILES, step, 0, unroll=16)

    def each_owner(do):
        def step(k, _):
            q = lax.rem(linear // stride + TILES + k, COPIES * TILES)

            @pl.when(q * stride != linear)
            def _():
                do(q)

            return 0

        lax.fori_loop(0, COPIES * TILES, step, 0, unroll=16)

    def each_device(do):
        each(count, lambda k: do(lax.rem(linear + k, count)))

    def each_near(do):
        each(group, lambda k: do(start + lax.rem(within + k, group)))

    per_band = length // TILE
    low = lax.broadcasted_iota(jnp.int32, (LANES, LANES), 1) < HALF

    def finish_block(n):
        early = rest_ref[pl.ds(n, LANES, stride=2 * per_band), :]
        late = rest_ref[pl.ds(per_band + n, LANES, stride=2 * per_band), :]
        block = jnp.where(low, early, pltpu.roll(late, HALF, 1)).astype(BF16)
        filt[n] = block
        quarter, inside = n // blocks, n % blocks
        for b in range(BANDS):
            fsend[b * split + quarter, :, inside * TILE : (inside + 1) * TILE] = block[
                b * det : (b + 1) * det, :
            ]

    def send_piece(p):
        quarter, h = p // PIECES, p % PIECES

        def send(k):
            if split == 1:
                signal_copy(h, k, me).start()
            else:

                @pl.when(lax.rem(td_peer(k), split) == quarter)
                def _():
                    signal_copy(h, k, me).start()

        each(td, send)

    for p in range(split * PIECES):
        for c in range(width // TILE):
            finish_block(p * (width // TILE) + c)
        send_piece(p)
    frecv[me] = fsend[me]

    mask_ref[...] = scan_mask(bounds_ref, length, n_bounds)
    for n in range(length // TILE):
        filt[n] = filt[n] * spread_rows(mask_ref[:, n * TILE : (n + 1) * TILE], det).astype(BF16)
    each(td, lambda k: tile_copy(k, td_source(k)).wait_recv())
    lane = lax.broadcasted_iota(jnp.int32, (blocks, LANES), 1) // det
    for quarter in range(split):
        tile = trecv[quarter]
        for b in range(1, BANDS):
            tile = jnp.where(lane == b, trecv[b * split + quarter], tile)
        tiles_ref[quarter * blocks : (quarter + 1) * blocks, :] = tile
    sums = jnp.zeros((det * TILES, TILE), F32)
    for n in range(length // TILE):
        pick = jnp.where(pick_matrix(tiles_ref[n : n + 1, :], det), 1.0, 0.0).astype(BF16)
        sums = sums + jnp.dot(pick, filt[n], preferred_element_type=F32)
    gsend[...] = sums.reshape(TILES, det, TILE).astype(BF16)
    each_owner(lambda q: bin_copy(q, linear).start())
    first = lax.broadcasted_iota(jnp.int32, (TILES, LANES), 1) % det == 0
    which = lax.broadcasted_iota(jnp.int32, (TILES, LANES), 0).astype(F32)
    counts = jnp.zeros((TILES, TILE), F32)
    for n in range(length // TILE):
        mask = spread_rows(mask_ref[:, n * TILE : (n + 1) * TILE], det).astype(BF16)
        pick = jnp.where(first & (which == tiles_ref[n : n + 1, :]), 1.0, 0.0).astype(BF16)
        counts = counts + jnp.dot(pick, mask, preferred_element_type=F32)

    @pl.when(owner)
    def _():
        grecv[linear] = gsend[mine]
        level = lax.broadcasted_iota(jnp.int32, (TILES, 8, TILE), 1)
        rows = jnp.broadcast_to(counts[:, None, :], (TILES, 8, TILE))
        weights = weights_ref[...].astype(F32)
        for q in range(folds):
            rows = jnp.where(level == q + 1, weights[:, None, q * TILE : (q + 1) * TILE], rows)
        hsend[...] = rows
        hrecv[obs] = hsend[mine]
        each(n_obs, lambda k: hit_copy(k, obs).start())

    p_high, p_low = projector(pos_ref, wafer_ref, dets)

    for h in range(PIECES):
        each(td, lambda k: signal_copy(h, k, td_source(k)).wait_recv())
        cols = slice(h * width, (h + 1) * width)
        cleaned = clean(p_high, p_low, frecv[:, :, cols].reshape(dets, width))
        csend[:, :, cols] = cleaned.reshape(td, det, width)
        each(td, lambda k: clean_copy(h, k, me).start())
    crecv[me] = csend[me]

    def band_rows(n):
        quarter, inside = n // blocks, n % blocks
        cols = slice(inside * TILE, (inside + 1) * TILE)
        return jnp.concatenate([crecv[b * split + quarter, :, cols] for b in range(BANDS)], axis=0)

    @pl.when(owner)
    def _():
        each(n_obs, lambda k: hit_copy(k, obs_source(k)).wait_recv())
        hit = jnp.zeros((TILE, TILE), F32)
        for o in range(n_obs):
            for q in range(folds):
                weight = jnp.broadcast_to(hrecv[o, q + 1 : q + 2, :], (TILE, TILE)).T
                hit = hit + weight * hrecv[o, 0:1, :]
                spread_w[o * folds + q] = weight
        hits_ref[...] = hit + prior_weight
        each_device(lambda d: bin_copy(linear // stride, d).wait_recv())
        total = jnp.zeros((TILE, TILE), F32)
        for o in range(n_obs):
            binned = grecv[o * td : (o + 1) * td].reshape(dets, TILE)
            fitted = jnp.dot(p_high, binned, preferred_element_type=F32) + jnp.dot(
                p_low, binned, preferred_element_type=F32
            )
            left = binned.astype(F32) - fitted
            for q in range(folds):
                total = total + spread_w[o * folds + q] * left[q * TILE : (q + 1) * TILE, :]
        sky = total / hits_ref[...]
        sky_b[...] = sky.astype(BF16)
        each_near(lambda d: rounded_copy(d, mine).start())
        for d in range(count):
            sky_f[d] = sky[d * own_rows : (d + 1) * own_rows, :]
        each_near(lambda d: row_copy(d, mine).start())
        own = pl.ds(pl.multiple_of(lax.rem(me, per_fold) * det, det), det)
        skyb_recv[mine] = sky_b[own, :]
        skyf_recv[mine] = sky_f[linear]

    grid = jnp.concatenate(
        [tiles_ref[...], jnp.zeros((LANES - length // TILE, LANES), F32)], axis=0
    ).T
    for n in range(length // TILE):
        spread[n] = jnp.where(spread_matrix(grid[:, n : n + 1], det), 1.0, 0.0).astype(BF16)
    for h in range(PIECES):
        each(td, lambda k: clean_copy(h, k, td_source(k)).wait_recv())
    each(td, lambda k: tile_copy(k, me).wait_send())
    for h in range(PIECES):
        each(td, lambda k: signal_copy(h, k, me).wait_send())
        each(td, lambda k: clean_copy(h, k, me).wait_send())
    each_owner(lambda q: bin_copy(q, linear).wait_send())


    @pl.when(owner)
    def _():
        each(n_obs, lambda k: hit_copy(k, obs).wait_send())

    each_tile(lambda p: rounded_copy(linear, p).wait_recv())
    chosen_from = skyb_recv[...].reshape(TILES * det, TILE)
    for n in range(length // TILE):
        mask = spread_rows(mask_ref[:, n * TILE : (n + 1) * TILE], det)
        chosen = jnp.dot(spread[n], chosen_from, preferred_element_type=F32)
        residual = (mask * (band_rows(n).astype(F32) - chosen)).astype(BF16)
        rest = residual.astype(F32)
        rest_ref[pl.ds(n, LANES, stride=2 * length // TILE), :] = rest
        rest_ref[pl.ds(length // TILE + n, LANES, stride=2 * length // TILE), :] = pltpu.roll(
            rest, HALF, 1
        )

    def give_copy(b):
        cols = pl.ds(b * length, length)
        return pltpu.make_async_copy(out_ref.at[:, cols], out_hbm.at[:, cols], give.at[b])

    sky_copy = pltpu.make_async_copy(skyf_recv, skyout_hbm, give.at[BANDS])
    adjoint_body(
        rest_ref, bands_ref, (near_ref, far_ref, near_half, far_half), out_ref, length, det,
        lambda b: give_copy(b).start(),
    )

    each_tile(lambda p: row_copy(linear, p).wait_recv())
    sky_copy.start()
    for b in range(BANDS):
        give_copy(b).wait()
    sky_copy.wait()

    @pl.when(owner)
    def _():
        each_near(lambda d: rounded_copy(d, mine).wait_send())
        each_near(lambda d: row_copy(d, mine).wait_send())


HB = pl.BlockSpec(memory_space=pltpu.HBM)
CUTS = 2


def hand_over(out_ref, sky_ref, out_hbm, sky_hbm, held, sky_held, taken, given):
    width = out_ref.shape[1] // CUTS
    pieces = [(sky_ref, sky_held, sky_hbm)]
    for n in range(CUTS):
        cols = pl.ds(n * width, width)
        pieces.append((out_ref.at[:, cols], held.at[:, cols], out_hbm.at[:, cols]))
    copies = []
    for n, (source, middle, target) in enumerate(pieces):
        take = pltpu.make_async_copy(source, middle, taken.at[n])
        take.start()
        copies.append((take, pltpu.make_async_copy(middle, target, given.at[n])))
    for take, give in copies:
        take.wait()
        give.start()
    for _, give in copies:
        give.wait()


def local(timestreams, filter_taps, scan_bounds, tile_index, det_weights, positions, wafer_group):
    _, det, samples = timestreams.shape
    td = lax.axis_size("td")
    n_obs = lax.axis_size("obs")
    dets = det * td
    length = samples // BANDS
    slab = samples // td
    blocks = slab // TILE
    count = n_obs * td
    own_rows = TILE // count
    dims = (n_obs, td, det, length, slab, scan_bounds.shape[1])
    dma = pltpu.SemaphoreType.DMA
    out, sky = pl.pallas_call(
        functools.partial(whole_kernel, dims),
        out_shape=(
            jax.ShapeDtypeStruct((det, samples), F32),
            jax.ShapeDtypeStruct((TILES, own_rows, TILE), F32),
        ),
        in_specs=[HB] * 7,
        out_specs=(HB, HB),
        scratch_shapes=[
            pltpu.VMEM((det, samples), F32),
            dma((BANDS + 1,)),
            pltpu.SMEM(scan_bounds.shape, jnp.int32),
            pltpu.SMEM(tile_index.shape, jnp.int32),
            pltpu.VMEM((det, samples), BF16),
            pltpu.VMEM((det, BANDS, TAPS), BF16),
            pltpu.VMEM((1, dets), BF16),
            pltpu.VMEM((2, dets), F32),
            pltpu.VMEM((1, dets), jnp.int32),
            dma((7,)),
            pltpu.VMEM((det * BANDS, LANES), F32),
            pltpu.VMEM((det * BANDS, LANES), F32),
            pltpu.VMEM((det * BANDS, HALF, 2 * LANES), BF16),
            pltpu.VMEM((2 * det * samples // TILE, LANES), F32),
            pltpu.VMEM((det * (samples // TILE + 8), LANES), F32),
            pltpu.VMEM((det * (samples // TILE + 8), LANES), F32),
            pltpu.VMEM((det * (samples // TILE + 8), LANES), F32),
            pltpu.VMEM((det * (samples // TILE + 8), LANES), F32),
            pltpu.VMEM((BANDS, length), F32),
            pltpu.VMEM((length // TILE, LANES), F32),
            pltpu.VMEM((td, det, slab), BF16),
            pltpu.VMEM((td, det, slab), BF16),
            pltpu.VMEM((td, det, slab), BF16),
            pltpu.VMEM((td, det, slab), BF16),
            pltpu.VMEM((blocks, LANES), F32),
            pltpu.VMEM((td, blocks, LANES), F32),
            pltpu.VMEM((length // TILE, LANES, TILE), BF16),
            pltpu.VMEM((length // TILE, LANES, det * TILES), BF16),
            pltpu.VMEM((TILES, det, TILE), BF16),
            pltpu.VMEM((count, det, TILE), BF16),
            pltpu.VMEM((TILES, 8, TILE), F32),
            pltpu.VMEM((n_obs, 8, TILE), F32),
            pltpu.VMEM((TILE, TILE), BF16),
            pltpu.VMEM((count, own_rows, TILE), F32),
            pltpu.VMEM((TILES, det, TILE), BF16),
            pltpu.VMEM((TILES, own_rows, TILE), F32),
            pltpu.VMEM((n_obs * dets // TILE, TILE, TILE), F32),
            pltpu.VMEM((TILE, TILE), F32),
            dma((PIECES, td)), dma((PIECES, td)), dma((PIECES, td)), dma((PIECES, td)),
            dma((td,)), dma((td,)), dma((COPIES * TILES,)), dma((count,)),
            dma((n_obs,)), dma((n_obs,)), dma((count,)), dma((TILES,)),
            dma((count,)), dma((TILES,)),
        ],
        compiler_params=pltpu.CompilerParams(
            collective_id=0, has_side_effects=True, vmem_limit_bytes=63 << 20
        ),
    )(
        scan_bounds, tile_index, timestreams[0], filter_taps[0], det_weights, positions,
        wafer_group.reshape(1, dets),
    )
    out, sky = pl.pallas_call(
        hand_over,
        out_shape=(
            jax.ShapeDtypeStruct((det, samples), F32),
            jax.ShapeDtypeStruct((TILES, own_rows, TILE), F32),
        ),
        in_specs=[HB, HB],
        out_specs=(HB, HB),
        scratch_shapes=[
            pltpu.VMEM((det, samples), F32), pltpu.VMEM((TILES, own_rows, TILE), F32),
            dma((CUTS + 1,)), dma((CUTS + 1,)),
        ],
        compiler_params=pltpu.CompilerParams(vmem_limit_bytes=63 << 20),
    )(out, sky)
    return out[None], sky


def solution(mesh):
    placed = (
        P("obs", "td", None),
        P("obs", "td", None, None),
        P("obs", None),
        P("obs", "td"),
        P("obs", None),
        P(),
        P(),
    )
    return jax.shard_map(
        local,
        mesh=mesh,
        in_specs=placed,
        out_specs=(P("obs", "td", None), P(None, ("obs", "td"), None)),
        check_vma=False,
    )
```

```python
import functools

import jax
import jax.numpy as jnp
from jax import lax
from jax.experimental import pallas as pl
from jax.experimental.pallas import tpu as pltpu
from jax.sharding import PartitionSpec as P

TAPS = 129
HALF = 64
BANDS = 8
TILE = 128
POLY = 6
TILES = 16
LANES = 128
prior_weight = 1.0
F32 = jnp.float32
BF16 = jnp.bfloat16


def projector(pos_ref, wafer_ref, dets):
    x = pos_ref[0:1, :]
    y = pos_ref[1:2, :]
    rows = [jnp.ones_like(x), x, y, x * x, x * y, y * y]
    q = [r.astype(BF16).astype(F32) for r in rows]
    group = jnp.broadcast_to(wafer_ref[...].astype(F32), (dets, dets))
    same = group == group.T
    same_b = jnp.where(same, 1.0, 0.0).astype(BF16)
    pairs = [(i, j) for i in range(POLY) for j in range(i + 1)]
    products = jnp.concatenate(
        [q[i] * q[j] for i, j in pairs] + [jnp.zeros((32 - len(pairs), dets), F32)], axis=0
    )
    high = products.astype(BF16)
    low = (products - high.astype(F32)).astype(BF16)
    gram = jnp.dot(high, same_b, preferred_element_type=F32) + jnp.dot(
        low, same_b, preferred_element_type=F32
    )
    entry = {pair: gram[n : n + 1, :] for n, pair in enumerate(pairs)}
    factor, inv, white = {}, {}, []
    for i in range(POLY):
        for j in range(i + 1):
            value = entry[(i, j)]
            for k in range(j):
                value = value - factor[(i, k)] * factor[(j, k)]
            if i == j:
                factor[(i, i)] = jnp.sqrt(value)
                inv[i] = 1.0 / factor[(i, i)]
            else:
                factor[(i, j)] = value * inv[j]
        value = q[i]
        for k in range(i):
            value = value - factor[(i, k)] * white[k]
        white.append(value * inv[i])
    whitened = jnp.concatenate(white + [jnp.zeros((8 - POLY, dets), F32)], axis=0)
    columns = jnp.concatenate([whitened, jnp.zeros((LANES - 8, dets), F32)], axis=0).T
    outer = columns[:, 0:1] * white[0]
    for m in range(1, POLY):
        outer = outer + columns[:, m : m + 1] * white[m]
    outer = jnp.where(same, outer, 0.0)
    p_high = outer.astype(BF16)
    p_low = (outer - p_high.astype(F32)).astype(BF16)
    return p_high, p_low


def clean(p_high, p_low, gathered):
    fitted = jnp.dot(p_high, gathered, preferred_element_type=F32) + jnp.dot(
        p_low, gathered, preferred_element_type=F32
    )
    return (gathered.astype(F32) - fitted).astype(BF16)


def scan_mask(bounds_ref, length, n_bounds):
    sample = lax.broadcasted_iota(jnp.int32, (BANDS, length), 0) * length + lax.broadcasted_iota(
        jnp.int32, (BANDS, length), 1
    )
    count = jnp.zeros((BANDS, length), jnp.int32)
    for n in range(n_bounds):
        count = count + jnp.where(bounds_ref[0, n] <= sample, 1, 0)
    return (count & 1).astype(F32)


def spread_rows(mask, det):
    return jnp.broadcast_to(mask[:, None, :], (BANDS, det, TILE)).reshape(BANDS * det, TILE)


def pick_matrix(tiles_row, det):
    shape = (det * TILES, LANES)
    row = lax.broadcasted_iota(jnp.int32, shape, 0)
    lane = lax.broadcasted_iota(jnp.int32, shape, 1)
    return (row % det == lane % det) & ((row // det).astype(F32) == tiles_row)


def spread_matrix(tiles_column, det):
    shape = (LANES, det * TILES)
    row = lax.broadcasted_iota(jnp.int32, shape, 0)
    lane = lax.broadcasted_iota(jnp.int32, shape, 1)
    return (row % det == lane % det) & ((lane // det).astype(F32) == tiles_column)


def load_taps(raw_ref, rows_ref, last_ref, det):
    taps = raw_ref[...].reshape(det * BANDS, TAPS)
    rows_ref[...] = taps[:, 0:TILE].astype(F32)
    last_ref[...] = jnp.broadcast_to(taps[:, TILE:TAPS].astype(F32), (det * BANDS, LANES))


def build_bands(rows_ref, last_ref, bands_ref):
    j = lax.broadcasted_iota(jnp.int32, (HALF, LANES), 0)
    m = lax.broadcasted_iota(jnp.int32, (HALF, LANES), 1)
    keep = jnp.where(m >= j, 1.0, 0.0).astype(BF16)
    same = jnp.where(m == j, 1.0, 0.0).astype(BF16)

    def one(pair, _):
        row = jnp.broadcast_to(rows_ref[pl.ds(pair, 1), :], (HALF, LANES))
        last = jnp.broadcast_to(last_ref[pl.ds(pair, 1), :], (HALF, LANES)).astype(BF16)
        turned = pltpu.roll(row, 0, 1, stride=1, stride_axis=0).astype(BF16)
        near = turned * keep
        bands_ref[pair, :, 0:LANES] = near
        bands_ref[pair, :, LANES : 2 * LANES] = (turned - near) + last * same
        return 0

    lax.fori_loop(0, rows_ref.shape[0], one, 0, unroll=64)


def load_signal(x_ref, block_ref, shift_ref, det):
    total = x_ref.shape[1] // TILE
    low = lax.broadcasted_iota(jnp.int32, (det, LANES), 1) < HALF
    before = jnp.zeros((det, LANES), F32)
    for i in range(total + 1):
        rows = pl.ds(i, det, stride=total + 8)
        if i < total:
            block = x_ref[:, i * TILE : (i + 1) * TILE].astype(F32)
        else:
            block = jnp.zeros((det, LANES), F32)
        block_ref[rows, :] = block
        turned = pltpu.roll(block, HALF, 1)
        shift_ref[rows, :] = jnp.where(low, before, turned)
        before = turned


def forward_body(block_ref, shift_ref, bands_ref, halves_ref, length, det):
    per_band = length // TILE
    per_det = BANDS * per_band + 8

    def one(d, _):
        base = pl.multiple_of(d * per_det, 8)
        for b in range(BANDS):
            here = pl.ds(base + b * per_band, per_band)
            after = pl.ds(base + b * per_band + 1, per_band)
            window = jnp.concatenate(
                [
                    jnp.concatenate([source[here, :], source[after, :]], axis=1)
                    for source in (shift_ref, block_ref)
                ],
                axis=0,
            ).astype(BF16)
            rows = pl.ds(pl.multiple_of((b * det + d) * 2 * per_band, 8), 2 * per_band)
            halves_ref[rows, 0:HALF] = lax.dot_general(
                window, bands_ref[d * BANDS + b], (((1,), (1,)), ((), ())),
                preferred_element_type=F32,
            )
        return 0

    lax.fori_loop(0, det, one, 0, unroll=UNROLL)


def adjoint_body(rest_ref, bands_ref, sums, out_ref, length, det, finish):
    per_band = length // TILE
    per_det = BANDS * per_band + 8
    near_ref, far_ref, near_half, far_half = sums

    def one(d, _):
        base = pl.multiple_of(d * per_det, 8)
        for far in (far_ref, far_half):
            far[pl.ds(base, 8), :] = jnp.zeros((8, LANES), F32)
        for near in (near_ref, near_half):
            near[pl.ds(base + per_det - 8, 8), :] = jnp.zeros((8, LANES), F32)
        for b in range(BANDS):
            pair = b * det + d
            rest = rest_ref[pl.ds(pl.multiple_of(pair * 2 * per_band, 8), 2 * per_band), :]
            both = jnp.dot(
                rest[:, 0:HALF].astype(BF16), bands_ref[d * BANDS + b], preferred_element_type=F32
            )
            here = pl.ds(base + b * per_band, per_band)
            after = pl.ds(base + b * per_band + 1, per_band)
            near_ref[here, :] = both[0:per_band, 0:LANES]
            far_ref[after, :] = both[0:per_band, LANES:]
            near_half[here, :] = both[per_band:, 0:LANES]
            far_half[after, :] = both[per_band:, LANES:]
        return 0

    lax.fori_loop(0, det, one, 0, unroll=UNROLL)
    for d in range(det):
        rows = slice(d * per_det, (d + 1) * per_det)
        near_ref[rows, :] = near_ref[rows, :] + far_ref[rows, :]
        near_half[rows, :] = near_half[rows, :] + far_half[rows, :]
    low = lax.broadcasted_iota(jnp.int32, (det, LANES), 1) < HALF

    def turned(i):
        return pltpu.roll(near_ref[pl.ds(i, det, stride=per_det), :], HALF, 1)

    here = turned(0)
    for b in range(BANDS):
        for i in range(b * per_band, (b + 1) * per_band):
            after = turned(i + 1)
            out_ref[:, i * TILE : (i + 1) * TILE] = (
                jnp.where(low, here, after) + near_half[pl.ds(i, det, stride=per_det), :]
            )
            here = after
        finish(b)


MESH = pl.DeviceIdType.MESH
PIECES = 1
COPIES = 2
UNROLL = 16


def whole_kernel(
    dims, bounds_hbm, index_hbm, x_hbm, taps_hbm, weights_hbm, pos_hbm, wafer_hbm,
    out_hbm, skyout_hbm, out_ref, give,
    bounds_ref, index_ref, x_ref, raw_ref, weights_ref, pos_ref, wafer_ref, load,
    rows_ref, last_ref, bands_ref, rest_ref, near_ref, far_ref, near_half, far_half,
    mask_ref, tiles_ref, fsend, frecv, csend, crecv, tsend, trecv,
    filt, spread, gsend, grecv, hsend, hrecv, sky_b, sky_f, skyb_recv, skyf_recv, spread_w, hits_ref,
    f_s, f_r, c_s, c_r, t_s, t_r, g_s, g_r, h_s, h_r, b_s, b_r, k_s, k_r,
):
    n_obs, td, det, length, slab, n_bounds = dims
    dets = det * td
    split = td // BANDS
    blocks = slab // TILE
    width = slab // PIECES
    folds = dets // TILE
    per_fold = td // folds
    count = n_obs * td
    group = count // COPIES
    stride = group // TILES
    own_rows = TILE // count
    obs = lax.axis_index("obs")
    me = lax.axis_index("td")
    linear = obs * td + me
    mine = lax.rem(linear // stride, TILES)
    within = lax.rem(linear, group)
    start = linear - within
    owner = lax.rem(linear, stride) == 0

    def place(device):
        return (device // td, lax.rem(device, td))

    def td_peer(k):
        return lax.rem(me + k, td)

    def td_source(k):
        return lax.rem(me + td - k, td)

    def obs_peer(k):
        return lax.rem(obs + k, n_obs)

    def obs_source(k):
        return lax.rem(obs + n_obs - k, n_obs)

    barrier = pltpu.get_barrier_semaphore()
    for k in range(1, td):
        pl.semaphore_signal(barrier, 1, device_id=(obs, td_peer(k)), device_id_type=MESH)
    for k in range(1, n_obs):
        pl.semaphore_signal(barrier, 1, device_id=(obs_peer(k), me), device_id_type=MESH)

    loads = [
        pltpu.make_async_copy(source, target, load.at[n])
        for n, (source, target) in enumerate(
            [
                (taps_hbm, raw_ref), (x_hbm, x_ref), (index_hbm, index_ref),
                (bounds_hbm, bounds_ref), (weights_hbm, weights_ref), (pos_hbm, pos_ref),
                (wafer_hbm, wafer_ref),
            ]
        )
    ]
    for n in (2, 0, 1, 3, 4, 5, 6):
        loads[n].start()
    def tile_copy(k, slot):
        return pltpu.make_async_remote_copy(
            src_ref=tsend, dst_ref=trecv.at[slot], send_sem=t_s.at[k], recv_sem=t_r.at[k],
            device_id=(obs, td_peer(k)), device_id_type=MESH,
        )

    def each(number, do):
        def step(k, _):
            do(k)
            return 0

        lax.fori_loop(1, number, step, 0, unroll=min(number - 1, 16))

    loads[0].wait()
    load_taps(raw_ref, rows_ref, last_ref, det)
    build_bands(rows_ref, last_ref, bands_ref)
    loads[2].wait()
    row = lax.broadcasted_iota(jnp.int32, (blocks, LANES), 0)
    tile = jnp.zeros((blocks, LANES), jnp.int32)
    for n in range(blocks):
        tile = jnp.where(row == n, index_ref[0, n], tile)
    tsend[...] = tile.astype(F32)
    trecv[me] = tile.astype(F32)
    pl.semaphore_wait(barrier, td - 1 + n_obs - 1)
    each(td, lambda k: tile_copy(k, me).start())
    for n in (1, 3, 4, 5, 6):
        loads[n].wait()
    load_signal(x_ref, near_ref, far_ref, det)
    forward_body(near_ref, far_ref, bands_ref, rest_ref, length, det)

    def signal_copy(h, k, slot):
        cols = pl.ds(pl.multiple_of(h * width, TILE), width)
        peer = td_peer(k)
        return pltpu.make_async_remote_copy(
            src_ref=fsend.at[peer, :, cols], dst_ref=frecv.at[slot, :, cols],
            send_sem=f_s.at[h, k], recv_sem=f_r.at[h, k],
            device_id=(obs, peer), device_id_type=MESH,
        )

    def clean_copy(h, k, slot):
        cols = pl.ds(pl.multiple_of(h * width, TILE), width)
        peer = td_peer(k)
        return pltpu.make_async_remote_copy(
            src_ref=csend.at[peer, :, cols], dst_ref=crecv.at[slot, :, cols],
            send_sem=c_s.at[h, k], recv_sem=c_r.at[h, k],
            device_id=(obs, peer), device_id_type=MESH,
        )

    def hit_copy(k, slot):
        peer = obs_peer(k)
        return pltpu.make_async_remote_copy(
            src_ref=hsend.at[lax.rem((peer * td + me) // stride, TILES)], dst_ref=hrecv.at[slot],
            send_sem=h_s.at[k], recv_sem=h_r.at[k],
            device_id=(peer, me), device_id_type=MESH,
        )

    def bin_copy(q, source):
        return pltpu.make_async_remote_copy(
            src_ref=gsend.at[lax.rem(q, TILES)], dst_ref=grecv.at[source],
            send_sem=g_s.at[q], recv_sem=g_r.at[source],
            device_id=place(q * stride), device_id_type=MESH,
        )

    def rounded_copy(device, p):
        rows = pl.ds(pl.multiple_of(lax.rem(lax.rem(device, td), per_fold) * det, det), det)
        return pltpu.make_async_remote_copy(
            src_ref=sky_b.at[rows], dst_ref=skyb_recv.at[p],
            send_sem=b_s.at[device], recv_sem=b_r.at[p],
            device_id=place(device), device_id_type=MESH,
        )

    def row_copy(device, p):
        return pltpu.make_async_remote_copy(
            src_ref=sky_f.at[device], dst_ref=skyf_recv.at[p],
            send_sem=k_s.at[device], recv_sem=k_r.at[p],
            device_id=place(device), device_id_type=MESH,
        )

    def each_tile(do):
        def step(k, _):
            p = lax.rem(mine + k, TILES)

            @pl.when(start + p * stride != linear)
            def _():
                do(p)

            return 0

        lax.fori_loop(0, TILES, step, 0, unroll=16)

    def each_owner(do):
        def step(k, _):
            q = lax.rem(linear // stride + TILES + k, COPIES * TILES)

            @pl.when(q * stride != linear)
            def _():
                do(q)

            return 0

        lax.fori_loop(0, COPIES * TILES, step, 0, unroll=16)

    def each_device(do):
        each(count, lambda k: do(lax.rem(linear + k, count)))

    def each_near(do):
        each(group, lambda k: do(start + lax.rem(within + k, group)))

    per_band = length // TILE
    low = lax.broadcasted_iota(jnp.int32, (LANES, LANES), 1) < HALF

    def finish_block(n):
        early = rest_ref[pl.ds(n, LANES, stride=2 * per_band), :]
        late = rest_ref[pl.ds(per_band + n, LANES, stride=2 * per_band), :]
        block = jnp.where(low, early, pltpu.roll(late, HALF, 1)).astype(BF16)
        filt[n] = block
        quarter, inside = n // blocks, n % blocks
        for b in range(BANDS):
            fsend[b * split + quarter, :, inside * TILE : (inside + 1) * TILE] = block[
                b * det : (b + 1) * det, :
            ]

    def send_piece(p):
        quarter, h = p // PIECES, p % PIECES

        def send(k):
            if split == 1:
                signal_copy(h, k, me).start()
            else:

                @pl.when(lax.rem(td_peer(k), split) == quarter)
                def _():
                    signal_copy(h, k, me).start()

        each(td, send)

    for p in range(split * PIECES):
        for c in range(width // TILE):
            finish_block(p * (width // TILE) + c)
        send_piece(p)
    frecv[me] = fsend[me]

    mask_ref[...] = scan_mask(bounds_ref, length, n_bounds)
    for n in range(length // TILE):
        filt[n] = filt[n] * spread_rows(mask_ref[:, n * TILE : (n + 1) * TILE], det).astype(BF16)
    each(td, lambda k: tile_copy(k, td_source(k)).wait_recv())
    lane = lax.broadcasted_iota(jnp.int32, (blocks, LANES), 1) // det
    for quarter in range(split):
        tile = trecv[quarter]
        for b in range(1, BANDS):
            tile = jnp.where(lane == b, trecv[b * split + quarter], tile)
        tiles_ref[quarter * blocks : (quarter + 1) * blocks, :] = tile
    sums = jnp.zeros((det * TILES, TILE), F32)
    for n in range(length // TILE):
        pick = jnp.where(pick_matrix(tiles_ref[n : n + 1, :], det), 1.0, 0.0).astype(BF16)
        sums = sums + jnp.dot(pick, filt[n], preferred_element_type=F32)
    gsend[...] = sums.reshape(TILES, det, TILE).astype(BF16)
    each_owner(lambda q: bin_copy(q, linear).start())
    first = lax.broadcasted_iota(jnp.int32, (TILES, LANES), 1) % det == 0
    which = lax.broadcasted_iota(jnp.int32, (TILES, LANES), 0).astype(F32)
    counts = jnp.zeros((TILES, TILE), F32)
    for n in range(length // TILE):
        mask = spread_rows(mask_ref[:, n * TILE : (n + 1) * TILE], det).astype(BF16)
        pick = jnp.where(first & (which == tiles_ref[n : n + 1, :]), 1.0, 0.0).astype(BF16)
        counts = counts + jnp.dot(pick, mask, preferred_element_type=F32)

    @pl.when(owner)
    def _():
        grecv[linear] = gsend[mine]
        level = lax.broadcasted_iota(jnp.int32, (TILES, 8, TILE), 1)
        rows = jnp.broadcast_to(counts[:, None, :], (TILES, 8, TILE))
        weights = weights_ref[...].astype(F32)
        for q in range(folds):
            rows = jnp.where(level == q + 1, weights[:, None, q * TILE : (q + 1) * TILE], rows)
        hsend[...] = rows
        hrecv[obs] = hsend[mine]
        each(n_obs, lambda k: hit_copy(k, obs).start())

    p_high, p_low = projector(pos_ref, wafer_ref, dets)

    for h in range(PIECES):
        each(td, lambda k: signal_copy(h, k, td_source(k)).wait_recv())
        cols = slice(h * width, (h + 1) * width)
        cleaned = clean(p_high, p_low, frecv[:, :, cols].reshape(dets, width))
        csend[:, :, cols] = cleaned.reshape(td, det, width)
        each(td, lambda k: clean_copy(h, k, me).start())
    crecv[me] = csend[me]

    def band_rows(n):
        quarter, inside = n // blocks, n % blocks
        cols = slice(inside * TILE, (inside + 1) * TILE)
        return jnp.concatenate([crecv[b * split + quarter, :, cols] for b in range(BANDS)], axis=0)

    @pl.when(owner)
    def _():
        each(n_obs, lambda k: hit_copy(k, obs_source(k)).wait_recv())
        hit = jnp.zeros((TILE, TILE), F32)
        for o in range(n_obs):
            for q in range(folds):
                weight = jnp.broadcast_to(hrecv[o, q + 1 : q + 2, :], (TILE, TILE)).T
                hit = hit + weight * hrecv[o, 0:1, :]
                spread_w[o * folds + q] = weight
        hits_ref[...] = hit + prior_weight
        each_device(lambda d: bin_copy(linear // stride, d).wait_recv())
        total = jnp.zeros((TILE, TILE), F32)
        for o in range(n_obs):
            binned = grecv[o * td : (o + 1) * td].reshape(dets, TILE)
            fitted = jnp.dot(p_high, binned, preferred_element_type=F32) + jnp.dot(
                p_low, binned, preferred_element_type=F32
            )
            left = binned.astype(F32) - fitted
            for q in range(folds):
                total = total + spread_w[o * folds + q] * left[q * TILE : (q + 1) * TILE, :]
        sky = total / hits_ref[...]
        sky_b[...] = sky.astype(BF16)
        each_near(lambda d: rounded_copy(d, mine).start())
        for d in range(count):
            sky_f[d] = sky[d * own_rows : (d + 1) * own_rows, :]
        each_near(lambda d: row_copy(d, mine).start())
        own = pl.ds(pl.multiple_of(lax.rem(me, per_fold) * det, det), det)
        skyb_recv[mine] = sky_b[own, :]
        skyf_recv[mine] = sky_f[linear]

    grid = jnp.concatenate(
        [tiles_ref[...], jnp.zeros((LANES - length // TILE, LANES), F32)], axis=0
    ).T
    for n in range(length // TILE):
        spread[n] = jnp.where(spread_matrix(grid[:, n : n + 1], det), 1.0, 0.0).astype(BF16)
    for h in range(PIECES):
        each(td, lambda k: clean_copy(h, k, td_source(k)).wait_recv())
    each(td, lambda k: tile_copy(k, me).wait_send())
    for h in range(PIECES):
        each(td, lambda k: signal_copy(h, k, me).wait_send())
        each(td, lambda k: clean_copy(h, k, me).wait_send())
    each_owner(lambda q: bin_copy(q, linear).wait_send())


    @pl.when(owner)
    def _():
        each(n_obs, lambda k: hit_copy(k, obs).wait_send())

    each_tile(lambda p: rounded_copy(linear, p).wait_recv())
    chosen_from = skyb_recv[...].reshape(TILES * det, TILE)
    for n in range(length // TILE):
        mask = spread_rows(mask_ref[:, n * TILE : (n + 1) * TILE], det)
        chosen = jnp.dot(spread[n], chosen_from, preferred_element_type=F32)
        residual = (mask * (band_rows(n).astype(F32) - chosen)).astype(BF16)
        rest = residual.astype(F32)
        rest_ref[pl.ds(n, LANES, stride=2 * length // TILE), :] = rest
        rest_ref[pl.ds(length // TILE + n, LANES, stride=2 * length // TILE), :] = pltpu.roll(
            rest, HALF, 1
        )

    def give_copy(b):
        cols = pl.ds(b * length, length)
        return pltpu.make_async_copy(out_ref.at[:, cols], out_hbm.at[:, cols], give.at[b])

    sky_copy = pltpu.make_async_copy(skyf_recv, skyout_hbm, give.at[BANDS])
    adjoint_body(
        rest_ref, bands_ref, (near_ref, far_ref, near_half, far_half), out_ref, length, det,
        lambda b: give_copy(b).start(),
    )

    each_tile(lambda p: row_copy(linear, p).wait_recv())
    sky_copy.start()
    for b in range(BANDS):
        give_copy(b).wait()
    sky_copy.wait()

    @pl.when(owner)
    def _():
        each_near(lambda d: rounded_copy(d, mine).wait_send())
        each_near(lambda d: row_copy(d, mine).wait_send())


HB = pl.BlockSpec(memory_space=pltpu.HBM)
CUTS = 2


def hand_over(out_ref, sky_ref, out_hbm, sky_hbm, held, sky_held, taken, given):
    width = out_ref.shape[1] // CUTS
    pieces = [(sky_ref, sky_held, sky_hbm)]
    for n in range(CUTS):
        cols = pl.ds(n * width, width)
        pieces.append((out_ref.at[:, cols], held.at[:, cols], out_hbm.at[:, cols]))
    copies = []
    for n, (source, middle, target) in enumerate(pieces):
        take = pltpu.make_async_copy(source, middle, taken.at[n])
        take.start()
        copies.append((take, pltpu.make_async_copy(middle, target, given.at[n])))
    for take, give in copies:
        take.wait()
        give.start()
    for _, give in copies:
        give.wait()


def local(timestreams, filter_taps, scan_bounds, tile_index, det_weights, positions, wafer_group):
    _, det, samples = timestreams.shape
    td = lax.axis_size("td")
    n_obs = lax.axis_size("obs")
    dets = det * td
    length = samples // BANDS
    slab = samples // td
    blocks = slab // TILE
    count = n_obs * td
    own_rows = TILE // count
    dims = (n_obs, td, det, length, slab, scan_bounds.shape[1])
    dma = pltpu.SemaphoreType.DMA
    out, sky = pl.pallas_call(
        functools.partial(whole_kernel, dims),
        out_shape=(
            jax.ShapeDtypeStruct((det, samples), F32),
            jax.ShapeDtypeStruct((TILES, own_rows, TILE), F32),
        ),
        in_specs=[HB] * 7,
        out_specs=(HB, HB),
        scratch_shapes=[
            pltpu.VMEM((det, samples), F32),
            dma((BANDS + 1,)),
            pltpu.SMEM(scan_bounds.shape, jnp.int32),
            pltpu.SMEM(tile_index.shape, jnp.int32),
            pltpu.VMEM((det, samples), BF16),
            pltpu.VMEM((det, BANDS, TAPS), BF16),
            pltpu.VMEM((1, dets), BF16),
            pltpu.VMEM((2, dets), F32),
            pltpu.VMEM((1, dets), jnp.int32),
            dma((7,)),
            pltpu.VMEM((det * BANDS, LANES), F32),
            pltpu.VMEM((det * BANDS, LANES), F32),
            pltpu.VMEM((det * BANDS, HALF, 2 * LANES), BF16),
            pltpu.VMEM((2 * (det * BANDS + 1) * (length // TILE), LANES), F32),
            pltpu.VMEM(((det + 1) * (samples // TILE + 8), LANES), F32),
            pltpu.VMEM(((det + 1) * (samples // TILE + 8), LANES), F32),
            pltpu.VMEM(((det + 1) * (samples // TILE + 8), LANES), F32),
            pltpu.VMEM(((det + 1) * (samples // TILE + 8), LANES), F32),
            pltpu.VMEM((BANDS, length), F32),
            pltpu.VMEM((length // TILE, LANES), F32),
            pltpu.VMEM((td, det, slab), BF16),
            pltpu.VMEM((td, det, slab), BF16),
            pltpu.VMEM((td, det, slab), BF16),
            pltpu.VMEM((td, det, slab), BF16),
            pltpu.VMEM((blocks, LANES), F32),
            pltpu.VMEM((td, blocks, LANES), F32),
            pltpu.VMEM((length // TILE, LANES, TILE), BF16),
            pltpu.VMEM((length // TILE, LANES, det * TILES), BF16),
            pltpu.VMEM((TILES, det, TILE), BF16),
            pltpu.VMEM((count, det, TILE), BF16),
            pltpu.VMEM((TILES, 8, TILE), F32),
            pltpu.VMEM((n_obs, 8, TILE), F32),
            pltpu.VMEM((TILE, TILE), BF16),
            pltpu.VMEM((count, own_rows, TILE), F32),
            pltpu.VMEM((TILES, det, TILE), BF16),
            pltpu.VMEM((TILES, own_rows, TILE), F32),
            pltpu.VMEM((n_obs * dets // TILE, TILE, TILE), F32),
            pltpu.VMEM((TILE, TILE), F32),
            dma((PIECES, td)), dma((PIECES, td)), dma((PIECES, td)), dma((PIECES, td)),
            dma((td,)), dma((td,)), dma((COPIES * TILES,)), dma((count,)),
            dma((n_obs,)), dma((n_obs,)), dma((count,)), dma((TILES,)),
            dma((count,)), dma((TILES,)),
        ],
        compiler_params=pltpu.CompilerParams(
            collective_id=0, has_side_effects=True, vmem_limit_bytes=63 << 20
        ),
    )(
        scan_bounds, tile_index, timestreams[0], filter_taps[0], det_weights, positions,
        wafer_group.reshape(1, dets),
    )
    out, sky = pl.pallas_call(
        hand_over,
        out_shape=(
            jax.ShapeDtypeStruct((det, samples), F32),
            jax.ShapeDtypeStruct((TILES, own_rows, TILE), F32),
        ),
        in_specs=[HB, HB],
        out_specs=(HB, HB),
        scratch_shapes=[
            pltpu.VMEM((det, samples), F32), pltpu.VMEM((TILES, own_rows, TILE), F32),
            dma((CUTS + 1,)), dma((CUTS + 1,)),
        ],
        compiler_params=pltpu.CompilerParams(vmem_limit_bytes=63 << 20),
    )(out, sky)
    return out[None], sky


def solution(mesh):
    placed = (
        P("obs", "td", None),
        P("obs", "td", None, None),
        P("obs", None),
        P("obs", "td"),
        P("obs", None),
        P(),
        P(),
    )
    return jax.shard_map(
        local,
        mesh=mesh,
        in_specs=placed,
        out_specs=(P("obs", "td", None), P(None, ("obs", "td"), None)),
        check_vma=False,
    )
```
